128 devices in a mesh: dp: 32 (over z, y_hi, x), tensor: 4 (over y_lo, core).
Axes of the slice: x: 4, y: 4 (y_hi: 2, y_lo: 2; y = y_hi * 2 + y_lo), z: 4, core: 2. Of those that a mesh axis runs over, the one named last changes fastest.
Arguments:
- tokens: bfloat16 [32, 4, 128, 2048], P('dp', 'tensor'), may hold values from -6 to 6
- doc_ids: int32 [32, 4, 128], P('dp'), may hold values from 0 to 3, never falling along the last dimension, each value on 1 to 64 neighbouring positions
- attn_gain: float32 [2048], P(('dp', 'tensor')), may hold values from 0.5 to 1.5
- forget_floor: float32 [2048], P(('dp', 'tensor')), may hold values from 0.5 to 0.98
- w_query: bfloat16 [2048, 2048], P('dp', 'tensor'), may hold values from -0.125 to 0.125
- w_forget: bfloat16 [2048, 2048], P('dp', 'tensor'), may hold values from -0.125 to 0.125
- w_value: bfloat16 [2048, 2048], P('dp', 'tensor'), may hold values from -0.125 to 0.125
- w_outgate: bfloat16 [2048, 2048], P('dp', 'tensor'), may hold values from -0.125 to 0.125
- w_output: bfloat16 [2048, 2048], P('tensor', 'dp'), may hold values from -0.125 to 0.125
- mlp_gain: float32 [2048], P(('dp', 'tensor')), may hold values from 0.5 to 1.5
- w_gate: bfloat16 [2048, 5632], P('dp', 'tensor'), may hold values from -0.125 to 0.125
- w_up: bfloat16 [2048, 5632], P('dp', 'tensor'), may hold values from -0.125 to 0.125
- w_down: bfloat16 [5632, 2048], P('tensor', 'dp'), may hold values from -0.078125 to 0.078125
- cotangent: bfloat16 [32, 4, 128, 2048], P('dp', 'tensor'), may hold values from -6 to 6
Outputs:
- layer_out: bfloat16 [32, 4, 128, 2048], P('dp', 'tensor')
- grad_tokens: float32 [32, 4, 128, 2048], P('dp', 'tensor')
- grad_attn_gain: float32 [2048], P(('dp', 'tensor'))
- grad_floor: float32 [2048], P(('dp', 'tensor'))
- grad_query: float32 [2048, 2048], P('dp', 'tensor')
- grad_forget: float32 [2048, 2048], P('dp', 'tensor')
- grad_value: float32 [2048, 2048], P('dp', 'tensor')
- grad_outgate: float32 [2048, 2048], P('dp', 'tensor')
- grad_output: float32 [2048, 2048], P('tensor', 'dp')
- grad_mlp_gain: float32 [2048], P(('dp', 'tensor'))
- grad_gate: float32 [2048, 5632], P('dp', 'tensor')
- grad_up: float32 [2048, 5632], P('dp', 'tensor')
- grad_down: float32 [5632, 2048], P('tensor', 'dp')
The draws below stay inside these ranges and needn't reach their ends.
Inputs may be any that keep to these rules, and one draw needn't show every extreme that they name: `doc_ids`: within each row of 128 tokens the sequence numbers never fall; each sequence has 1 to 64 tokens, and the longest has exactly 64.
All inputs are finite; a program needn't handle non-finite values.
Results may differ from the reference program's by a relative error of at most 0.025.
Values may be sent and summed in bfloat16 or wider, within the bound.
No kernel may reach another device: no remote copies, remote signals or barrier semaphores. Data moves between devices by JAX's collectives and lax.ppermute only.
A program may use at most 192 MiB of HBM per device.

```python
import math
import jax
import jax.numpy as jnp
import numpy as np
from jax import lax

D = 2048
NH = 16
HK = 128
FF = 5632
ROWS = 128
MB = 4
BLOCK = 64
DOCS = 4
DOC_MOST = 64
GROUPS = 32


def steps_of(key, extent, split, least, top_value):
    level, own = 1.0, jax.random.fold_in(key, 6)
    for dim, shards_of in split:
        steps = jnp.exp(jax.random.uniform(jax.random.fold_in(own, dim), (shards_of,), jnp.float32, least / len(split), top_value / len(split)))
        level = level * jnp.repeat(steps, extent[dim] // shards_of).reshape([-1 if axis == dim else 1 for axis in range(len(extent))])
    return level


def length_profile(number_of, total, limit, slope):
    loads = [(1 << 20) // math.isqrt(rank ** slope) + 1 for rank in range(2, number_of + 1)]
    spare, holding = total - limit - (number_of - 1), [1] * (number_of - 1)
    while spare > 0:
        movable = [i for i in range(number_of - 1) if holding[i] < limit]
        whole, budget = sum([loads[i] for i in movable]), spare
        for i in movable:
            extra = min(limit - holding[i], max(1, budget * loads[i] // whole), spare)
            holding[i] = holding[i] + extra
            spare = spare - extra
    return np.array([limit] + holding)


def uneven(stream_key, number_of, total, bound, lean):
    if number_of == 2:
        one = jax.random.randint(stream_key, (), max(1, total - bound), min(bound, total - 1) + 1)
        return jnp.stack([one, total - one])
    sizes = jnp.asarray(length_profile(number_of, total, bound, lean), jnp.int32)
    pairs = (number_of - 1) // 2
    giver, taker = sizes[1:1 + 2 * pairs:2], sizes[2:2 + 2 * pairs:2]
    room = jnp.minimum(giver - 1, bound - taker)
    shifted = jax.random.randint(jax.random.fold_in(stream_key, 1), (pairs,), 0, 1 << 20) % (room + 1)
    sizes = sizes.at[1:1 + 2 * pairs:2].set(giver - shifted).at[2:2 + 2 * pairs:2].set(taker + shifted)
    return sizes[jax.random.permutation(jax.random.fold_in(stream_key, 2), number_of)]


def noise(stream_key, shape, scale, limit, split=(), dtype=jnp.bfloat16):
    values = scale * jax.random.normal(stream_key, shape, jnp.float32)
    if split:
        values = values * steps_of(stream_key, shape, split, -0.22, 0.18)
    return jnp.clip(values, -limit, limit).astype(dtype)


def setup_inputs(seed: int = 0) -> dict:
    splits = jax.random.split(jax.random.key(seed), 15)
    return {
        "tokens": noise(splits[0], (GROUPS, MB, ROWS, D), 1.0, 6.0, ((0, 32), (1, 4))),
        "doc_ids": jax.vmap(lambda own: jnp.searchsorted(jnp.cumsum(uneven(own, DOCS, ROWS, DOC_MOST, 2)), jnp.arange(ROWS), side="right"))(jax.random.split(splits[1], GROUPS * MB)).reshape((GROUPS, MB, ROWS)).astype(jnp.int32),
        "attn_gain": jnp.clip(1.0 + 0.1 * jax.random.normal(splits[2], (D,), jnp.float32), 0.5, 1.5),
        "forget_floor": jnp.clip(0.5 + 0.48000002 * jax.random.uniform(splits[3], (D,), jnp.float32) ** steps_of(splits[3], (D,), ((0, 128),), -0.2, 0.2), 0.5, 0.98),
        "w_query": noise(splits[4], (D, D), D ** -0.5, 0.125, ((0, 32), (1, 4))),
        "w_forget": noise(splits[5], (D, D), D ** -0.5, 0.125, ((0, 32), (1, 4))),
        "w_value": noise(splits[6], (D, D), D ** -0.5, 0.125, ((0, 32), (1, 4))),
        "w_outgate": noise(splits[7], (D, D), D ** -0.5, 0.125, ((0, 32), (1, 4))),
        "w_output": noise(splits[8], (D, D), D ** -0.5, 0.125, ((0, 4), (1, 32))),
        "mlp_gain": jnp.clip(1.0 + 0.1 * jax.random.normal(splits[9], (D,), jnp.float32), 0.5, 1.5),
        "w_gate": noise(splits[10], (D, FF), D ** -0.5, 0.125, ((0, 32), (1, 4))),
        "w_up": noise(splits[11], (D, FF), D ** -0.5, 0.125, ((0, 32), (1, 4))),
        "w_down": noise(splits[12], (FF, D), FF ** -0.5, 0.078125, ((0, 4), (1, 32))),
        "cotangent": noise(splits[13], (GROUPS, MB, ROWS, D), 1.0, 6.0, ((0, 32), (1, 4))),
    }


epsilon = 1e-06

@jax.custom_vjp
def low(v):
    return lax.optimization_barrier(v.astype(jnp.bfloat16)).astype(jnp.float32)

@jax.custom_vjp
def low_back(v):
    return v

def low_keep(v):
    return (low(v), None)

def low_pass(kept, grad):
    return (grad,)

def back_keep(v):
    return (v, None)

def back_low(kept, grad):
    return (low(grad),)
low.defvjp(low_keep, low_pass)
low_back.defvjp(back_keep, back_low)

def row_scale(values):
    return lax.rsqrt(lax.optimization_barrier(jnp.mean(values * values, axis=-1, keepdims=True)) + epsilon)

def precise(left, right):
    return jnp.dot(left, right, precision=lax.Precision.HIGHEST)

def recurrence(query, forget_raw, value, floor_vec, doc_row):
    length, heads_n, chan = query.shape
    forget = floor_vec + (1.0 - floor_vec) * jax.nn.sigmoid(forget_raw)
    log_forget = jnp.log(forget)
    keyed = 1.0 - forget
    block_count = length // BLOCK

    def split_blocks(arr):
        return arr.reshape(block_count, BLOCK, heads_n, chan)
    doc_blocks = doc_row.astype(jnp.int32).reshape(block_count, BLOCK)
    before = jnp.concatenate([jnp.full((1,), -1, jnp.int32), doc_blocks[:-1, -1]])
    position = jnp.arange(BLOCK)
    causal = position[:, None] >= position[None, :]

    @jax.checkpoint
    def block_step(recurrent_state, pieces):
        query_block, log_b, key_b, value_block, doc_b, prev_doc = pieces
        running_total = jnp.cumsum(log_b, axis=0)
        same_doc = (causal & (doc_b[:, None] == doc_b[None, :]))[:, :, None, None]
        log_gap = running_total[:, None] - running_total[None, :]
        decay = jnp.where(same_doc, jnp.exp(jnp.where(same_doc, log_gap, 0.0)), 0.0)
        scores = jnp.einsum('ihk,jhk,ijhk->ijh', query_block, key_b, decay, precision=lax.Precision.HIGHEST)
        intra = jnp.einsum('ijh,jhv->ihv', scores, value_block, precision=lax.Precision.HIGHEST)
        carried_over = (doc_b == prev_doc).astype(jnp.float32)[:, None, None]
        across_blocks = jnp.einsum('bma,maf->bmf', query_block * jnp.exp(running_total), recurrent_state, precision=lax.Precision.HIGHEST) * carried_over
        block_finish = running_total[-1]
        end_flag = (doc_b == doc_b[-1]).astype(jnp.float32)[:, None, None]
        weighted_values = key_b * jnp.exp(block_finish[None] - running_total) * end_flag
        carry_marker = (doc_b[-1] == prev_doc).astype(jnp.float32)
        recurrent_state = recurrent_state * (jnp.exp(block_finish)[:, :, None] * carry_marker) + jnp.einsum('dmf,dmb->mfb', weighted_values, value_block, precision=lax.Precision.HIGHEST)
        return (recurrent_state, intra + across_blocks)
    start_state = jnp.zeros((heads_n, chan, chan), jnp.float32)
    final_state, results = lax.scan(block_step, start_state, (split_blocks(query), split_blocks(log_forget), split_blocks(keyed), split_blocks(value), doc_blocks, before))
    return results.reshape(length, heads_n, chan)

def block_layer(resid_in, params, doc_rows):
    attn_gain, forget_floor, w_query, w_forget, w_value, w_outgate, w_output, mlp_gain, w_gate, w_up, w_down = params
    flat_rows = resid_in.reshape(-1, D)
    normed = low(flat_rows * row_scale(flat_rows) * attn_gain)
    query = low_back(precise(normed, w_query))
    forget_raw = low_back(precise(normed, w_forget))
    value = low_back(precise(normed, w_value))
    out_gate = low_back(precise(normed, w_outgate))

    def to_heads(arr):
        return arr.reshape(MB, ROWS, NH, HK)
    mixed = jax.vmap(recurrence, in_axes=(0, 0, 0, None, 0))(to_heads(query), to_heads(forget_raw), to_heads(value), forget_floor.reshape(NH, HK), doc_rows).reshape(-1, D)
    gated = low(mixed * jax.nn.silu(out_gate))
    branch = low_back(precise(gated, w_output))
    resid = flat_rows + branch
    normed2 = low(resid * row_scale(resid) * mlp_gain)
    gate_proj = low_back(precise(normed2, w_gate))
    up_proj = low_back(precise(normed2, w_up))
    hidden = low(jax.nn.silu(gate_proj) * up_proj)
    result = resid + precise(hidden, w_down)
    return result.reshape(resid_in.shape)

def reference(tokens, doc_ids, attn_gain, forget_floor, w_query, w_forget, w_value, w_outgate, w_output, mlp_gain, w_gate, w_up, w_down, cotangent):
    params = tuple((item.astype(jnp.float32) for item in (attn_gain, forget_floor, w_query, w_forget, w_value, w_outgate, w_output, mlp_gain, w_gate, w_up, w_down)))

    def group_step(totals, pieces):
        tokens_g, docs_g, cot_g = pieces
        result, pullback = jax.vjp(lambda resid_in, param_in: block_layer(resid_in, param_in, docs_g), tokens_g.astype(jnp.float32), params)
        grad_in, grad_params = pullback(cot_g.astype(jnp.float32))
        totals = jax.tree.map(lambda first, second: first + second, totals, grad_params)
        return (totals, (result.astype(jnp.bfloat16), grad_in))
    zeros = tuple((jnp.zeros_like(item) for item in params))
    totals, (layer_out, grad_tokens) = lax.scan(group_step, zeros, (tokens, doc_ids, cotangent))
    return (layer_out, grad_tokens, totals[0], totals[1], totals[2], totals[3], totals[4], totals[5], totals[6], totals[7], totals[8], totals[9], totals[10])
```

```python
import jax
import jax.numpy as jnp
from jax import lax
from jax.sharding import PartitionSpec as P

HK = 128
BLOCK = 64


epsilon = 1e-06


def row_scale(values):
    return lax.rsqrt(jnp.mean(values * values, axis=-1, keepdims=True) + epsilon)


def silu_slope(values):
    sigmoid_val = jax.nn.sigmoid(values)
    return sigmoid_val * (1.0 + values * (1.0 - sigmoid_val))


def matmul_plain(left, right):
    return jnp.dot(left, right, preferred_element_type=jnp.float32)


def times_trans(left, right):
    return lax.dot_general(
        left, right, (((1,), (1,)), ((), ())), preferred_element_type=jnp.float32
    )


def trans_times(left, right):
    return lax.dot_general(
        left, right, (((0,), (0,)), ((), ())), preferred_element_type=jnp.float32
    )


def recurrence(query, forget_raw, value, floor_vec, doc_row):
    length, heads_n, chan = query.shape
    forget = floor_vec + (1.0 - floor_vec) * jax.nn.sigmoid(forget_raw)
    log_forget = jnp.log(forget)
    keyed = 1.0 - forget
    block_count = length // BLOCK

    def split_blocks(arr):
        return arr.reshape(block_count, BLOCK, heads_n, chan)

    doc_blocks = doc_row.reshape(block_count, BLOCK)
    before = jnp.concatenate([jnp.full((1,), -1, jnp.int32), doc_blocks[:-1, -1]])
    position = jnp.arange(BLOCK)
    causal = position[:, None] >= position[None, :]

    @jax.checkpoint
    def block_step(recurrent_state, pieces):
        query_block, log_b, key_b, value_block, doc_b, prev_doc = pieces
        running_total = jnp.cumsum(log_b, axis=0)
        same_doc = (causal & (doc_b[:, None] == doc_b[None, :]))[:, :, None, None]
        log_gap = running_total[:, None] - running_total[None, :]
        decay = jnp.where(same_doc, jnp.exp(jnp.where(same_doc, log_gap, 0.0)), 0.0)
        scores = jnp.einsum(
            "ihk,jhk,ijhk->ijh", query_block, key_b, decay, precision=lax.Precision.HIGHEST
        )
        intra = jnp.einsum("ijh,jhv->ihv", scores, value_block, precision=lax.Precision.HIGHEST)
        carried_over = (doc_b == prev_doc).astype(jnp.float32)[:, None, None]
        across_blocks = (
            jnp.einsum(
                "bma,maf->bmf",
                query_block * jnp.exp(running_total),
                recurrent_state,
                precision=lax.Precision.HIGHEST,
            )
            * carried_over
        )
        block_finish = running_total[-1]
        end_flag = (doc_b == doc_b[-1]).astype(jnp.float32)[:, None, None]
        weighted_values = key_b * jnp.exp(block_finish[None] - running_total) * end_flag
        carry_marker = (doc_b[-1] == prev_doc).astype(jnp.float32)
        recurrent_state = recurrent_state * (
            jnp.exp(block_finish)[:, :, None] * carry_marker
        ) + jnp.einsum(
            "dmf,dmb->mfb", weighted_values, value_block, precision=lax.Precision.HIGHEST
        )
        return (recurrent_state, intra + across_blocks)

    start_state = jnp.zeros((heads_n, chan, chan), jnp.float32)
    final_state, results = lax.scan(
        block_step,
        start_state,
        (
            split_blocks(query),
            split_blocks(log_forget),
            split_blocks(keyed),
            split_blocks(value),
            doc_blocks,
            before,
        ),
    )
    return results.reshape(length, heads_n, chan)


def row_gather(values):
    count = 4
    spread = jnp.broadcast_to(values[None], (count,) + values.shape)
    got = lax.all_to_all(spread, "tensor", 0, 0, tiled=False)
    return got.reshape((-1,) + values.shape[1:])


def row_sum(values):
    count = 4
    blocks = values.reshape((count, -1) + values.shape[1:])
    got = lax.all_to_all(blocks, "tensor", 0, 0, tiled=False)
    return got.sum(axis=0)


def small_gather(vectors):
    count = 128
    spread = jnp.broadcast_to(vectors[None], (count,) + vectors.shape)
    got = lax.all_to_all(spread, ("dp", "tensor"), 0, 0, tiled=False)
    return jnp.swapaxes(got, 0, 1).reshape(vectors.shape[0], -1)


def small_sum(vectors):
    count = 128
    blocks = vectors.reshape(vectors.shape[0], count, -1)
    got = lax.all_to_all(jnp.swapaxes(blocks, 0, 1), ("dp", "tensor"), 0, 0, tiled=False)
    return got.sum(axis=0)


def shards(
    tokens,
    doc_ids,
    attn_gain,
    forget_floor,
    w_query,
    w_forget,
    w_value,
    w_outgate,
    w_output,
    mlp_gain,
    w_gate,
    w_up,
    w_down,
    cotangent,
):
    gains = small_gather(jnp.stack([attn_gain, forget_floor, mlp_gain]))
    attn_full, floor_full, mlp_full = gains[0], gains[1], gains[2]
    part_index = lax.axis_index("tensor")
    local_width = w_query.shape[1]
    local_heads = local_width // HK
    hidden_width = w_gate.shape[1]
    floor_local = lax.dynamic_slice_in_dim(
        floor_full, part_index * local_width, local_width
    ).reshape(local_heads, HK)
    model_width = attn_full.shape[0]
    doc_all = doc_ids[0]
    row_count = doc_all.shape[0]
    resid_in = tokens[0].reshape(-1, model_width).astype(jnp.float32)
    cot_local = cotangent[0].reshape(-1, model_width)
    attn_pack = jnp.concatenate([w_query, w_forget, w_value, w_outgate, w_output.T], axis=1)
    mlp_pack = jnp.concatenate([w_gate, w_up, w_down.T], axis=1)
    attn_all = lax.all_gather(attn_pack, "dp", axis=0, tiled=True)
    mlp_all = lax.all_gather(mlp_pack, "dp", axis=0, tiled=True)
    wq_all = attn_all[:, 0 * local_width : 1 * local_width]
    wf_all = attn_all[:, 1 * local_width : 2 * local_width]
    wv_all = attn_all[:, 2 * local_width : 3 * local_width]
    wg_all = attn_all[:, 3 * local_width : 4 * local_width]
    wo_t = attn_all[:, 4 * local_width : 5 * local_width]
    wgate_all = mlp_all[:, 0:hidden_width]
    wup_all = mlp_all[:, hidden_width : 2 * hidden_width]
    wdown_t = mlp_all[:, 2 * hidden_width : 3 * hidden_width]
    scale_one = row_scale(resid_in)
    normed = row_gather((resid_in * scale_one * attn_full).astype(jnp.bfloat16))
    query = matmul_plain(normed, wq_all)
    forget_raw = matmul_plain(normed, wf_all)
    value = matmul_plain(normed, wv_all)
    out_gate = matmul_plain(normed, wg_all)

    def mixer(query_in, forget_in, value_in, floor_in):

        def shaped(arr):
            return arr.reshape(row_count, -1, local_heads, HK)

        mixed_rows = jax.vmap(recurrence, in_axes=(0, 0, 0, None, 0))(
            shaped(query_in), shaped(forget_in), shaped(value_in), floor_in, doc_all
        )
        return mixed_rows.reshape(query_in.shape[0], local_width)

    mixed, pullback = jax.vjp(mixer, query, forget_raw, value, floor_local)
    gate_act = jax.nn.silu(out_gate)
    gated = (mixed * gate_act).astype(jnp.bfloat16)
    branch = row_sum(times_trans(gated, wo_t))
    resid = resid_in + branch
    scale_two = row_scale(resid)
    normed2 = row_gather((resid * scale_two * mlp_full).astype(jnp.bfloat16))
    gate_proj = matmul_plain(normed2, wgate_all)
    up_proj = matmul_plain(normed2, wup_all)
    gate_silu = jax.nn.silu(gate_proj)
    hidden = (gate_silu * up_proj).astype(jnp.bfloat16)
    ffn_out = row_sum(times_trans(hidden, wdown_t))
    layer_out = (resid + ffn_out).astype(jnp.bfloat16).reshape(tokens.shape)
    cot_full = row_gather(cot_local)
    d_hidden = matmul_plain(cot_full, wdown_t)
    grad_down_t = trans_times(cot_full, hidden)
    d_gate = (d_hidden * up_proj * silu_slope(gate_proj)).astype(jnp.bfloat16)
    d_up = (d_hidden * gate_silu).astype(jnp.bfloat16)
    grad_gate = trans_times(normed2, d_gate)
    grad_up = trans_times(normed2, d_up)
    mlp_grads = jnp.concatenate(
        [grad_gate.astype(jnp.bfloat16), grad_up.astype(jnp.bfloat16), grad_down_t.astype(jnp.bfloat16)],
        axis=1,
    )
    mlp_red = lax.psum_scatter(mlp_grads, "dp", scatter_dimension=0, tiled=True).astype(jnp.float32)
    d_normed2 = row_sum(times_trans(d_gate, wgate_all) + times_trans(d_up, wup_all))
    grad_mlp = jnp.sum(d_normed2 * resid * scale_two, axis=0)
    inner_two = jnp.mean(d_normed2 * mlp_full * resid, axis=-1, keepdims=True)
    d_resid = (
        cot_local.astype(jnp.float32)
        + d_normed2 * mlp_full * scale_two
        - resid * scale_two**3 * inner_two
    )
    d_branch = row_gather(d_resid.astype(jnp.bfloat16))
    d_gated = matmul_plain(d_branch, wo_t)
    grad_output_t = trans_times(d_branch, gated)
    d_mixed = d_gated * gate_act
    d_outgate = (d_gated * mixed * silu_slope(out_gate)).astype(jnp.bfloat16)
    d_query, d_forget, d_value, d_floor = pullback(d_mixed)
    d_query = d_query.astype(jnp.bfloat16)
    d_forget = d_forget.astype(jnp.bfloat16)
    d_value = d_value.astype(jnp.bfloat16)
    grad_query = trans_times(normed, d_query)
    grad_forget = trans_times(normed, d_forget)
    grad_value = trans_times(normed, d_value)
    grad_outgate = trans_times(normed, d_outgate)
    attn_grads = jnp.concatenate(
        [
            grad_query.astype(jnp.bfloat16),
            grad_forget.astype(jnp.bfloat16),
            grad_value.astype(jnp.bfloat16),
            grad_outgate.astype(jnp.bfloat16),
            grad_output_t.astype(jnp.bfloat16),
        ],
        axis=1,
    )
    attn_red = lax.psum_scatter(attn_grads, "dp", scatter_dimension=0, tiled=True).astype(jnp.float32)
    d_normed = row_sum(
        times_trans(d_query, wq_all)
        + times_trans(d_forget, wf_all)
        + times_trans(d_value, wv_all)
        + times_trans(d_outgate, wg_all)
    )
    grad_attn = jnp.sum(d_normed * resid_in * scale_one, axis=0)
    inner_one = jnp.mean(d_normed * attn_full * resid_in, axis=-1, keepdims=True)
    grad_tokens = (
        d_resid + d_normed * attn_full * scale_one - resid_in * scale_one**3 * inner_one
    ).reshape(tokens.shape)
    floor_vector = lax.dynamic_update_slice(
        jnp.zeros((model_width,), jnp.float32), d_floor.reshape(-1), (part_index * local_width,)
    )
    reduced_small = small_sum(jnp.stack([grad_attn, floor_vector, grad_mlp]))
    return (
        layer_out,
        grad_tokens,
        reduced_small[0],
        reduced_small[1],
        attn_red[:, 0 * local_width : 1 * local_width],
        attn_red[:, 1 * local_width : 2 * local_width],
        attn_red[:, 2 * local_width : 3 * local_width],
        attn_red[:, 3 * local_width : 4 * local_width],
        attn_red[:, 4 * local_width : 5 * local_width].T,
        reduced_small[2],
        mlp_red[:, 0:hidden_width],
        mlp_red[:, hidden_width : 2 * hidden_width],
        mlp_red[:, 2 * hidden_width : 3 * hidden_width].T,
    )


def solution(mesh):
    return jax.shard_map(
        shards,
        mesh=mesh,
        in_specs=(
            P("dp", "tensor", None, None),
            P("dp", None, None),
            P(("dp", "tensor")),
            P(("dp", "tensor")),
            P("dp", "tensor"),
            P("dp", "tensor"),
            P("dp", "tensor"),
            P("dp", "tensor"),
            P("tensor", "dp"),
            P(("dp", "tensor")),
            P("dp", "tensor"),
            P("dp", "tensor"),
            P("tensor", "dp"),
            P("dp", "tensor", None, None),
        ),
        out_specs=(
            P("dp", "tensor", None, None),
            P("dp", "tensor", None, None),
            P(("dp", "tensor")),
            P(("dp", "tensor")),
            P("dp", "tensor"),
            P("dp", "tensor"),
            P("dp", "tensor"),
            P("dp", "tensor"),
            P("tensor", "dp"),
            P(("dp", "tensor")),
            P("dp", "tensor"),
            P("dp", "tensor"),
            P("tensor", "dp"),
        ),
        check_vma=False,
    )
```

```python
import jax
import jax.numpy as jnp
from jax import lax
from jax.sharding import PartitionSpec as P

HK = 128
HIGHEST = lax.Precision.HIGHEST


epsilon = 1e-06


def row_scale(values):
    return lax.rsqrt(jnp.mean(values * values, axis=-1, keepdims=True) + epsilon)


def silu_slope(values):
    sigmoid_val = jax.nn.sigmoid(values)
    return sigmoid_val * (1.0 + values * (1.0 - sigmoid_val))


def matmul_plain(left, right):
    return jnp.dot(left, right, preferred_element_type=jnp.float32)


def times_trans(left, right):
    return lax.dot_general(
        left, right, (((1,), (1,)), ((), ())), preferred_element_type=jnp.float32
    )


def trans_times(left, right):
    return lax.dot_general(
        left, right, (((0,), (0,)), ((), ())), preferred_element_type=jnp.float32
    )


def recurrence(query, forget_raw, value, floor_vec, doc_rows):
    length = query.shape[1]
    forget = floor_vec + (1.0 - floor_vec) * jax.nn.sigmoid(forget_raw)
    log_forget = jnp.log(forget)
    keyed = 1.0 - forget
    position = jnp.arange(length)
    same_doc = doc_rows[:, :, None] == doc_rows[:, None, :]
    causal = same_doc & (position[:, None] >= position[None, :])
    starts = jnp.concatenate(
        [jnp.zeros_like(doc_rows[:, :1], dtype=bool), doc_rows[:, 1:] == doc_rows[:, :-1]], axis=1
    )
    summing = (causal & starts[:, None, :]).astype(jnp.float32)
    running = jnp.einsum("rij,rjhk->rihk", summing, log_forget, precision=HIGHEST)
    query_t = query * jnp.exp(running)
    key_t = keyed * jnp.exp(-running)
    scores = jnp.einsum("rihk,rjhk->rhij", query_t, key_t, precision=HIGHEST)
    scores = jnp.where(causal[:, None], scores, 0.0)
    return jnp.einsum("rhij,rjhv->rihv", scores, value, precision=HIGHEST)


def row_gather(values):
    count = 4
    spread = jnp.broadcast_to(values[None], (count,) + values.shape)
    got = lax.all_to_all(spread, "tensor", 0, 0, tiled=False)
    return got.reshape((-1,) + values.shape[1:])


def row_sum(values):
    count = 4
    blocks = values.reshape((count, -1) + values.shape[1:])
    got = lax.all_to_all(blocks, "tensor", 0, 0, tiled=False)
    return got.sum(axis=0)


def small_gather(vectors):
    count = 128
    spread = jnp.broadcast_to(vectors[None], (count,) + vectors.shape)
    got = lax.all_to_all(spread, ("dp", "tensor"), 0, 0, tiled=False)
    return jnp.swapaxes(got, 0, 1).reshape(vectors.shape[0], -1)


def small_sum(vectors):
    count = 128
    blocks = vectors.reshape(vectors.shape[0], count, -1)
    got = lax.all_to_all(jnp.swapaxes(blocks, 0, 1), ("dp", "tensor"), 0, 0, tiled=False)
    return got.sum(axis=0)


def shards(
    tokens,
    doc_ids,
    attn_gain,
    forget_floor,
    w_query,
    w_forget,
    w_value,
    w_outgate,
    w_output,
    mlp_gain,
    w_gate,
    w_up,
    w_down,
    cotangent,
):
    gains = small_gather(jnp.stack([attn_gain, forget_floor, mlp_gain]))
    attn_full, floor_full, mlp_full = gains[0], gains[1], gains[2]
    part_index = lax.axis_index("tensor")
    local_width = w_query.shape[1]
    local_heads = local_width // HK
    hidden_width = w_gate.shape[1]
    floor_local = lax.dynamic_slice_in_dim(
        floor_full, part_index * local_width, local_width
    ).reshape(local_heads, HK)
    model_width = attn_full.shape[0]
    doc_all = doc_ids[0]
    row_count = doc_all.shape[0]
    resid_in = tokens[0].reshape(-1, model_width).astype(jnp.float32)
    cot_local = cotangent[0].reshape(-1, model_width)
    attn_pack = jnp.concatenate([w_query, w_forget, w_value, w_outgate, w_output.T], axis=1)
    mlp_pack = jnp.concatenate([w_gate, w_up, w_down.T], axis=1)
    attn_all = lax.all_gather(attn_pack, "dp", axis=0, tiled=True)
    mlp_all = lax.all_gather(mlp_pack, "dp", axis=0, tiled=True)
    wq_all = attn_all[:, 0 * local_width : 1 * local_width]
    wf_all = attn_all[:, 1 * local_width : 2 * local_width]
    wv_all = attn_all[:, 2 * local_width : 3 * local_width]
    wg_all = attn_all[:, 3 * local_width : 4 * local_width]
    wo_t = attn_all[:, 4 * local_width : 5 * local_width]
    wgate_all = mlp_all[:, 0:hidden_width]
    wup_all = mlp_all[:, hidden_width : 2 * hidden_width]
    wdown_t = mlp_all[:, 2 * hidden_width : 3 * hidden_width]
    scale_one = row_scale(resid_in)
    normed = row_gather((resid_in * scale_one * attn_full).astype(jnp.bfloat16))
    query = matmul_plain(normed, wq_all)
    forget_raw = matmul_plain(normed, wf_all)
    value = matmul_plain(normed, wv_all)
    out_gate = matmul_plain(normed, wg_all)

    def mixer(query_in, forget_in, value_in, floor_in):

        def shaped(arr):
            return arr.reshape(row_count, -1, local_heads, HK)

        mixed_rows = recurrence(
            shaped(query_in), shaped(forget_in), shaped(value_in), floor_in, doc_all
        )
        return mixed_rows.reshape(query_in.shape[0], local_width)

    mixed, pullback = jax.vjp(mixer, query, forget_raw, value, floor_local)
    gate_act = jax.nn.silu(out_gate)
    gated = (mixed * gate_act).astype(jnp.bfloat16)
    branch = row_sum(times_trans(gated, wo_t))
    resid = resid_in + branch
    scale_two = row_scale(resid)
    normed2 = row_gather((resid * scale_two * mlp_full).astype(jnp.bfloat16))
    gate_proj = matmul_plain(normed2, wgate_all)
    up_proj = matmul_plain(normed2, wup_all)
    gate_silu = jax.nn.silu(gate_proj)
    hidden = (gate_silu * up_proj).astype(jnp.bfloat16)
    ffn_out = row_sum(times_trans(hidden, wdown_t))
    layer_out = (resid + ffn_out).astype(jnp.bfloat16).reshape(tokens.shape)
    cot_full = row_gather(cot_local)
    d_hidden = matmul_plain(cot_full, wdown_t)
    grad_down_t = trans_times(cot_full, hidden)
    d_gate = (d_hidden * up_proj * silu_slope(gate_proj)).astype(jnp.bfloat16)
    d_up = (d_hidden * gate_silu).astype(jnp.bfloat16)
    grad_gate = trans_times(normed2, d_gate)
    grad_up = trans_times(normed2, d_up)
    mlp_grads = jnp.concatenate(
        [grad_gate.astype(jnp.bfloat16), grad_up.astype(jnp.bfloat16), grad_down_t.astype(jnp.bfloat16)],
        axis=1,
    )
    mlp_red = lax.psum_scatter(mlp_grads, "dp", scatter_dimension=0, tiled=True).astype(jnp.float32)
    d_normed2 = row_sum(times_trans(d_gate, wgate_all) + times_trans(d_up, wup_all))
    grad_mlp = jnp.sum(d_normed2 * resid * scale_two, axis=0)
    inner_two = jnp.mean(d_normed2 * mlp_full * resid, axis=-1, keepdims=True)
    d_resid = (
        cot_local.astype(jnp.float32)
        + d_normed2 * mlp_full * scale_two
        - resid * scale_two**3 * inner_two
    )
    d_branch = row_gather(d_resid.astype(jnp.bfloat16))
    d_gated = matmul_plain(d_branch, wo_t)
    grad_output_t = trans_times(d_branch, gated)
    d_mixed = d_gated * gate_act
    d_outgate = (d_gated * mixed * silu_slope(out_gate)).astype(jnp.bfloat16)
    d_query, d_forget, d_value, d_floor = pullback(d_mixed)
    d_query = d_query.astype(jnp.bfloat16)
    d_forget = d_forget.astype(jnp.bfloat16)
    d_value = d_value.astype(jnp.bfloat16)
    grad_query = trans_times(normed, d_query)
    grad_forget = trans_times(normed, d_forget)
    grad_value = trans_times(normed, d_value)
    grad_outgate = trans_times(normed, d_outgate)
    attn_grads = jnp.concatenate(
        [
            grad_query.astype(jnp.bfloat16),
            grad_forget.astype(jnp.bfloat16),
            grad_value.astype(jnp.bfloat16),
            grad_outgate.astype(jnp.bfloat16),
            grad_output_t.astype(jnp.bfloat16),
        ],
        axis=1,
    )
    attn_red = lax.psum_scatter(attn_grads, "dp", scatter_dimension=0, tiled=True).astype(jnp.float32)
    d_normed = row_sum(
        times_trans(d_query, wq_all)
        + times_trans(d_forget, wf_all)
        + times_trans(d_value, wv_all)
        + times_trans(d_outgate, wg_all)
    )
    grad_attn = jnp.sum(d_normed * resid_in * scale_one, axis=0)
    inner_one = jnp.mean(d_normed * attn_full * resid_in, axis=-1, keepdims=True)
    grad_tokens = (
        d_resid + d_normed * attn_full * scale_one - resid_in * scale_one**3 * inner_one
    ).reshape(tokens.shape)
    floor_vector = lax.dynamic_update_slice(
        jnp.zeros((model_width,), jnp.float32), d_floor.reshape(-1), (part_index * local_width,)
    )
    reduced_small = small_sum(jnp.stack([grad_attn, floor_vector, grad_mlp]))
    return (
        layer_out,
        grad_tokens,
        reduced_small[0],
        reduced_small[1],
        attn_red[:, 0 * local_width : 1 * local_width],
        attn_red[:, 1 * local_width : 2 * local_width],
        attn_red[:, 2 * local_width : 3 * local_width],
        attn_red[:, 3 * local_width : 4 * local_width],
        attn_red[:, 4 * local_width : 5 * local_width].T,
        reduced_small[2],
        mlp_red[:, 0:hidden_width],
        mlp_red[:, hidden_width : 2 * hidden_width],
        mlp_red[:, 2 * hidden_width : 3 * hidden_width].T,
    )


def solution(mesh):
    return jax.shard_map(
        shards,
        mesh=mesh,
        in_specs=(
            P("dp", "tensor", None, None),
            P("dp", None, None),
            P(("dp", "tensor")),
            P(("dp", "tensor")),
            P("dp", "tensor"),
            P("dp", "tensor"),
            P("dp", "tensor"),
            P("dp", "tensor"),
            P("tensor", "dp"),
            P(("dp", "tensor")),
            P("dp", "tensor"),
            P("dp", "tensor"),
            P("tensor", "dp"),
            P("dp", "tensor", None, None),
        ),
        out_specs=(
            P("dp", "tensor", None, None),
            P("dp", "tensor", None, None),
            P(("dp", "tensor")),
            P(("dp", "tensor")),
            P("dp", "tensor"),
            P("dp", "tensor"),
            P("dp", "tensor"),
            P("dp", "tensor"),
            P("tensor", "dp"),
            P(("dp", "tensor")),
            P("dp", "tensor"),
            P("dp", "tensor"),
            P("tensor", "dp"),
        ),
        check_vma=False,
    )
```

```python
import jax
import jax.numpy as jnp
from jax import lax
from jax.sharding import PartitionSpec as P

HK = 128
HIGHEST = lax.Precision.HIGHEST


epsilon = 1e-06


def row_scale(values):
    return lax.rsqrt(jnp.mean(values * values, axis=-1, keepdims=True) + epsilon)


def silu_slope(values):
    sigmoid_val = jax.nn.sigmoid(values)
    return sigmoid_val * (1.0 + values * (1.0 - sigmoid_val))


def matmul_plain(left, right):
    return jnp.dot(left, right, preferred_element_type=jnp.float32)


def times_trans(left, right):
    return lax.dot_general(
        left, right, (((1,), (1,)), ((), ())), preferred_element_type=jnp.float32
    )


def trans_times(left, right):
    return lax.dot_general(
        left, right, (((0,), (0,)), ((), ())), preferred_element_type=jnp.float32
    )


def recurrence(query, forget_raw, value, floor_vec, doc_rows):
    length = query.shape[1]
    forget = floor_vec + (1.0 - floor_vec) * jax.nn.sigmoid(forget_raw)
    log_forget = jnp.log(forget)
    keyed = 1.0 - forget
    position = jnp.arange(length)
    same_doc = doc_rows[:, :, None] == doc_rows[:, None, :]
    causal = same_doc & (position[:, None] >= position[None, :])
    starts = jnp.concatenate(
        [jnp.zeros_like(doc_rows[:, :1], dtype=bool), doc_rows[:, 1:] == doc_rows[:, :-1]], axis=1
    )
    summing = (causal & starts[:, None, :]).astype(jnp.float32)
    running = jnp.einsum("rij,rjhk->rihk", summing, log_forget, precision=HIGHEST)
    query_t = query * jnp.exp(running)
    key_t = keyed * jnp.exp(-running)
    scores = jnp.einsum("rihk,rjhk->rhij", query_t, key_t, precision=HIGHEST)
    scores = jnp.where(causal[:, None], scores, 0.0)
    return jnp.einsum("rhij,rjhv->rihv", scores, value, precision=HIGHEST)


ON_CHIP = [(0, 1), (1, 0), (2, 3), (3, 2)]
ACROSS = [(0, 2), (2, 0), (1, 3), (3, 1)]
SLOT_XOR = (0, 2, 1, 3)


def row_gather(values):
    across = lax.ppermute(values, "tensor", ACROSS)
    pair = jnp.stack([values, across])
    other = lax.ppermute(pair, "tensor", ON_CHIP)
    return jnp.concatenate([pair, other]).reshape((-1,) + values.shape[1:])


def row_sum(values):
    blocks = values.reshape((4, -1) + values.shape[1:])
    got = lax.ppermute(blocks[2:], "tensor", ON_CHIP)
    mine = blocks[0] + got[0]
    theirs = blocks[1] + got[1]
    return mine + lax.ppermute(theirs, "tensor", ACROSS)


def small_gather(vectors):
    count = 128
    spread = jnp.broadcast_to(vectors[None], (count,) + vectors.shape)
    got = lax.all_to_all(spread, ("dp", "tensor"), 0, 0, tiled=False)
    return jnp.swapaxes(got, 0, 1).reshape(vectors.shape[0], -1)


def small_sum(vectors):
    count = 128
    blocks = vectors.reshape(vectors.shape[0], count, -1)
    got = lax.all_to_all(jnp.swapaxes(blocks, 0, 1), ("dp", "tensor"), 0, 0, tiled=False)
    return got.sum(axis=0)


def shards(
    tokens,
    doc_ids,
    attn_gain,
    forget_floor,
    w_query,
    w_forget,
    w_value,
    w_outgate,
    w_output,
    mlp_gain,
    w_gate,
    w_up,
    w_down,
    cotangent,
):
    gains = small_gather(jnp.stack([attn_gain, forget_floor, mlp_gain]))
    attn_full, floor_full, mlp_full = gains[0], gains[1], gains[2]
    part_index = lax.axis_index("tensor")
    local_width = w_query.shape[1]
    local_heads = local_width // HK
    hidden_width = w_gate.shape[1]
    floor_local = lax.dynamic_slice_in_dim(
        floor_full, part_index * local_width, local_width
    ).reshape(local_heads, HK)
    model_width = attn_full.shape[0]
    slot_rows = jnp.bitwise_xor(part_index, jnp.array(SLOT_XOR, jnp.int32))
    doc_all = jnp.take(doc_ids[0], slot_rows, axis=0)
    row_count = doc_all.shape[0]
    resid_in = tokens[0].reshape(-1, model_width).astype(jnp.float32)
    cot_local = cotangent[0].reshape(-1, model_width)
    attn_pack = jnp.concatenate([w_query, w_forget, w_value, w_outgate, w_output.T], axis=1)
    mlp_pack = jnp.concatenate([w_gate, w_up, w_down.T], axis=1)
    attn_all = lax.all_gather(attn_pack, "dp", axis=0, tiled=True)
    mlp_all = lax.all_gather(mlp_pack, "dp", axis=0, tiled=True)
    wq_all = attn_all[:, 0 * local_width : 1 * local_width]
    wf_all = attn_all[:, 1 * local_width : 2 * local_width]
    wv_all = attn_all[:, 2 * local_width : 3 * local_width]
    wg_all = attn_all[:, 3 * local_width : 4 * local_width]
    wo_t = attn_all[:, 4 * local_width : 5 * local_width]
    wgate_all = mlp_all[:, 0:hidden_width]
    wup_all = mlp_all[:, hidden_width : 2 * hidden_width]
    wdown_t = mlp_all[:, 2 * hidden_width : 3 * hidden_width]
    scale_one = row_scale(resid_in)
    normed = row_gather((resid_in * scale_one * attn_full).astype(jnp.bfloat16))
    query = matmul_plain(normed, wq_all)
    forget_raw = matmul_plain(normed, wf_all)
    value = matmul_plain(normed, wv_all)
    out_gate = matmul_plain(normed, wg_all)

    def mixer(query_in, forget_in, value_in, floor_in):

        def shaped(arr):
            return arr.reshape(row_count, -1, local_heads, HK)

        mixed_rows = recurrence(
            shaped(query_in), shaped(forget_in), shaped(value_in), floor_in, doc_all
        )
        return mixed_rows.reshape(query_in.shape[0], local_width)

    mixed, pullback = jax.vjp(mixer, query, forget_raw, value, floor_local)
    gate_act = jax.nn.silu(out_gate)
    gated = (mixed * gate_act).astype(jnp.bfloat16)
    branch = row_sum(times_trans(gated, wo_t))
    resid = resid_in + branch
    scale_two = row_scale(resid)
    normed2 = row_gather((resid * scale_two * mlp_full).astype(jnp.bfloat16))
    gate_proj = matmul_plain(normed2, wgate_all)
    up_proj = matmul_plain(normed2, wup_all)
    gate_silu = jax.nn.silu(gate_proj)
    hidden = (gate_silu * up_proj).astype(jnp.bfloat16)
    ffn_out = row_sum(times_trans(hidden, wdown_t))
    layer_out = (resid + ffn_out).astype(jnp.bfloat16).reshape(tokens.shape)
    cot_full = row_gather(cot_local)
    d_hidden = matmul_plain(cot_full, wdown_t)
    grad_down_t = trans_times(cot_full, hidden)
    d_gate = (d_hidden * up_proj * silu_slope(gate_proj)).astype(jnp.bfloat16)
    d_up = (d_hidden * gate_silu).astype(jnp.bfloat16)
    grad_gate = trans_times(normed2, d_gate)
    grad_up = trans_times(normed2, d_up)
    mlp_grads = jnp.concatenate(
        [grad_gate.astype(jnp.bfloat16), grad_up.astype(jnp.bfloat16), grad_down_t.astype(jnp.bfloat16)],
        axis=1,
    )
    mlp_red = lax.psum_scatter(mlp_grads, "dp", scatter_dimension=0, tiled=True).astype(jnp.float32)
    d_normed2 = row_sum(times_trans(d_gate, wgate_all) + times_trans(d_up, wup_all))
    grad_mlp = jnp.sum(d_normed2 * resid * scale_two, axis=0)
    inner_two = jnp.mean(d_normed2 * mlp_full * resid, axis=-1, keepdims=True)
    d_resid = (
        cot_local.astype(jnp.float32)
        + d_normed2 * mlp_full * scale_two
        - resid * scale_two**3 * inner_two
    )
    d_branch = row_gather(d_resid.astype(jnp.bfloat16))
    d_gated = matmul_plain(d_branch, wo_t)
    grad_output_t = trans_times(d_branch, gated)
    d_mixed = d_gated * gate_act
    d_outgate = (d_gated * mixed * silu_slope(out_gate)).astype(jnp.bfloat16)
    d_query, d_forget, d_value, d_floor = pullback(d_mixed)
    d_query = d_query.astype(jnp.bfloat16)
    d_forget = d_forget.astype(jnp.bfloat16)
    d_value = d_value.astype(jnp.bfloat16)
    grad_query = trans_times(normed, d_query)
    grad_forget = trans_times(normed, d_forget)
    grad_value = trans_times(normed, d_value)
    grad_outgate = trans_times(normed, d_outgate)
    attn_grads = jnp.concatenate(
        [
            grad_query.astype(jnp.bfloat16),
            grad_forget.astype(jnp.bfloat16),
            grad_value.astype(jnp.bfloat16),
            grad_outgate.astype(jnp.bfloat16),
            grad_output_t.astype(jnp.bfloat16),
        ],
        axis=1,
    )
    attn_red = lax.psum_scatter(attn_grads, "dp", scatter_dimension=0, tiled=True).astype(jnp.float32)
    d_normed = row_sum(
        times_trans(d_query, wq_all)
        + times_trans(d_forget, wf_all)
        + times_trans(d_value, wv_all)
        + times_trans(d_outgate, wg_all)
    )
    grad_attn = jnp.sum(d_normed * resid_in * scale_one, axis=0)
    inner_one = jnp.mean(d_normed * attn_full * resid_in, axis=-1, keepdims=True)
    grad_tokens = (
        d_resid + d_normed * attn_full * scale_one - resid_in * scale_one**3 * inner_one
    ).reshape(tokens.shape)
    floor_vector = lax.dynamic_update_slice(
        jnp.zeros((model_width,), jnp.float32), d_floor.reshape(-1), (part_index * local_width,)
    )
    reduced_small = small_sum(jnp.stack([grad_attn, floor_vector, grad_mlp]))
    return (
        layer_out,
        grad_tokens,
        reduced_small[0],
        reduced_small[1],
        attn_red[:, 0 * local_width : 1 * local_width],
        attn_red[:, 1 * local_width : 2 * local_width],
        attn_red[:, 2 * local_width : 3 * local_width],
        attn_red[:, 3 * local_width : 4 * local_width],
        attn_red[:, 4 * local_width : 5 * local_width].T,
        reduced_small[2],
        mlp_red[:, 0:hidden_width],
        mlp_red[:, hidden_width : 2 * hidden_width],
        mlp_red[:, 2 * hidden_width : 3 * hidden_width].T,
    )


def solution(mesh):
    return jax.shard_map(
        shards,
        mesh=mesh,
        in_specs=(
            P("dp", "tensor", None, None),
            P("dp", None, None),
            P(("dp", "tensor")),
            P(("dp", "tensor")),
            P("dp", "tensor"),
            P("dp", "tensor"),
            P("dp", "tensor"),
            P("dp", "tensor"),
            P("tensor", "dp"),
            P(("dp", "tensor")),
            P("dp", "tensor"),
            P("dp", "tensor"),
            P("tensor", "dp"),
            P("dp", "tensor", None, None),
        ),
        out_specs=(
            P("dp", "tensor", None, None),
            P("dp", "tensor", None, None),
            P(("dp", "tensor")),
            P(("dp", "tensor")),
            P("dp", "tensor"),
            P("dp", "tensor"),
            P("dp", "tensor"),
            P("dp", "tensor"),
            P("tensor", "dp"),
            P(("dp", "tensor")),
            P("dp", "tensor"),
            P("dp", "tensor"),
            P("tensor", "dp"),
        ),
        check_vma=False,
    )
```

```python
import jax
import jax.numpy as jnp
from jax import lax
from jax.sharding import PartitionSpec as P

HK = 128
HIGHEST = lax.Precision.HIGHEST


epsilon = 1e-06


def row_scale(values):
    return lax.rsqrt(jnp.mean(values * values, axis=-1, keepdims=True) + epsilon)


def silu_slope(values):
    sigmoid_val = jax.nn.sigmoid(values)
    return sigmoid_val * (1.0 + values * (1.0 - sigmoid_val))


def matmul_plain(left, right):
    return jnp.dot(left, right, preferred_element_type=jnp.float32)


def times_trans(left, right):
    return lax.dot_general(
        left, right, (((1,), (1,)), ((), ())), preferred_element_type=jnp.float32
    )


def trans_times(left, right):
    return lax.dot_general(
        left, right, (((0,), (0,)), ((), ())), preferred_element_type=jnp.float32
    )


def recurrence(query, forget_raw, value, floor_vec, doc_rows):
    length = query.shape[1]
    forget = floor_vec + (1.0 - floor_vec) * jax.nn.sigmoid(forget_raw)
    log_forget = jnp.log(forget)
    keyed = 1.0 - forget
    position = jnp.arange(length)
    same_doc = doc_rows[:, :, None] == doc_rows[:, None, :]
    causal = same_doc & (position[:, None] >= position[None, :])
    starts = jnp.concatenate(
        [jnp.zeros_like(doc_rows[:, :1], dtype=bool), doc_rows[:, 1:] == doc_rows[:, :-1]], axis=1
    )
    summing = (causal & starts[:, None, :]).astype(jnp.float32)
    running = jnp.einsum("rij,rjhk->rihk", summing, log_forget, precision=HIGHEST)
    query_t = query * jnp.exp(running)
    key_t = keyed * jnp.exp(-running)
    scores = jnp.einsum("rihk,rjhk->rhij", query_t, key_t, precision=HIGHEST)
    scores = jnp.where(causal[:, None], scores, 0.0)
    return jnp.einsum("rhij,rjhv->rihv", scores, value, precision=HIGHEST)


ON_CHIP = [(0, 1), (1, 0), (2, 3), (3, 2)]
ACROSS = [(0, 2), (2, 0), (1, 3), (3, 1)]
SLOT_XOR = (0, 2, 1, 3)


def row_gather(values):
    across = lax.ppermute(values, "tensor", ACROSS)
    pair = jnp.stack([values, across])
    other = lax.ppermute(pair, "tensor", ON_CHIP)
    return jnp.concatenate([pair, other]).reshape((-1,) + values.shape[1:])


def row_sum(values):
    blocks = values.reshape((4, -1) + values.shape[1:])
    got = lax.ppermute(blocks[2:], "tensor", ON_CHIP)
    mine = blocks[0] + got[0]
    theirs = blocks[1] + got[1]
    return mine + lax.ppermute(theirs, "tensor", ACROSS)


def spread_sum(values, axis, count):
    blocks = values.reshape((count, -1) + values.shape[1:])
    got = lax.all_to_all(blocks, axis, 0, 0, tiled=False)
    return got.astype(jnp.float32).sum(axis=0)


def small_gather(vectors):
    count = 128
    spread = jnp.broadcast_to(vectors[None], (count,) + vectors.shape)
    got = lax.all_to_all(spread, ("dp", "tensor"), 0, 0, tiled=False)
    return jnp.swapaxes(got, 0, 1).reshape(vectors.shape[0], -1)


def small_sum(vectors):
    count = 128
    blocks = vectors.reshape(vectors.shape[0], count, -1)
    got = lax.all_to_all(jnp.swapaxes(blocks, 0, 1), ("dp", "tensor"), 0, 0, tiled=False)
    return got.sum(axis=0)


def shards(
    tokens,
    doc_ids,
    attn_gain,
    forget_floor,
    w_query,
    w_forget,
    w_value,
    w_outgate,
    w_output,
    mlp_gain,
    w_gate,
    w_up,
    w_down,
    cotangent,
):
    gains = small_gather(jnp.stack([attn_gain, forget_floor, mlp_gain]))
    attn_full, floor_full, mlp_full = gains[0], gains[1], gains[2]
    part_index = lax.axis_index("tensor")
    local_width = w_query.shape[1]
    local_heads = local_width // HK
    hidden_width = w_gate.shape[1]
    floor_local = lax.dynamic_slice_in_dim(
        floor_full, part_index * local_width, local_width
    ).reshape(local_heads, HK)
    model_width = attn_full.shape[0]
    slot_rows = jnp.bitwise_xor(part_index, jnp.array(SLOT_XOR, jnp.int32))
    doc_all = jnp.take(doc_ids[0], slot_rows, axis=0)
    row_count = doc_all.shape[0]
    resid_in = tokens[0].reshape(-1, model_width).astype(jnp.float32)
    cot_local = cotangent[0].reshape(-1, model_width)
    attn_pack = jnp.concatenate([w_query, w_forget, w_value, w_outgate, w_output.T], axis=1)
    mlp_pack = jnp.concatenate([w_gate, w_up, w_down.T], axis=1)
    attn_all = lax.all_gather(attn_pack, "dp", axis=0, tiled=True)
    mlp_all = lax.all_gather(mlp_pack, "dp", axis=0, tiled=True)
    wq_all = attn_all[:, 0 * local_width : 1 * local_width]
    wf_all = attn_all[:, 1 * local_width : 2 * local_width]
    wv_all = attn_all[:, 2 * local_width : 3 * local_width]
    wg_all = attn_all[:, 3 * local_width : 4 * local_width]
    wo_t = attn_all[:, 4 * local_width : 5 * local_width]
    wgate_all = mlp_all[:, 0:hidden_width]
    wup_all = mlp_all[:, hidden_width : 2 * hidden_width]
    wdown_t = mlp_all[:, 2 * hidden_width : 3 * hidden_width]
    scale_one = row_scale(resid_in)
    normed = row_gather((resid_in * scale_one * attn_full).astype(jnp.bfloat16))
    query = matmul_plain(normed, wq_all)
    forget_raw = matmul_plain(normed, wf_all)
    value = matmul_plain(normed, wv_all)
    out_gate = matmul_plain(normed, wg_all)

    def mixer(query_in, forget_in, value_in, floor_in):

        def shaped(arr):
            return arr.reshape(row_count, -1, local_heads, HK)

        mixed_rows = recurrence(
            shaped(query_in), shaped(forget_in), shaped(value_in), floor_in, doc_all
        )
        return mixed_rows.reshape(query_in.shape[0], local_width)

    mixed, pullback = jax.vjp(mixer, query, forget_raw, value, floor_local)
    gate_act = jax.nn.silu(out_gate)
    gated = (mixed * gate_act).astype(jnp.bfloat16)
    branch = row_sum(times_trans(gated, wo_t))
    resid = resid_in + branch
    scale_two = row_scale(resid)
    normed2 = row_gather((resid * scale_two * mlp_full).astype(jnp.bfloat16))
    gate_proj = matmul_plain(normed2, wgate_all)
    up_proj = matmul_plain(normed2, wup_all)
    gate_silu = jax.nn.silu(gate_proj)
    hidden = (gate_silu * up_proj).astype(jnp.bfloat16)
    ffn_out = row_sum(times_trans(hidden, wdown_t))
    layer_out = (resid + ffn_out).astype(jnp.bfloat16).reshape(tokens.shape)
    cot_full = row_gather(cot_local)
    d_hidden = matmul_plain(cot_full, wdown_t)
    grad_down_t = trans_times(cot_full, hidden)
    d_gate = (d_hidden * up_proj * silu_slope(gate_proj)).astype(jnp.bfloat16)
    d_up = (d_hidden * gate_silu).astype(jnp.bfloat16)
    grad_gate = trans_times(normed2, d_gate)
    grad_up = trans_times(normed2, d_up)
    mlp_grads = jnp.concatenate(
        [grad_gate.astype(jnp.bfloat16), grad_up.astype(jnp.bfloat16), grad_down_t.astype(jnp.bfloat16)],
        axis=1,
    )
    mlp_red = lax.psum_scatter(mlp_grads, "dp", scatter_dimension=0, tiled=True).astype(jnp.float32)
    d_normed2 = row_sum(times_trans(d_gate, wgate_all) + times_trans(d_up, wup_all))
    grad_mlp = jnp.sum(d_normed2 * resid * scale_two, axis=0)
    inner_two = jnp.mean(d_normed2 * mlp_full * resid, axis=-1, keepdims=True)
    d_resid = (
        cot_local.astype(jnp.float32)
        + d_normed2 * mlp_full * scale_two
        - resid * scale_two**3 * inner_two
    )
    d_branch = row_gather(d_resid.astype(jnp.bfloat16))
    d_gated = matmul_plain(d_branch, wo_t)
    grad_output_t = trans_times(d_branch, gated)
    d_mixed = d_gated * gate_act
    d_outgate = (d_gated * mixed * silu_slope(out_gate)).astype(jnp.bfloat16)
    d_query, d_forget, d_value, d_floor = pullback(d_mixed)
    d_query = d_query.astype(jnp.bfloat16)
    d_forget = d_forget.astype(jnp.bfloat16)
    d_value = d_value.astype(jnp.bfloat16)
    grad_query = trans_times(normed, d_query)
    grad_forget = trans_times(normed, d_forget)
    grad_value = trans_times(normed, d_value)
    grad_outgate = trans_times(normed, d_outgate)
    attn_grads = jnp.concatenate(
        [
            grad_query.astype(jnp.bfloat16),
            grad_forget.astype(jnp.bfloat16),
            grad_value.astype(jnp.bfloat16),
            grad_outgate.astype(jnp.bfloat16),
            grad_output_t.astype(jnp.bfloat16),
        ],
        axis=1,
    )
    attn_red = spread_sum(attn_grads, "dp", 32)
    d_normed = row_sum(
        times_trans(d_query, wq_all)
        + times_trans(d_forget, wf_all)
        + times_trans(d_value, wv_all)
        + times_trans(d_outgate, wg_all)
    )
    grad_attn = jnp.sum(d_normed * resid_in * scale_one, axis=0)
    inner_one = jnp.mean(d_normed * attn_full * resid_in, axis=-1, keepdims=True)
    grad_tokens = (
        d_resid + d_normed * attn_full * scale_one - resid_in * scale_one**3 * inner_one
    ).reshape(tokens.shape)
    floor_vector = lax.dynamic_update_slice(
        jnp.zeros((model_width,), jnp.float32), d_floor.reshape(-1), (part_index * local_width,)
    )
    reduced_small = small_sum(jnp.stack([grad_attn, floor_vector, grad_mlp]))
    return (
        layer_out,
        grad_tokens,
        reduced_small[0],
        reduced_small[1],
        attn_red[:, 0 * local_width : 1 * local_width],
        attn_red[:, 1 * local_width : 2 * local_width],
        attn_red[:, 2 * local_width : 3 * local_width],
        attn_red[:, 3 * local_width : 4 * local_width],
        attn_red[:, 4 * local_width : 5 * local_width].T,
        reduced_small[2],
        mlp_red[:, 0:hidden_width],
        mlp_red[:, hidden_width : 2 * hidden_width],
        mlp_red[:, 2 * hidden_width : 3 * hidden_width].T,
    )


def solution(mesh):
    return jax.shard_map(
        shards,
        mesh=mesh,
        in_specs=(
            P("dp", "tensor", None, None),
            P("dp", None, None),
            P(("dp", "tensor")),
            P(("dp", "tensor")),
            P("dp", "tensor"),
            P("dp", "tensor"),
            P("dp", "tensor"),
            P("dp", "tensor"),
            P("tensor", "dp"),
            P(("dp", "tensor")),
            P("dp", "tensor"),
            P("dp", "tensor"),
            P("tensor", "dp"),
            P("dp", "tensor", None, None),
        ),
        out_specs=(
            P("dp", "tensor", None, None),
            P("dp", "tensor", None, None),
            P(("dp", "tensor")),
            P(("dp", "tensor")),
            P("dp", "tensor"),
            P("dp", "tensor"),
            P("dp", "tensor"),
            P("dp", "tensor"),
            P("tensor", "dp"),
            P(("dp", "tensor")),
            P("dp", "tensor"),
            P("dp", "tensor"),
            P("tensor", "dp"),
        ),
        check_vma=False,
    )
```

```python
import functools

import jax
import jax.numpy as jnp
from jax import lax
from jax.experimental import pallas as pl
from jax.experimental.pallas import tpu as pltpu
from jax.sharding import PartitionSpec as P

HK = 128
HIGHEST = lax.Precision.HIGHEST


epsilon = 1e-06


def row_scale(values):
    return lax.rsqrt(jnp.mean(values * values, axis=-1, keepdims=True) + epsilon)


def silu_slope(values):
    sigmoid_val = jax.nn.sigmoid(values)
    return sigmoid_val * (1.0 + values * (1.0 - sigmoid_val))


def matmul_plain(left, right):
    return jnp.dot(left, right, preferred_element_type=jnp.float32)


def times_trans(left, right):
    return lax.dot_general(
        left, right, (((1,), (1,)), ((), ())), preferred_element_type=jnp.float32
    )


def trans_times(left, right):
    return lax.dot_general(
        left, right, (((0,), (0,)), ((), ())), preferred_element_type=jnp.float32
    )


def pack_kernel(per, first_ref, second_ref, right_ref, out_ref):
    col = pl.program_id(1)

    @pl.when(col < per)
    def _():
        out_ref[...] = jnp.dot(
            first_ref[...].T, right_ref[...], preferred_element_type=jnp.float32
        ).astype(out_ref.dtype)

    @pl.when(col >= per)
    def _():
        out_ref[...] = jnp.dot(
            second_ref[...].T, right_ref[...], preferred_element_type=jnp.float32
        ).astype(out_ref.dtype)


def grad_pack(first, second, right, width):
    depth, rows_out = first.shape
    cols = right.shape[1]
    blocks = cols // width
    per = blocks - 1
    tile = 512
    return pl.pallas_call(
        functools.partial(pack_kernel, per),
        grid=(rows_out // tile, blocks),
        in_specs=[
            pl.BlockSpec((depth, tile), lambda i, j: (0, i)),
            pl.BlockSpec((depth, tile), lambda i, j: (0, i)),
            pl.BlockSpec((depth, width), lambda i, j: (0, j)),
        ],
        out_specs=pl.BlockSpec((tile, width), lambda i, j: (i, j)),
        out_shape=jax.ShapeDtypeStruct((rows_out, cols), jnp.bfloat16),
        cost_estimate=pl.CostEstimate(
            flops=2 * depth * rows_out * cols,
            transcendentals=0,
            bytes_accessed=2 * (2 * depth * rows_out + depth * cols + rows_out * cols),
        ),
    )(first, second, right)


def recurrence(query, forget_raw, value, floor_vec, doc_rows):
    length = query.shape[1]
    forget = floor_vec + (1.0 - floor_vec) * jax.nn.sigmoid(forget_raw)
    log_forget = jnp.log(forget)
    keyed = 1.0 - forget
    position = jnp.arange(length)
    same_doc = doc_rows[:, :, None] == doc_rows[:, None, :]
    causal = same_doc & (position[:, None] >= position[None, :])
    starts = jnp.concatenate(
        [jnp.zeros_like(doc_rows[:, :1], dtype=bool), doc_rows[:, 1:] == doc_rows[:, :-1]], axis=1
    )
    summing = (causal & starts[:, None, :]).astype(jnp.float32)
    running = jnp.einsum("rij,rjhk->rihk", summing, log_forget, precision=HIGHEST)
    query_t = query * jnp.exp(running)
    key_t = keyed * jnp.exp(-running)
    scores = jnp.einsum("rihk,rjhk->rhij", query_t, key_t, precision=HIGHEST)
    scores = jnp.where(causal[:, None], scores, 0.0)
    return jnp.einsum("rhij,rjhv->rihv", scores, value, precision=HIGHEST)


ON_CHIP = [(0, 1), (1, 0), (2, 3), (3, 2)]
ACROSS = [(0, 2), (2, 0), (1, 3), (3, 1)]
SLOT_XOR = (0, 2, 1, 3)


def row_gather(values):
    across = lax.ppermute(values, "tensor", ACROSS)
    pair = jnp.stack([values, across])
    other = lax.ppermute(pair, "tensor", ON_CHIP)
    return jnp.concatenate([pair, other]).reshape((-1,) + values.shape[1:])


def row_sum(values):
    blocks = values.reshape((4, -1) + values.shape[1:])
    got = lax.ppermute(blocks[2:], "tensor", ON_CHIP)
    mine = blocks[0] + got[0]
    theirs = blocks[1] + got[1]
    return mine + lax.ppermute(theirs, "tensor", ACROSS)


def spread_sum(values, axis, count):
    blocks = values.reshape((count, -1) + values.shape[1:])
    got = lax.all_to_all(blocks, axis, 0, 0, tiled=False)
    return got.astype(jnp.float32).sum(axis=0)


def small_gather(vectors):
    count = 128
    spread = jnp.broadcast_to(vectors[None], (count,) + vectors.shape)
    got = lax.all_to_all(spread, ("dp", "tensor"), 0, 0, tiled=False)
    return jnp.swapaxes(got, 0, 1).reshape(vectors.shape[0], -1)


def small_sum(vectors):
    count = 128
    blocks = vectors.reshape(vectors.shape[0], count, -1)
    got = lax.all_to_all(jnp.swapaxes(blocks, 0, 1), ("dp", "tensor"), 0, 0, tiled=False)
    return got.sum(axis=0)


def shards(
    tokens,
    doc_ids,
    attn_gain,
    forget_floor,
    w_query,
    w_forget,
    w_value,
    w_outgate,
    w_output,
    mlp_gain,
    w_gate,
    w_up,
    w_down,
    cotangent,
):
    gains = small_gather(jnp.stack([attn_gain, forget_floor, mlp_gain]))
    attn_full, floor_full, mlp_full = gains[0], gains[1], gains[2]
    part_index = lax.axis_index("tensor")
    local_width = w_query.shape[1]
    local_heads = local_width // HK
    hidden_width = w_gate.shape[1]
    floor_local = lax.dynamic_slice_in_dim(
        floor_full, part_index * local_width, local_width
    ).reshape(local_heads, HK)
    model_width = attn_full.shape[0]
    slot_rows = jnp.bitwise_xor(part_index, jnp.array(SLOT_XOR, jnp.int32))
    doc_all = jnp.take(doc_ids[0], slot_rows, axis=0)
    row_count = doc_all.shape[0]
    resid_in = tokens[0].reshape(-1, model_width).astype(jnp.float32)
    cot_local = cotangent[0].reshape(-1, model_width)
    attn_pack = jnp.concatenate([w_query, w_forget, w_value, w_outgate, w_output.T], axis=1)
    mlp_pack = jnp.concatenate([w_gate, w_up, w_down.T], axis=1)
    attn_all = lax.all_gather(attn_pack, "dp", axis=0, tiled=True)
    mlp_all = lax.all_gather(mlp_pack, "dp", axis=0, tiled=True)
    wq_all = attn_all[:, 0 * local_width : 1 * local_width]
    wf_all = attn_all[:, 1 * local_width : 2 * local_width]
    wv_all = attn_all[:, 2 * local_width : 3 * local_width]
    wg_all = attn_all[:, 3 * local_width : 4 * local_width]
    wo_t = attn_all[:, 4 * local_width : 5 * local_width]
    wgate_all = mlp_all[:, 0:hidden_width]
    wup_all = mlp_all[:, hidden_width : 2 * hidden_width]
    wdown_t = mlp_all[:, 2 * hidden_width : 3 * hidden_width]
    scale_one = row_scale(resid_in)
    normed = row_gather((resid_in * scale_one * attn_full).astype(jnp.bfloat16))
    query = matmul_plain(normed, wq_all)
    forget_raw = matmul_plain(normed, wf_all)
    value = matmul_plain(normed, wv_all)
    out_gate = matmul_plain(normed, wg_all)

    def mixer(query_in, forget_in, value_in, floor_in):

        def shaped(arr):
            return arr.reshape(row_count, -1, local_heads, HK)

        mixed_rows = recurrence(
            shaped(query_in), shaped(forget_in), shaped(value_in), floor_in, doc_all
        )
        return mixed_rows.reshape(query_in.shape[0], local_width)

    mixed, pullback = jax.vjp(mixer, query, forget_raw, value, floor_local)
    gate_act = jax.nn.silu(out_gate)
    gated = (mixed * gate_act).astype(jnp.bfloat16)
    branch = row_sum(times_trans(gated, wo_t))
    resid = resid_in + branch
    scale_two = row_scale(resid)
    normed2 = row_gather((resid * scale_two * mlp_full).astype(jnp.bfloat16))
    gate_proj = matmul_plain(normed2, wgate_all)
    up_proj = matmul_plain(normed2, wup_all)
    gate_silu = jax.nn.silu(gate_proj)
    hidden = (gate_silu * up_proj).astype(jnp.bfloat16)
    ffn_out = row_sum(times_trans(hidden, wdown_t))
    layer_out = (resid + ffn_out).astype(jnp.bfloat16).reshape(tokens.shape)
    cot_full = row_gather(cot_local)
    d_hidden = matmul_plain(cot_full, wdown_t)
    d_gate = (d_hidden * up_proj * silu_slope(gate_proj)).astype(jnp.bfloat16)
    d_up = (d_hidden * gate_silu).astype(jnp.bfloat16)
    mlp_grads = grad_pack(
        normed2, cot_full, jnp.concatenate([d_gate, d_up, hidden], axis=1), hidden_width
    )
    mlp_red = lax.psum_scatter(mlp_grads, "dp", scatter_dimension=0, tiled=True).astype(jnp.float32)
    d_normed2 = row_sum(times_trans(d_gate, wgate_all) + times_trans(d_up, wup_all))
    grad_mlp = jnp.sum(d_normed2 * resid * scale_two, axis=0)
    inner_two = jnp.mean(d_normed2 * mlp_full * resid, axis=-1, keepdims=True)
    d_resid = (
        cot_local.astype(jnp.float32)
        + d_normed2 * mlp_full * scale_two
        - resid * scale_two**3 * inner_two
    )
    d_branch = row_gather(d_resid.astype(jnp.bfloat16))
    d_gated = matmul_plain(d_branch, wo_t)
    d_mixed = d_gated * gate_act
    d_outgate = (d_gated * mixed * silu_slope(out_gate)).astype(jnp.bfloat16)
    d_query, d_forget, d_value, d_floor = pullback(d_mixed)
    d_query = d_query.astype(jnp.bfloat16)
    d_forget = d_forget.astype(jnp.bfloat16)
    d_value = d_value.astype(jnp.bfloat16)
    attn_grads = grad_pack(
        normed,
        d_branch,
        jnp.concatenate([d_query, d_forget, d_value, d_outgate, gated], axis=1),
        local_width,
    )
    attn_red = spread_sum(attn_grads, "dp", 32)
    d_normed = row_sum(
        times_trans(d_query, wq_all)
        + times_trans(d_forget, wf_all)
        + times_trans(d_value, wv_all)
        + times_trans(d_outgate, wg_all)
    )
    grad_attn = jnp.sum(d_normed * resid_in * scale_one, axis=0)
    inner_one = jnp.mean(d_normed * attn_full * resid_in, axis=-1, keepdims=True)
    grad_tokens = (
        d_resid + d_normed * attn_full * scale_one - resid_in * scale_one**3 * inner_one
    ).reshape(tokens.shape)
    floor_vector = lax.dynamic_update_slice(
        jnp.zeros((model_width,), jnp.float32), d_floor.reshape(-1), (part_index * local_width,)
    )
    reduced_small = small_sum(jnp.stack([grad_attn, floor_vector, grad_mlp]))
    return (
        layer_out,
        grad_tokens,
        reduced_small[0],
        reduced_small[1],
        attn_red[:, 0 * local_width : 1 * local_width],
        attn_red[:, 1 * local_width : 2 * local_width],
        attn_red[:, 2 * local_width : 3 * local_width],
        attn_red[:, 3 * local_width : 4 * local_width],
        attn_red[:, 4 * local_width : 5 * local_width].T,
        reduced_small[2],
        mlp_red[:, 0:hidden_width],
        mlp_red[:, hidden_width : 2 * hidden_width],
        mlp_red[:, 2 * hidden_width : 3 * hidden_width].T,
    )


def solution(mesh):
    return jax.shard_map(
        shards,
        mesh=mesh,
        in_specs=(
            P("dp", "tensor", None, None),
            P("dp", None, None),
            P(("dp", "tensor")),
            P(("dp", "tensor")),
            P("dp", "tensor"),
            P("dp", "tensor"),
            P("dp", "tensor"),
            P("dp", "tensor"),
            P("tensor", "dp"),
            P(("dp", "tensor")),
            P("dp", "tensor"),
            P("dp", "tensor"),
            P("tensor", "dp"),
            P("dp", "tensor", None, None),
        ),
        out_specs=(
            P("dp", "tensor", None, None),
            P("dp", "tensor", None, None),
            P(("dp", "tensor")),
            P(("dp", "tensor")),
            P("dp", "tensor"),
            P("dp", "tensor"),
            P("dp", "tensor"),
            P("dp", "tensor"),
            P("tensor", "dp"),
            P(("dp", "tensor")),
            P("dp", "tensor"),
            P("dp", "tensor"),
            P("tensor", "dp"),
        ),
        check_vma=False,
    )
```

```python
import functools

import jax
import jax.numpy as jnp
from jax import lax
from jax.experimental import pallas as pl
from jax.experimental.pallas import tpu as pltpu
from jax.sharding import PartitionSpec as P

HK = 128
HIGHEST = lax.Precision.HIGHEST


epsilon = 1e-06


def row_scale(values):
    return lax.rsqrt(jnp.mean(values * values, axis=-1, keepdims=True) + epsilon)


def silu_slope(values):
    sigmoid_val = jax.nn.sigmoid(values)
    return sigmoid_val * (1.0 + values * (1.0 - sigmoid_val))


def matmul_plain(left, right):
    return jnp.dot(left, right, preferred_element_type=jnp.float32)


def times_trans(left, right):
    return lax.dot_general(
        left, right, (((1,), (1,)), ((), ())), preferred_element_type=jnp.float32
    )


def trans_times(left, right):
    return lax.dot_general(
        left, right, (((0,), (0,)), ((), ())), preferred_element_type=jnp.float32
    )


def pack_kernel(per, first_ref, second_ref, right_ref, out_ref):
    col = pl.program_id(1)

    @pl.when(col < per)
    def _():
        out_ref[...] = jnp.dot(
            first_ref[...].T, right_ref[...], preferred_element_type=jnp.float32
        ).astype(out_ref.dtype)

    @pl.when(col >= per)
    def _():
        out_ref[...] = jnp.dot(
            second_ref[...].T, right_ref[...], preferred_element_type=jnp.float32
        ).astype(out_ref.dtype)


def grad_pack(first, second, right, width):
    depth, rows_out = first.shape
    cols = right.shape[1]
    blocks = cols // width
    per = blocks - 1
    tile = 512
    return pl.pallas_call(
        functools.partial(pack_kernel, per),
        grid=(rows_out // tile, blocks),
        in_specs=[
            pl.BlockSpec((depth, tile), lambda i, j: (0, i)),
            pl.BlockSpec((depth, tile), lambda i, j: (0, i)),
            pl.BlockSpec((depth, width), lambda i, j: (0, j)),
        ],
        out_specs=pl.BlockSpec((tile, width), lambda i, j: (i, j)),
        out_shape=jax.ShapeDtypeStruct((rows_out, cols), jnp.bfloat16),
        cost_estimate=pl.CostEstimate(
            flops=2 * depth * rows_out * cols,
            transcendentals=0,
            bytes_accessed=2 * (2 * depth * rows_out + depth * cols + rows_out * cols),
        ),
    )(first, second, right)


def recurrence(query, forget_raw, value, floor_vec, doc_rows):
    length = query.shape[1]
    forget = floor_vec + (1.0 - floor_vec) * jax.nn.sigmoid(forget_raw)
    log_forget = jnp.log(forget)
    keyed = 1.0 - forget
    position = jnp.arange(length)
    same_doc = doc_rows[:, :, None] == doc_rows[:, None, :]
    causal = same_doc & (position[:, None] >= position[None, :])
    starts = jnp.concatenate(
        [jnp.zeros_like(doc_rows[:, :1], dtype=bool), doc_rows[:, 1:] == doc_rows[:, :-1]], axis=1
    )
    summing = (causal & starts[:, None, :]).astype(jnp.float32)
    running = jnp.einsum("rij,rjhk->rihk", summing, log_forget, precision=HIGHEST)
    query_t = query * jnp.exp(running)
    key_t = keyed * jnp.exp(-running)
    scores = jnp.einsum("rihk,rjhk->rhij", query_t, key_t, precision=HIGHEST)
    scores = jnp.where(causal[:, None], scores, 0.0)
    return jnp.einsum("rhij,rjhv->rihv", scores, value, precision=HIGHEST)


ON_CHIP = [(0, 1), (1, 0), (2, 3), (3, 2)]
ACROSS = [(0, 2), (2, 0), (1, 3), (3, 1)]
SLOT_XOR = (0, 2, 1, 3)


def row_gather(values):
    across = lax.ppermute(values, "tensor", ACROSS)
    pair = jnp.stack([values, across])
    other = lax.ppermute(pair, "tensor", ON_CHIP)
    return jnp.concatenate([pair, other]).reshape((-1,) + values.shape[1:])


def row_sum(values):
    blocks = values.reshape((4, -1) + values.shape[1:])
    got = lax.ppermute(blocks[2:], "tensor", ON_CHIP)
    mine = blocks[0] + got[0]
    theirs = blocks[1] + got[1]
    return mine + lax.ppermute(theirs, "tensor", ACROSS)


def spread_sum(values, axis, count):
    blocks = values.reshape((count, -1) + values.shape[1:])
    got = lax.all_to_all(blocks, axis, 0, 0, tiled=False)
    return got.astype(jnp.float32).sum(axis=0)


def small_gather(vectors):
    count = 128
    spread = jnp.broadcast_to(vectors[None], (count,) + vectors.shape)
    got = lax.all_to_all(spread, ("dp", "tensor"), 0, 0, tiled=False)
    return jnp.swapaxes(got, 0, 1).reshape(vectors.shape[0], -1)


def small_sum(vectors):
    count = 128
    blocks = vectors.reshape(vectors.shape[0], count, -1)
    got = lax.all_to_all(jnp.swapaxes(blocks, 0, 1), ("dp", "tensor"), 0, 0, tiled=False)
    return got.sum(axis=0)


def shards(
    tokens,
    doc_ids,
    attn_gain,
    forget_floor,
    w_query,
    w_forget,
    w_value,
    w_outgate,
    w_output,
    mlp_gain,
    w_gate,
    w_up,
    w_down,
    cotangent,
):
    gains = small_gather(jnp.stack([attn_gain, forget_floor, mlp_gain]))
    attn_full, floor_full, mlp_full = gains[0], gains[1], gains[2]
    part_index = lax.axis_index("tensor")
    local_width = w_query.shape[1]
    local_heads = local_width // HK
    hidden_width = w_gate.shape[1]
    floor_local = lax.dynamic_slice_in_dim(
        floor_full, part_index * local_width, local_width
    ).reshape(local_heads, HK)
    model_width = attn_full.shape[0]
    slot_rows = jnp.bitwise_xor(part_index, jnp.array(SLOT_XOR, jnp.int32))
    doc_all = jnp.take(doc_ids[0], slot_rows, axis=0)
    row_count = doc_all.shape[0]
    resid_in = tokens[0].reshape(-1, model_width).astype(jnp.float32)
    cot_local = cotangent[0].reshape(-1, model_width)
    attn_pack = jnp.concatenate([w_query, w_forget, w_value, w_outgate, w_output.T], axis=1)
    mlp_pack = jnp.concatenate([w_gate, w_up, w_down.T], axis=1)
    attn_all = lax.all_gather(attn_pack, "dp", axis=0, tiled=True)
    mlp_all = lax.all_gather(mlp_pack, "dp", axis=0, tiled=True)
    wq_all = attn_all[:, 0 * local_width : 1 * local_width]
    wf_all = attn_all[:, 1 * local_width : 2 * local_width]
    wv_all = attn_all[:, 2 * local_width : 3 * local_width]
    wg_all = attn_all[:, 3 * local_width : 4 * local_width]
    wo_t = attn_all[:, 4 * local_width : 5 * local_width]
    wgate_all = mlp_all[:, 0:hidden_width]
    wup_all = mlp_all[:, hidden_width : 2 * hidden_width]
    wdown_t = mlp_all[:, 2 * hidden_width : 3 * hidden_width]
    scale_one = row_scale(resid_in)
    normed = row_gather((resid_in * scale_one * attn_full).astype(jnp.bfloat16))
    query = matmul_plain(normed, wq_all)
    forget_raw = matmul_plain(normed, wf_all)
    value = matmul_plain(normed, wv_all)
    out_gate = matmul_plain(normed, wg_all)

    def mixer(query_in, forget_in, value_in, floor_in):

        def shaped(arr):
            return arr.reshape(row_count, -1, local_heads, HK)

        mixed_rows = recurrence(
            shaped(query_in), shaped(forget_in), shaped(value_in), floor_in, doc_all
        )
        return mixed_rows.reshape(query_in.shape[0], local_width)

    mixed, pullback = jax.vjp(mixer, query, forget_raw, value, floor_local)
    gate_act = jax.nn.silu(out_gate)
    gated = (mixed * gate_act).astype(jnp.bfloat16)
    branch = row_sum(times_trans(gated, wo_t))
    resid = resid_in + branch
    scale_two = row_scale(resid)
    normed2 = row_gather((resid * scale_two * mlp_full).astype(jnp.bfloat16))
    gate_proj = matmul_plain(normed2, wgate_all)
    up_proj = matmul_plain(normed2, wup_all)
    gate_silu = jax.nn.silu(gate_proj)
    hidden = (gate_silu * up_proj).astype(jnp.bfloat16)
    ffn_out = row_sum(times_trans(hidden, wdown_t))
    layer_out = (resid + ffn_out).astype(jnp.bfloat16).reshape(tokens.shape)
    cot_full = row_gather(cot_local)
    d_hidden = matmul_plain(cot_full, wdown_t)
    d_gate = (d_hidden * up_proj * silu_slope(gate_proj)).astype(jnp.bfloat16)
    d_up = (d_hidden * gate_silu).astype(jnp.bfloat16)
    mlp_grads = grad_pack(
        normed2, cot_full, jnp.concatenate([d_gate, d_up, hidden], axis=1), hidden_width
    )
    mlp_red = spread_sum(mlp_grads, "dp", 32)
    d_normed2 = row_sum(times_trans(d_gate, wgate_all) + times_trans(d_up, wup_all))
    grad_mlp = jnp.sum(d_normed2 * resid * scale_two, axis=0)
    inner_two = jnp.mean(d_normed2 * mlp_full * resid, axis=-1, keepdims=True)
    d_resid = (
        cot_local.astype(jnp.float32)
        + d_normed2 * mlp_full * scale_two
        - resid * scale_two**3 * inner_two
    )
    d_branch = row_gather(d_resid.astype(jnp.bfloat16))
    d_gated = matmul_plain(d_branch, wo_t)
    d_mixed = d_gated * gate_act
    d_outgate = (d_gated * mixed * silu_slope(out_gate)).astype(jnp.bfloat16)
    d_query, d_forget, d_value, d_floor = pullback(d_mixed)
    d_query = d_query.astype(jnp.bfloat16)
    d_forget = d_forget.astype(jnp.bfloat16)
    d_value = d_value.astype(jnp.bfloat16)
    attn_grads = grad_pack(
        normed,
        d_branch,
        jnp.concatenate([d_query, d_forget, d_value, d_outgate, gated], axis=1),
        local_width,
    )
    attn_red = spread_sum(attn_grads, "dp", 32)
    d_normed = row_sum(
        times_trans(d_query, wq_all)
        + times_trans(d_forget, wf_all)
        + times_trans(d_value, wv_all)
        + times_trans(d_outgate, wg_all)
    )
    grad_attn = jnp.sum(d_normed * resid_in * scale_one, axis=0)
    inner_one = jnp.mean(d_normed * attn_full * resid_in, axis=-1, keepdims=True)
    grad_tokens = (
        d_resid + d_normed * attn_full * scale_one - resid_in * scale_one**3 * inner_one
    ).reshape(tokens.shape)
    floor_vector = lax.dynamic_update_slice(
        jnp.zeros((model_width,), jnp.float32), d_floor.reshape(-1), (part_index * local_width,)
    )
    reduced_small = small_sum(jnp.stack([grad_attn, floor_vector, grad_mlp]))
    return (
        layer_out,
        grad_tokens,
        reduced_small[0],
        reduced_small[1],
        attn_red[:, 0 * local_width : 1 * local_width],
        attn_red[:, 1 * local_width : 2 * local_width],
        attn_red[:, 2 * local_width : 3 * local_width],
        attn_red[:, 3 * local_width : 4 * local_width],
        attn_red[:, 4 * local_width : 5 * local_width].T,
        reduced_small[2],
        mlp_red[:, 0:hidden_width],
        mlp_red[:, hidden_width : 2 * hidden_width],
        mlp_red[:, 2 * hidden_width : 3 * hidden_width].T,
    )


def solution(mesh):
    return jax.shard_map(
        shards,
        mesh=mesh,
        in_specs=(
            P("dp", "tensor", None, None),
            P("dp", None, None),
            P(("dp", "tensor")),
            P(("dp", "tensor")),
            P("dp", "tensor"),
            P("dp", "tensor"),
            P("dp", "tensor"),
            P("dp", "tensor"),
            P("tensor", "dp"),
            P(("dp", "tensor")),
            P("dp", "tensor"),
            P("dp", "tensor"),
            P("tensor", "dp"),
            P("dp", "tensor", None, None),
        ),
        out_specs=(
            P("dp", "tensor", None, None),
            P("dp", "tensor", None, None),
            P(("dp", "tensor")),
            P(("dp", "tensor")),
            P("dp", "tensor"),
            P("dp", "tensor"),
            P("dp", "tensor"),
            P("dp", "tensor"),
            P("tensor", "dp"),
            P(("dp", "tensor")),
            P("dp", "tensor"),
            P("dp", "tensor"),
            P("tensor", "dp"),
        ),
        check_vma=False,
    )
```

```python
import functools

import jax
import jax.numpy as jnp
from jax import lax
from jax.experimental import pallas as pl
from jax.experimental.pallas import tpu as pltpu
from jax.sharding import PartitionSpec as P

HK = 128
HIGHEST = lax.Precision.HIGHEST


epsilon = 1e-06


def row_scale(values):
    return lax.rsqrt(jnp.mean(values * values, axis=-1, keepdims=True) + epsilon)


def silu_slope(values):
    sigmoid_val = jax.nn.sigmoid(values)
    return sigmoid_val * (1.0 + values * (1.0 - sigmoid_val))


def matmul_plain(left, right):
    return jnp.dot(left, right, preferred_element_type=jnp.float32)


def times_trans(left, right):
    return lax.dot_general(
        left, right, (((1,), (1,)), ((), ())), preferred_element_type=jnp.float32
    )


def trans_times(left, right):
    return lax.dot_general(
        left, right, (((0,), (0,)), ((), ())), preferred_element_type=jnp.float32
    )


def pack_kernel(per, first_ref, second_ref, right_ref, out_ref):
    col = pl.program_id(1)

    @pl.when(col < per)
    def _():
        out_ref[...] = jnp.dot(
            first_ref[...].T, right_ref[...], preferred_element_type=jnp.float32
        ).astype(out_ref.dtype)

    @pl.when(col >= per)
    def _():
        out_ref[...] = jnp.dot(
            second_ref[...].T, right_ref[...], preferred_element_type=jnp.float32
        ).astype(out_ref.dtype)


def grad_pack(first, second, right, width):
    depth, rows_out = first.shape
    cols = right.shape[1]
    blocks = cols // width
    per = blocks - 1
    tile = 512
    return pl.pallas_call(
        functools.partial(pack_kernel, per),
        grid=(rows_out // tile, blocks),
        in_specs=[
            pl.BlockSpec((depth, tile), lambda i, j: (0, i)),
            pl.BlockSpec((depth, tile), lambda i, j: (0, i)),
            pl.BlockSpec((depth, width), lambda i, j: (0, j)),
        ],
        out_specs=pl.BlockSpec((tile, width), lambda i, j: (i, j)),
        out_shape=jax.ShapeDtypeStruct((rows_out, cols), jnp.bfloat16),
        cost_estimate=pl.CostEstimate(
            flops=2 * depth * rows_out * cols,
            transcendentals=0,
            bytes_accessed=2 * (2 * depth * rows_out + depth * cols + rows_out * cols),
        ),
    )(first, second, right)


def recurrence(query, forget_raw, value, floor_vec, doc_rows):
    length = query.shape[1]
    forget = floor_vec + (1.0 - floor_vec) * jax.nn.sigmoid(forget_raw)
    log_forget = jnp.log(forget)
    keyed = 1.0 - forget
    position = jnp.arange(length)
    same_doc = doc_rows[:, :, None] == doc_rows[:, None, :]
    causal = same_doc & (position[:, None] >= position[None, :])
    starts = jnp.concatenate(
        [jnp.zeros_like(doc_rows[:, :1], dtype=bool), doc_rows[:, 1:] == doc_rows[:, :-1]], axis=1
    )
    summing = (causal & starts[:, None, :]).astype(jnp.float32)
    running = jnp.einsum("rij,rjhk->rihk", summing, log_forget, precision=HIGHEST)
    query_t = query * jnp.exp(running)
    key_t = keyed * jnp.exp(-running)
    scores = jnp.einsum("rihk,rjhk->rhij", query_t, key_t, precision=HIGHEST)
    scores = jnp.where(causal[:, None], scores, 0.0)
    return jnp.einsum("rhij,rjhv->rihv", scores, value, precision=HIGHEST)


ON_CHIP = [(0, 1), (1, 0), (2, 3), (3, 2)]
ACROSS = [(0, 2), (2, 0), (1, 3), (3, 1)]
SLOT_XOR = (0, 2, 1, 3)


def row_gather(values):
    across = lax.ppermute(values, "tensor", ACROSS)
    pair = jnp.stack([values, across])
    other = lax.ppermute(pair, "tensor", ON_CHIP)
    return jnp.concatenate([pair, other]).reshape((-1,) + values.shape[1:])


def row_sum(values):
    blocks = values.reshape((4, -1) + values.shape[1:])
    got = lax.ppermute(blocks[2:], "tensor", ON_CHIP)
    mine = blocks[0] + got[0]
    theirs = blocks[1] + got[1]
    return mine + lax.ppermute(theirs.astype(jnp.bfloat16), "tensor", ACROSS).astype(jnp.float32)


def spread_sum(values, axis, count):
    blocks = values.reshape((count, -1) + values.shape[1:])
    got = lax.all_to_all(blocks, axis, 0, 0, tiled=False)
    return got.astype(jnp.float32).sum(axis=0)


def small_gather(vectors):
    count = 128
    spread = jnp.broadcast_to(vectors[None], (count,) + vectors.shape)
    got = lax.all_to_all(spread, ("dp", "tensor"), 0, 0, tiled=False)
    return jnp.swapaxes(got, 0, 1).reshape(vectors.shape[0], -1)


def small_sum(vectors):
    count = 128
    blocks = vectors.reshape(vectors.shape[0], count, -1)
    got = lax.all_to_all(jnp.swapaxes(blocks, 0, 1), ("dp", "tensor"), 0, 0, tiled=False)
    return got.sum(axis=0)


def shards(
    tokens,
    doc_ids,
    attn_gain,
    forget_floor,
    w_query,
    w_forget,
    w_value,
    w_outgate,
    w_output,
    mlp_gain,
    w_gate,
    w_up,
    w_down,
    cotangent,
):
    gains = small_gather(jnp.stack([attn_gain, forget_floor, mlp_gain]))
    attn_full, floor_full, mlp_full = gains[0], gains[1], gains[2]
    part_index = lax.axis_index("tensor")
    local_width = w_query.shape[1]
    local_heads = local_width // HK
    hidden_width = w_gate.shape[1]
    floor_local = lax.dynamic_slice_in_dim(
        floor_full, part_index * local_width, local_width
    ).reshape(local_heads, HK)
    model_width = attn_full.shape[0]
    slot_rows = jnp.bitwise_xor(part_index, jnp.array(SLOT_XOR, jnp.int32))
    doc_all = jnp.take(doc_ids[0], slot_rows, axis=0)
    row_count = doc_all.shape[0]
    resid_in = tokens[0].reshape(-1, model_width).astype(jnp.float32)
    cot_local = cotangent[0].reshape(-1, model_width)
    attn_pack = jnp.concatenate([w_query, w_forget, w_value, w_outgate, w_output.T], axis=1)
    mlp_pack = jnp.concatenate([w_gate, w_up, w_down.T], axis=1)
    attn_all = lax.all_gather(attn_pack, "dp", axis=0, tiled=True)
    mlp_all = lax.all_gather(mlp_pack, "dp", axis=0, tiled=True)
    wq_all = attn_all[:, 0 * local_width : 1 * local_width]
    wf_all = attn_all[:, 1 * local_width : 2 * local_width]
    wv_all = attn_all[:, 2 * local_width : 3 * local_width]
    wg_all = attn_all[:, 3 * local_width : 4 * local_width]
    wo_t = attn_all[:, 4 * local_width : 5 * local_width]
    wgate_all = mlp_all[:, 0:hidden_width]
    wup_all = mlp_all[:, hidden_width : 2 * hidden_width]
    wdown_t = mlp_all[:, 2 * hidden_width : 3 * hidden_width]
    scale_one = row_scale(resid_in)
    normed = row_gather((resid_in * scale_one * attn_full).astype(jnp.bfloat16))
    query = matmul_plain(normed, wq_all)
    forget_raw = matmul_plain(normed, wf_all)
    value = matmul_plain(normed, wv_all)
    out_gate = matmul_plain(normed, wg_all)

    def mixer(query_in, forget_in, value_in, floor_in):

        def shaped(arr):
            return arr.reshape(row_count, -1, local_heads, HK)

        mixed_rows = recurrence(
            shaped(query_in), shaped(forget_in), shaped(value_in), floor_in, doc_all
        )
        return mixed_rows.reshape(query_in.shape[0], local_width)

    mixed, pullback = jax.vjp(mixer, query, forget_raw, value, floor_local)
    gate_act = jax.nn.silu(out_gate)
    gated = (mixed * gate_act).astype(jnp.bfloat16)
    branch = row_sum(times_trans(gated, wo_t))
    resid = resid_in + branch
    scale_two = row_scale(resid)
    normed2 = row_gather((resid * scale_two * mlp_full).astype(jnp.bfloat16))
    gate_proj = matmul_plain(normed2, wgate_all)
    up_proj = matmul_plain(normed2, wup_all)
    gate_silu = jax.nn.silu(gate_proj)
    hidden = (gate_silu * up_proj).astype(jnp.bfloat16)
    ffn_out = row_sum(times_trans(hidden, wdown_t))
    layer_out = (resid + ffn_out).astype(jnp.bfloat16).reshape(tokens.shape)
    cot_full = row_gather(cot_local)
    d_hidden = matmul_plain(cot_full, wdown_t)
    d_gate = (d_hidden * up_proj * silu_slope(gate_proj)).astype(jnp.bfloat16)
    d_up = (d_hidden * gate_silu).astype(jnp.bfloat16)
    mlp_grads = grad_pack(
        normed2, cot_full, jnp.concatenate([d_gate, d_up, hidden], axis=1), hidden_width
    )
    mlp_red = lax.psum_scatter(mlp_grads, "dp", scatter_dimension=0, tiled=True).astype(jnp.float32)
    d_normed2 = row_sum(times_trans(d_gate, wgate_all) + times_trans(d_up, wup_all))
    grad_mlp = jnp.sum(d_normed2 * resid * scale_two, axis=0)
    inner_two = jnp.mean(d_normed2 * mlp_full * resid, axis=-1, keepdims=True)
    d_resid = (
        cot_local.astype(jnp.float32)
        + d_normed2 * mlp_full * scale_two
        - resid * scale_two**3 * inner_two
    )
    d_branch = row_gather(d_resid.astype(jnp.bfloat16))
    d_gated = matmul_plain(d_branch, wo_t)
    d_mixed = d_gated * gate_act
    d_outgate = (d_gated * mixed * silu_slope(out_gate)).astype(jnp.bfloat16)
    d_query, d_forget, d_value, d_floor = pullback(d_mixed)
    d_query = d_query.astype(jnp.bfloat16)
    d_forget = d_forget.astype(jnp.bfloat16)
    d_value = d_value.astype(jnp.bfloat16)
    attn_grads = grad_pack(
        normed,
        d_branch,
        jnp.concatenate([d_query, d_forget, d_value, d_outgate, gated], axis=1),
        local_width,
    )
    attn_red = spread_sum(attn_grads, "dp", 32)
    d_normed = row_sum(
        times_trans(d_query, wq_all)
        + times_trans(d_forget, wf_all)
        + times_trans(d_value, wv_all)
        + times_trans(d_outgate, wg_all)
    )
    grad_attn = jnp.sum(d_normed * resid_in * scale_one, axis=0)
    inner_one = jnp.mean(d_normed * attn_full * resid_in, axis=-1, keepdims=True)
    grad_tokens = (
        d_resid + d_normed * attn_full * scale_one - resid_in * scale_one**3 * inner_one
    ).reshape(tokens.shape)
    floor_vector = lax.dynamic_update_slice(
        jnp.zeros((model_width,), jnp.float32), d_floor.reshape(-1), (part_index * local_width,)
    )
    reduced_small = small_sum(jnp.stack([grad_attn, floor_vector, grad_mlp]))
    return (
        layer_out,
        grad_tokens,
        reduced_small[0],
        reduced_small[1],
        attn_red[:, 0 * local_width : 1 * local_width],
        attn_red[:, 1 * local_width : 2 * local_width],
        attn_red[:, 2 * local_width : 3 * local_width],
        attn_red[:, 3 * local_width : 4 * local_width],
        attn_red[:, 4 * local_width : 5 * local_width].T,
        reduced_small[2],
        mlp_red[:, 0:hidden_width],
        mlp_red[:, hidden_width : 2 * hidden_width],
        mlp_red[:, 2 * hidden_width : 3 * hidden_width].T,
    )


def solution(mesh):
    return jax.shard_map(
        shards,
        mesh=mesh,
        in_specs=(
            P("dp", "tensor", None, None),
            P("dp", None, None),
            P(("dp", "tensor")),
            P(("dp", "tensor")),
            P("dp", "tensor"),
            P("dp", "tensor"),
            P("dp", "tensor"),
            P("dp", "tensor"),
            P("tensor", "dp"),
            P(("dp", "tensor")),
            P("dp", "tensor"),
            P("dp", "tensor"),
            P("tensor", "dp"),
            P("dp", "tensor", None, None),
        ),
        out_specs=(
            P("dp", "tensor", None, None),
            P("dp", "tensor", None, None),
            P(("dp", "tensor")),
            P(("dp", "tensor")),
            P("dp", "tensor"),
            P("dp", "tensor"),
            P("dp", "tensor"),
            P("dp", "tensor"),
            P("tensor", "dp"),
            P(("dp", "tensor")),
            P("dp", "tensor"),
            P("dp", "tensor"),
            P("tensor", "dp"),
        ),
        check_vma=False,
    )
```

```python
import functools

import jax
import jax.numpy as jnp
from jax import lax
from jax.experimental import pallas as pl
from jax.experimental.pallas import tpu as pltpu
from jax.sharding import PartitionSpec as P

HK = 128
HIGHEST = lax.Precision.HIGHEST


epsilon = 1e-06


def row_scale(values):
    return lax.rsqrt(jnp.mean(values * values, axis=-1, keepdims=True) + epsilon)


def silu_slope(values):
    sigmoid_val = jax.nn.sigmoid(values)
    return sigmoid_val * (1.0 + values * (1.0 - sigmoid_val))


def matmul_plain(left, right):
    return jnp.dot(left, right, preferred_element_type=jnp.float32)


def times_trans(left, right):
    return lax.dot_general(
        left, right, (((1,), (1,)), ((), ())), preferred_element_type=jnp.float32
    )


def trans_times(left, right):
    return lax.dot_general(
        left, right, (((0,), (0,)), ((), ())), preferred_element_type=jnp.float32
    )


def pack_kernel(per, first_ref, second_ref, right_ref, out_ref):
    col = pl.program_id(1)

    @pl.when(col < per)
    def _():
        out_ref[...] = jnp.dot(
            first_ref[...].T, right_ref[...], preferred_element_type=jnp.float32
        ).astype(out_ref.dtype)

    @pl.when(col >= per)
    def _():
        out_ref[...] = jnp.dot(
            second_ref[...].T, right_ref[...], preferred_element_type=jnp.float32
        ).astype(out_ref.dtype)


def grad_pack(first, second, right, width):
    depth, rows_out = first.shape
    cols = right.shape[1]
    blocks = cols // width
    per = blocks - 1
    tile = 512
    return pl.pallas_call(
        functools.partial(pack_kernel, per),
        grid=(rows_out // tile, blocks),
        in_specs=[
            pl.BlockSpec((depth, tile), lambda i, j: (0, i)),
            pl.BlockSpec((depth, tile), lambda i, j: (0, i)),
            pl.BlockSpec((depth, width), lambda i, j: (0, j)),
        ],
        out_specs=pl.BlockSpec((tile, width), lambda i, j: (i, j)),
        out_shape=jax.ShapeDtypeStruct((rows_out, cols), jnp.bfloat16),
        cost_estimate=pl.CostEstimate(
            flops=2 * depth * rows_out * cols,
            transcendentals=0,
            bytes_accessed=2 * (2 * depth * rows_out + depth * cols + rows_out * cols),
        ),
    )(first, second, right)


def recurrence(query, forget_raw, value, floor_vec, doc_rows):
    length = query.shape[1]
    forget = floor_vec + (1.0 - floor_vec) * jax.nn.sigmoid(forget_raw)
    log_forget = jnp.log(forget)
    keyed = 1.0 - forget
    position = jnp.arange(length)
    same_doc = doc_rows[:, :, None] == doc_rows[:, None, :]
    causal = same_doc & (position[:, None] >= position[None, :])
    starts = jnp.concatenate(
        [jnp.zeros_like(doc_rows[:, :1], dtype=bool), doc_rows[:, 1:] == doc_rows[:, :-1]], axis=1
    )
    summing = (causal & starts[:, None, :]).astype(jnp.float32)
    running = jnp.einsum("rij,rjhk->rihk", summing, log_forget, precision=HIGHEST)
    query_t = query * jnp.exp(running)
    key_t = keyed * jnp.exp(-running)
    scores = jnp.einsum("rihk,rjhk->rhij", query_t, key_t, precision=HIGHEST)
    scores = jnp.where(causal[:, None], scores, 0.0)
    return jnp.einsum("rhij,rjhv->rihv", scores, value, precision=HIGHEST)


ON_CHIP = [(0, 1), (1, 0), (2, 3), (3, 2)]
ACROSS = [(0, 2), (2, 0), (1, 3), (3, 1)]
SLOT_XOR = (0, 2, 1, 3)


def row_gather(values):
    across = lax.ppermute(values, "tensor", ACROSS)
    pair = jnp.stack([values, across])
    other = lax.ppermute(pair, "tensor", ON_CHIP)
    return jnp.concatenate([pair, other]).reshape((-1,) + values.shape[1:])


def row_sum(values):
    blocks = values.reshape((4, -1) + values.shape[1:])
    got = lax.ppermute(blocks[2:], "tensor", ON_CHIP)
    mine = blocks[0] + got[0]
    theirs = blocks[1] + got[1]
    return mine + lax.ppermute(theirs.astype(jnp.bfloat16), "tensor", ACROSS).astype(jnp.float32)


def spread_sum(values, axis, count):
    blocks = values.reshape((count, -1) + values.shape[1:])
    got = lax.all_to_all(blocks, axis, 0, 0, tiled=False)
    return got.astype(jnp.float32).sum(axis=0)


def small_gather(vectors):
    count = 128
    spread = jnp.broadcast_to(vectors[None], (count,) + vectors.shape)
    got = lax.all_to_all(spread, ("dp", "tensor"), 0, 0, tiled=False)
    return jnp.swapaxes(got, 0, 1).reshape(vectors.shape[0], -1)


def small_sum(vectors):
    count = 128
    blocks = vectors.reshape(vectors.shape[0], count, -1)
    got = lax.all_to_all(jnp.swapaxes(blocks, 0, 1), ("dp", "tensor"), 0, 0, tiled=False)
    return got.sum(axis=0)


def shards(
    tokens,
    doc_ids,
    attn_gain,
    forget_floor,
    w_query,
    w_forget,
    w_value,
    w_outgate,
    w_output,
    mlp_gain,
    w_gate,
    w_up,
    w_down,
    cotangent,
):
    gains = small_gather(jnp.stack([attn_gain, forget_floor, mlp_gain]))
    attn_full, floor_full, mlp_full = gains[0], gains[1], gains[2]
    part_index = lax.axis_index("tensor")
    local_width = w_query.shape[1]
    local_heads = local_width // HK
    hidden_width = w_gate.shape[1]
    floor_local = lax.dynamic_slice_in_dim(
        floor_full, part_index * local_width, local_width
    ).reshape(local_heads, HK)
    model_width = attn_full.shape[0]
    slot_rows = jnp.bitwise_xor(part_index, jnp.array(SLOT_XOR, jnp.int32))
    doc_all = jnp.take(doc_ids[0], slot_rows, axis=0)
    row_count = doc_all.shape[0]
    resid_in = tokens[0].reshape(-1, model_width).astype(jnp.float32)
    cot_local = cotangent[0].reshape(-1, model_width)
    attn_pack = jnp.concatenate([w_query, w_forget, w_value, w_outgate, w_output.T], axis=1)
    mlp_pack = jnp.concatenate([w_gate, w_up, w_down.T], axis=1)
    attn_all = lax.all_gather(attn_pack, "dp", axis=0, tiled=True)
    mlp_all = lax.all_gather(mlp_pack, "dp", axis=0, tiled=True)
    wq_all = attn_all[:, 0 * local_width : 1 * local_width]
    wf_all = attn_all[:, 1 * local_width : 2 * local_width]
    wv_all = attn_all[:, 2 * local_width : 3 * local_width]
    wg_all = attn_all[:, 3 * local_width : 4 * local_width]
    wo_t = attn_all[:, 4 * local_width : 5 * local_width]
    wgate_all = mlp_all[:, 0:hidden_width]
    wup_all = mlp_all[:, hidden_width : 2 * hidden_width]
    wdown_t = mlp_all[:, 2 * hidden_width : 3 * hidden_width]
    scale_one = row_scale(resid_in)
    normed = row_gather((resid_in * scale_one * attn_full).astype(jnp.bfloat16))
    query = matmul_plain(normed, wq_all)
    forget_raw = matmul_plain(normed, wf_all)
    value = matmul_plain(normed, wv_all)
    out_gate = matmul_plain(normed, wg_all)

    def mixer(query_in, forget_in, value_in, floor_in):

        def shaped(arr):
            return arr.reshape(row_count, -1, local_heads, HK)

        mixed_rows = recurrence(
            shaped(query_in), shaped(forget_in), shaped(value_in), floor_in, doc_all
        )
        return mixed_rows.reshape(query_in.shape[0], local_width)

    mixed, pullback = jax.vjp(mixer, query, forget_raw, value, floor_local)
    gate_act = jax.nn.silu(out_gate)
    gated = (mixed * gate_act).astype(jnp.bfloat16)
    branch = row_sum(times_trans(gated, wo_t))
    resid = resid_in + branch
    scale_two = row_scale(resid)
    normed2 = row_gather((resid * scale_two * mlp_full).astype(jnp.bfloat16))
    gate_proj = matmul_plain(normed2, wgate_all)
    up_proj = matmul_plain(normed2, wup_all)
    gate_silu = jax.nn.silu(gate_proj)
    hidden = (gate_silu * up_proj).astype(jnp.bfloat16)
    ffn_out = row_sum(times_trans(hidden, wdown_t))
    layer_out = (resid + ffn_out).astype(jnp.bfloat16).reshape(tokens.shape)
    cot_full = row_gather(cot_local)
    d_hidden = matmul_plain(cot_full, wdown_t)
    d_gate = (d_hidden * up_proj * silu_slope(gate_proj)).astype(jnp.bfloat16)
    d_up = (d_hidden * gate_silu).astype(jnp.bfloat16)
    mlp_grads = grad_pack(
        normed2, cot_full, jnp.concatenate([d_gate, d_up, hidden], axis=1), hidden_width
    )
    mlp_red = lax.psum_scatter(mlp_grads, "dp", scatter_dimension=0, tiled=True).astype(jnp.float32)
    d_normed2 = row_sum(times_trans(d_gate, wgate_all) + times_trans(d_up, wup_all))
    grad_mlp = jnp.sum(d_normed2 * resid * scale_two, axis=0)
    inner_two = jnp.mean(d_normed2 * mlp_full * resid, axis=-1, keepdims=True)
    d_resid = (
        cot_local.astype(jnp.float32)
        + d_normed2 * mlp_full * scale_two
        - resid * scale_two**3 * inner_two
    )
    d_branch = row_gather(d_resid.astype(jnp.bfloat16))
    d_gated = matmul_plain(d_branch, wo_t)
    d_mixed = d_gated * gate_act
    d_outgate = (d_gated * mixed * silu_slope(out_gate)).astype(jnp.bfloat16)
    d_query, d_forget, d_value, d_floor = pullback(d_mixed)
    d_query = d_query.astype(jnp.bfloat16)
    d_forget = d_forget.astype(jnp.bfloat16)
    d_value = d_value.astype(jnp.bfloat16)
    attn_grads = grad_pack(
        normed,
        d_branch,
        jnp.concatenate([d_query, d_forget, d_value, d_outgate, gated], axis=1),
        local_width,
    )
    attn_grads, mlp_red = lax.optimization_barrier((attn_grads, mlp_red))
    attn_red = spread_sum(attn_grads, "dp", 32)
    d_normed = row_sum(
        times_trans(d_query, wq_all)
        + times_trans(d_forget, wf_all)
        + times_trans(d_value, wv_all)
        + times_trans(d_outgate, wg_all)
    )
    grad_attn = jnp.sum(d_normed * resid_in * scale_one, axis=0)
    inner_one = jnp.mean(d_normed * attn_full * resid_in, axis=-1, keepdims=True)
    grad_tokens = (
        d_resid + d_normed * attn_full * scale_one - resid_in * scale_one**3 * inner_one
    ).reshape(tokens.shape)
    floor_vector = lax.dynamic_update_slice(
        jnp.zeros((model_width,), jnp.float32), d_floor.reshape(-1), (part_index * local_width,)
    )
    reduced_small = small_sum(jnp.stack([grad_attn, floor_vector, grad_mlp]))
    return (
        layer_out,
        grad_tokens,
        reduced_small[0],
        reduced_small[1],
        attn_red[:, 0 * local_width : 1 * local_width],
        attn_red[:, 1 * local_width : 2 * local_width],
        attn_red[:, 2 * local_width : 3 * local_width],
        attn_red[:, 3 * local_width : 4 * local_width],
        attn_red[:, 4 * local_width : 5 * local_width].T,
        reduced_small[2],
        mlp_red[:, 0:hidden_width],
        mlp_red[:, hidden_width : 2 * hidden_width],
        mlp_red[:, 2 * hidden_width : 3 * hidden_width].T,
    )


def solution(mesh):
    return jax.shard_map(
        shards,
        mesh=mesh,
        in_specs=(
            P("dp", "tensor", None, None),
            P("dp", None, None),
            P(("dp", "tensor")),
            P(("dp", "tensor")),
            P("dp", "tensor"),
            P("dp", "tensor"),
            P("dp", "tensor"),
            P("dp", "tensor"),
            P("tensor", "dp"),
            P(("dp", "tensor")),
            P("dp", "tensor"),
            P("dp", "tensor"),
            P("tensor", "dp"),
            P("dp", "tensor", None, None),
        ),
        out_specs=(
            P("dp", "tensor", None, None),
            P("dp", "tensor", None, None),
            P(("dp", "tensor")),
            P(("dp", "tensor")),
            P("dp", "tensor"),
            P("dp", "tensor"),
            P("dp", "tensor"),
            P("dp", "tensor"),
            P("tensor", "dp"),
            P(("dp", "tensor")),
            P("dp", "tensor"),
            P("dp", "tensor"),
            P("tensor", "dp"),
        ),
        check_vma=False,
    )
```

```python
import functools

import jax
import jax.numpy as jnp
from jax import lax
from jax.experimental import pallas as pl
from jax.experimental.pallas import tpu as pltpu
from jax.sharding import PartitionSpec as P

HK = 128
HIGHEST = lax.Precision.HIGHEST


epsilon = 1e-06


def row_scale(values):
    return lax.rsqrt(jnp.mean(values * values, axis=-1, keepdims=True) + epsilon)


def silu_slope(values):
    sigmoid_val = jax.nn.sigmoid(values)
    return sigmoid_val * (1.0 + values * (1.0 - sigmoid_val))


def matmul_plain(left, right):
    return jnp.dot(left, right, preferred_element_type=jnp.float32)


def times_trans(left, right):
    return lax.dot_general(
        left, right, (((1,), (1,)), ((), ())), preferred_element_type=jnp.float32
    )


def trans_times(left, right):
    return lax.dot_general(
        left, right, (((0,), (0,)), ((), ())), preferred_element_type=jnp.float32
    )


def pack_kernel(per, first_ref, second_ref, right_ref, out_ref):
    col = pl.program_id(1)

    @pl.when(col < per)
    def _():
        out_ref[...] = jnp.dot(
            first_ref[...].T, right_ref[...], preferred_element_type=jnp.float32
        ).astype(out_ref.dtype)

    @pl.when(col >= per)
    def _():
        out_ref[...] = jnp.dot(
            second_ref[...].T, right_ref[...], preferred_element_type=jnp.float32
        ).astype(out_ref.dtype)


def grad_pack(first, second, right, width):
    depth, rows_out = first.shape
    cols = right.shape[1]
    blocks = cols // width
    per = blocks - 1
    tile = rows_out
    return pl.pallas_call(
        functools.partial(pack_kernel, per),
        grid=(rows_out // tile, blocks),
        in_specs=[
            pl.BlockSpec((depth, tile), lambda i, j: (0, i)),
            pl.BlockSpec((depth, tile), lambda i, j: (0, i)),
            pl.BlockSpec((depth, width), lambda i, j: (0, j)),
        ],
        out_specs=pl.BlockSpec((tile, width), lambda i, j: (i, j)),
        out_shape=jax.ShapeDtypeStruct((rows_out, cols), jnp.bfloat16),
        cost_estimate=pl.CostEstimate(
            flops=2 * depth * rows_out * cols,
            transcendentals=0,
            bytes_accessed=2 * (2 * depth * rows_out + depth * cols + rows_out * cols),
        ),
    )(first, second, right)


def recurrence(query, forget_raw, value, floor_vec, doc_rows):
    length = query.shape[1]
    forget = floor_vec + (1.0 - floor_vec) * jax.nn.sigmoid(forget_raw)
    log_forget = jnp.log(forget)
    keyed = 1.0 - forget
    position = jnp.arange(length)
    same_doc = doc_rows[:, :, None] == doc_rows[:, None, :]
    causal = same_doc & (position[:, None] >= position[None, :])
    starts = jnp.concatenate(
        [jnp.zeros_like(doc_rows[:, :1], dtype=bool), doc_rows[:, 1:] == doc_rows[:, :-1]], axis=1
    )
    summing = (causal & starts[:, None, :]).astype(jnp.float32)
    running = jnp.einsum("rij,rjhk->rihk", summing, log_forget, precision=HIGHEST)
    query_t = query * jnp.exp(running)
    key_t = keyed * jnp.exp(-running)
    scores = jnp.einsum("rihk,rjhk->rhij", query_t, key_t, precision=HIGHEST)
    scores = jnp.where(causal[:, None], scores, 0.0)
    return jnp.einsum("rhij,rjhv->rihv", scores, value, precision=HIGHEST)


ON_CHIP = [(0, 1), (1, 0), (2, 3), (3, 2)]
ACROSS = [(0, 2), (2, 0), (1, 3), (3, 1)]
SLOT_XOR = (0, 2, 1, 3)


def row_gather(values):
    across = lax.ppermute(values, "tensor", ACROSS)
    pair = jnp.stack([values, across])
    other = lax.ppermute(pair, "tensor", ON_CHIP)
    return jnp.concatenate([pair, other]).reshape((-1,) + values.shape[1:])


def row_sum(values):
    blocks = values.reshape((4, -1) + values.shape[1:])
    got = lax.ppermute(blocks[2:], "tensor", ON_CHIP)
    mine = blocks[0] + got[0]
    theirs = blocks[1] + got[1]
    return mine + lax.ppermute(theirs.astype(jnp.bfloat16), "tensor", ACROSS).astype(jnp.float32)


def spread_sum(values, axis, count):
    blocks = values.reshape((count, -1) + values.shape[1:])
    got = lax.all_to_all(blocks, axis, 0, 0, tiled=False)
    return got.astype(jnp.float32).sum(axis=0)


def small_gather(vectors):
    count = 128
    spread = jnp.broadcast_to(vectors[None], (count,) + vectors.shape)
    got = lax.all_to_all(spread, ("dp", "tensor"), 0, 0, tiled=False)
    return jnp.swapaxes(got, 0, 1).reshape(vectors.shape[0], -1)


def small_sum(vectors):
    count = 128
    blocks = vectors.reshape(vectors.shape[0], count, -1)
    got = lax.all_to_all(jnp.swapaxes(blocks, 0, 1), ("dp", "tensor"), 0, 0, tiled=False)
    return got.sum(axis=0)


def shards(
    tokens,
    doc_ids,
    attn_gain,
    forget_floor,
    w_query,
    w_forget,
    w_value,
    w_outgate,
    w_output,
    mlp_gain,
    w_gate,
    w_up,
    w_down,
    cotangent,
):
    gains = small_gather(jnp.stack([attn_gain, forget_floor, mlp_gain]))
    attn_full, floor_full, mlp_full = gains[0], gains[1], gains[2]
    part_index = lax.axis_index("tensor")
    local_width = w_query.shape[1]
    local_heads = local_width // HK
    hidden_width = w_gate.shape[1]
    floor_local = lax.dynamic_slice_in_dim(
        floor_full, part_index * local_width, local_width
    ).reshape(local_heads, HK)
    model_width = attn_full.shape[0]
    slot_rows = jnp.bitwise_xor(part_index, jnp.array(SLOT_XOR, jnp.int32))
    doc_all = jnp.take(doc_ids[0], slot_rows, axis=0)
    row_count = doc_all.shape[0]
    resid_in = tokens[0].reshape(-1, model_width).astype(jnp.float32)
    cot_local = cotangent[0].reshape(-1, model_width)
    attn_pack = jnp.concatenate([w_query, w_forget, w_value, w_outgate, w_output.T], axis=1)
    mlp_pack = jnp.concatenate([w_gate, w_up, w_down.T], axis=1)
    attn_all = lax.all_gather(attn_pack, "dp", axis=0, tiled=True)
    mlp_all = lax.all_gather(mlp_pack, "dp", axis=0, tiled=True)
    wq_all = attn_all[:, 0 * local_width : 1 * local_width]
    wf_all = attn_all[:, 1 * local_width : 2 * local_width]
    wv_all = attn_all[:, 2 * local_width : 3 * local_width]
    wg_all = attn_all[:, 3 * local_width : 4 * local_width]
    wo_t = attn_all[:, 4 * local_width : 5 * local_width]
    wgate_all = mlp_all[:, 0:hidden_width]
    wup_all = mlp_all[:, hidden_width : 2 * hidden_width]
    wdown_t = mlp_all[:, 2 * hidden_width : 3 * hidden_width]
    scale_one = row_scale(resid_in)
    normed = row_gather((resid_in * scale_one * attn_full).astype(jnp.bfloat16))
    query = matmul_plain(normed, wq_all)
    forget_raw = matmul_plain(normed, wf_all)
    value = matmul_plain(normed, wv_all)
    out_gate = matmul_plain(normed, wg_all)

    def mixer(query_in, forget_in, value_in, floor_in):

        def shaped(arr):
            return arr.reshape(row_count, -1, local_heads, HK)

        mixed_rows = recurrence(
            shaped(query_in), shaped(forget_in), shaped(value_in), floor_in, doc_all
        )
        return mixed_rows.reshape(query_in.shape[0], local_width)

    mixed, pullback = jax.vjp(mixer, query, forget_raw, value, floor_local)
    gate_act = jax.nn.silu(out_gate)
    gated = (mixed * gate_act).astype(jnp.bfloat16)
    branch = row_sum(times_trans(gated, wo_t))
    resid = resid_in + branch
    scale_two = row_scale(resid)
    normed2 = row_gather((resid * scale_two * mlp_full).astype(jnp.bfloat16))
    gate_proj = matmul_plain(normed2, wgate_all)
    up_proj = matmul_plain(normed2, wup_all)
    gate_silu = jax.nn.silu(gate_proj)
    hidden = (gate_silu * up_proj).astype(jnp.bfloat16)
    ffn_out = row_sum(times_trans(hidden, wdown_t))
    layer_out = (resid + ffn_out).astype(jnp.bfloat16).reshape(tokens.shape)
    cot_full = row_gather(cot_local)
    d_hidden = matmul_plain(cot_full, wdown_t)
    d_gate = (d_hidden * up_proj * silu_slope(gate_proj)).astype(jnp.bfloat16)
    d_up = (d_hidden * gate_silu).astype(jnp.bfloat16)
    mlp_grads = grad_pack(
        normed2, cot_full, jnp.concatenate([d_gate, d_up, hidden], axis=1), hidden_width
    )
    mlp_red = lax.psum_scatter(mlp_grads, "dp", scatter_dimension=0, tiled=True).astype(jnp.float32)
    d_normed2 = row_sum(times_trans(d_gate, wgate_all) + times_trans(d_up, wup_all))
    grad_mlp = jnp.sum(d_normed2 * resid * scale_two, axis=0)
    inner_two = jnp.mean(d_normed2 * mlp_full * resid, axis=-1, keepdims=True)
    d_resid = (
        cot_local.astype(jnp.float32)
        + d_normed2 * mlp_full * scale_two
        - resid * scale_two**3 * inner_two
    )
    d_branch = row_gather(d_resid.astype(jnp.bfloat16))
    d_gated = matmul_plain(d_branch, wo_t)
    d_mixed = d_gated * gate_act
    d_outgate = (d_gated * mixed * silu_slope(out_gate)).astype(jnp.bfloat16)
    d_query, d_forget, d_value, d_floor = pullback(d_mixed)
    d_query = d_query.astype(jnp.bfloat16)
    d_forget = d_forget.astype(jnp.bfloat16)
    d_value = d_value.astype(jnp.bfloat16)
    attn_grads = grad_pack(
        normed,
        d_branch,
        jnp.concatenate([d_query, d_forget, d_value, d_outgate, gated], axis=1),
        local_width,
    )
    attn_red = spread_sum(attn_grads, "dp", 32)
    d_normed = row_sum(
        times_trans(d_query, wq_all)
        + times_trans(d_forget, wf_all)
        + times_trans(d_value, wv_all)
        + times_trans(d_outgate, wg_all)
    )
    grad_attn = jnp.sum(d_normed * resid_in * scale_one, axis=0)
    inner_one = jnp.mean(d_normed * attn_full * resid_in, axis=-1, keepdims=True)
    grad_tokens = (
        d_resid + d_normed * attn_full * scale_one - resid_in * scale_one**3 * inner_one
    ).reshape(tokens.shape)
    floor_vector = lax.dynamic_update_slice(
        jnp.zeros((model_width,), jnp.float32), d_floor.reshape(-1), (part_index * local_width,)
    )
    reduced_small = small_sum(jnp.stack([grad_attn, floor_vector, grad_mlp]))
    return (
        layer_out,
        grad_tokens,
        reduced_small[0],
        reduced_small[1],
        attn_red[:, 0 * local_width : 1 * local_width],
        attn_red[:, 1 * local_width : 2 * local_width],
        attn_red[:, 2 * local_width : 3 * local_width],
        attn_red[:, 3 * local_width : 4 * local_width],
        attn_red[:, 4 * local_width : 5 * local_width].T,
        reduced_small[2],
        mlp_red[:, 0:hidden_width],
        mlp_red[:, hidden_width : 2 * hidden_width],
        mlp_red[:, 2 * hidden_width : 3 * hidden_width].T,
    )


def solution(mesh):
    return jax.shard_map(
        shards,
        mesh=mesh,
        in_specs=(
            P("dp", "tensor", None, None),
            P("dp", None, None),
            P(("dp", "tensor")),
            P(("dp", "tensor")),
            P("dp", "tensor"),
            P("dp", "tensor"),
            P("dp", "tensor"),
            P("dp", "tensor"),
            P("tensor", "dp"),
            P(("dp", "tensor")),
            P("dp", "tensor"),
            P("dp", "tensor"),
            P("tensor", "dp"),
            P("dp", "tensor", None, None),
        ),
        out_specs=(
            P("dp", "tensor", None, None),
            P("dp", "tensor", None, None),
            P(("dp", "tensor")),
            P(("dp", "tensor")),
            P("dp", "tensor"),
            P("dp", "tensor"),
            P("dp", "tensor"),
            P("dp", "tensor"),
            P("tensor", "dp"),
            P(("dp", "tensor")),
            P("dp", "tensor"),
            P("dp", "tensor"),
            P("tensor", "dp"),
        ),
        check_vma=False,
    )
```

```python
import functools

import jax
import jax.numpy as jnp
from jax import lax
from jax.experimental import pallas as pl
from jax.experimental.pallas import tpu as pltpu
from jax.sharding import PartitionSpec as P

HK = 128
HIGHEST = lax.Precision.HIGHEST


epsilon = 1e-06


def row_scale(values):
    return lax.rsqrt(jnp.mean(values * values, axis=-1, keepdims=True) + epsilon)


def silu_slope(values):
    sigmoid_val = jax.nn.sigmoid(values)
    return sigmoid_val * (1.0 + values * (1.0 - sigmoid_val))


def matmul_plain(left, right):
    return jnp.dot(left, right, preferred_element_type=jnp.float32)


def times_trans(left, right):
    return lax.dot_general(
        left, right, (((1,), (1,)), ((), ())), preferred_element_type=jnp.float32
    )


def trans_times(left, right):
    return lax.dot_general(
        left, right, (((0,), (0,)), ((), ())), preferred_element_type=jnp.float32
    )


def pack_kernel(per, first_ref, second_ref, right_ref, out_ref):
    col = pl.program_id(1)

    @pl.when(col < per)
    def _():
        out_ref[...] = jnp.dot(
            first_ref[...].T, right_ref[...], preferred_element_type=jnp.float32
        ).astype(out_ref.dtype)

    @pl.when(col >= per)
    def _():
        out_ref[...] = jnp.dot(
            second_ref[...].T, right_ref[...], preferred_element_type=jnp.float32
        ).astype(out_ref.dtype)


def grad_pack(first, second, right, width):
    depth, rows_out = first.shape
    cols = right.shape[1]
    blocks = cols // width
    per = blocks - 1
    tile = rows_out
    return pl.pallas_call(
        functools.partial(pack_kernel, per),
        grid=(rows_out // tile, blocks),
        in_specs=[
            pl.BlockSpec((depth, tile), lambda i, j: (0, i)),
            pl.BlockSpec((depth, tile), lambda i, j: (0, i)),
            pl.BlockSpec((depth, width), lambda i, j: (0, j)),
        ],
        out_specs=pl.BlockSpec((tile, width), lambda i, j: (i, j)),
        out_shape=jax.ShapeDtypeStruct((rows_out, cols), jnp.bfloat16),
        cost_estimate=pl.CostEstimate(
            flops=2 * depth * rows_out * cols,
            transcendentals=0,
            bytes_accessed=2 * (2 * depth * rows_out + depth * cols + rows_out * cols),
        ),
    )(first, second, right)


def recurrence(query, forget_raw, value, floor_vec, doc_rows):
    length = query.shape[1]
    forget = floor_vec + (1.0 - floor_vec) * jax.nn.sigmoid(forget_raw)
    log_forget = jnp.log(forget)
    keyed = 1.0 - forget
    position = jnp.arange(length)
    same_doc = doc_rows[:, :, None] == doc_rows[:, None, :]
    causal = same_doc & (position[:, None] >= position[None, :])
    starts = jnp.concatenate(
        [jnp.zeros_like(doc_rows[:, :1], dtype=bool), doc_rows[:, 1:] == doc_rows[:, :-1]], axis=1
    )
    summing = (causal & starts[:, None, :]).astype(jnp.float32)
    running = jnp.einsum("rij,rjhk->rihk", summing, log_forget, precision=HIGHEST)
    query_t = query * jnp.exp(running)
    key_t = keyed * jnp.exp(-running)
    scores = jnp.einsum("rihk,rjhk->rhij", query_t, key_t, precision=HIGHEST)
    scores = jnp.where(causal[:, None], scores, 0.0)
    return jnp.einsum("rhij,rjhv->rihv", scores, value, precision=HIGHEST)


ON_CHIP = [(0, 1), (1, 0), (2, 3), (3, 2)]
ACROSS = [(0, 2), (2, 0), (1, 3), (3, 1)]
SLOT_XOR = (0, 2, 1, 3)


def row_gather(values):
    across = lax.ppermute(values, "tensor", ACROSS)
    pair = jnp.stack([values, across])
    other = lax.ppermute(pair, "tensor", ON_CHIP)
    return jnp.concatenate([pair, other]).reshape((-1,) + values.shape[1:])


def row_sum(values):
    blocks = values.reshape((4, -1) + values.shape[1:])
    got = lax.ppermute(blocks[2:], "tensor", ON_CHIP)
    mine = blocks[0] + got[0]
    theirs = blocks[1] + got[1]
    return mine + lax.ppermute(theirs.astype(jnp.bfloat16), "tensor", ACROSS).astype(jnp.float32)


def spread_sum(values, axis, count):
    blocks = values.reshape((count, -1) + values.shape[1:])
    got = lax.all_to_all(blocks, axis, 0, 0, tiled=False)
    return got.astype(jnp.float32).sum(axis=0)


def ring_pairs(step, stride, size):
    pairs = []
    for i in range(32):
        pos = (i // stride) % size
        pairs.append((i, i + (((pos + step) % size) - pos) * stride))
    return pairs


def ring_stage(chunks, pos, stride, size):
    half = chunks.shape[-1] // 2
    result = []
    for step, cols in ((1, slice(0, half)), (size - 1, slice(half, None))):
        own = chunks[..., cols]
        pairs = ring_pairs(step, stride, size)

        def pick(k):
            return lax.dynamic_index_in_dim(own, (pos - k * step) % size, 0, keepdims=False)

        acc = pick(1).astype(jnp.float32)
        for k in range(2, size + 1):
            got = lax.ppermute(acc.astype(jnp.bfloat16), "dp", pairs)
            acc = pick(k % size).astype(jnp.float32) + got.astype(jnp.float32)
        result.append(acc)
    return jnp.concatenate(result, axis=-1)


def ring_sum(values):
    index = lax.axis_index("dp")
    x_pos, y_pos, z_pos = index % 4, (index // 4) % 2, index // 8
    blocks = values.reshape((4, 2, 4, -1) + values.shape[1:])
    along_x = ring_stage(jnp.moveaxis(blocks, 2, 0), x_pos, 1, 4)
    along_z = ring_stage(along_x.astype(jnp.bfloat16), z_pos, 8, 4)
    keep = lax.dynamic_index_in_dim(along_z, y_pos, 0, keepdims=False)
    give = lax.dynamic_index_in_dim(along_z, 1 - y_pos, 0, keepdims=False)
    pair = [(i, i ^ 4) for i in range(32)]
    return keep + lax.ppermute(give.astype(jnp.bfloat16), "dp", pair).astype(jnp.float32)


def small_gather(vectors):
    count = 128
    spread = jnp.broadcast_to(vectors[None], (count,) + vectors.shape)
    got = lax.all_to_all(spread, ("dp", "tensor"), 0, 0, tiled=False)
    return jnp.swapaxes(got, 0, 1).reshape(vectors.shape[0], -1)


def small_sum(vectors):
    count = 128
    blocks = vectors.reshape(vectors.shape[0], count, -1)
    got = lax.all_to_all(jnp.swapaxes(blocks, 0, 1), ("dp", "tensor"), 0, 0, tiled=False)
    return got.sum(axis=0)


def shards(
    tokens,
    doc_ids,
    attn_gain,
    forget_floor,
    w_query,
    w_forget,
    w_value,
    w_outgate,
    w_output,
    mlp_gain,
    w_gate,
    w_up,
    w_down,
    cotangent,
):
    gains = small_gather(jnp.stack([attn_gain, forget_floor, mlp_gain]))
    attn_full, floor_full, mlp_full = gains[0], gains[1], gains[2]
    part_index = lax.axis_index("tensor")
    local_width = w_query.shape[1]
    local_heads = local_width // HK
    hidden_width = w_gate.shape[1]
    floor_local = lax.dynamic_slice_in_dim(
        floor_full, part_index * local_width, local_width
    ).reshape(local_heads, HK)
    model_width = attn_full.shape[0]
    slot_rows = jnp.bitwise_xor(part_index, jnp.array(SLOT_XOR, jnp.int32))
    doc_all = jnp.take(doc_ids[0], slot_rows, axis=0)
    row_count = doc_all.shape[0]
    resid_in = tokens[0].reshape(-1, model_width).astype(jnp.float32)
    cot_local = cotangent[0].reshape(-1, model_width)
    attn_pack = jnp.concatenate([w_query, w_forget, w_value, w_outgate, w_output.T], axis=1)
    mlp_pack = jnp.concatenate([w_gate, w_up, w_down.T], axis=1)
    attn_all = lax.all_gather(attn_pack, "dp", axis=0, tiled=True)
    mlp_all = lax.all_gather(mlp_pack, "dp", axis=0, tiled=True)
    wq_all = attn_all[:, 0 * local_width : 1 * local_width]
    wf_all = attn_all[:, 1 * local_width : 2 * local_width]
    wv_all = attn_all[:, 2 * local_width : 3 * local_width]
    wg_all = attn_all[:, 3 * local_width : 4 * local_width]
    wo_t = attn_all[:, 4 * local_width : 5 * local_width]
    wgate_all = mlp_all[:, 0:hidden_width]
    wup_all = mlp_all[:, hidden_width : 2 * hidden_width]
    wdown_t = mlp_all[:, 2 * hidden_width : 3 * hidden_width]
    scale_one = row_scale(resid_in)
    normed = row_gather((resid_in * scale_one * attn_full).astype(jnp.bfloat16))
    query = matmul_plain(normed, wq_all)
    forget_raw = matmul_plain(normed, wf_all)
    value = matmul_plain(normed, wv_all)
    out_gate = matmul_plain(normed, wg_all)

    def mixer(query_in, forget_in, value_in, floor_in):

        def shaped(arr):
            return arr.reshape(row_count, -1, local_heads, HK)

        mixed_rows = recurrence(
            shaped(query_in), shaped(forget_in), shaped(value_in), floor_in, doc_all
        )
        return mixed_rows.reshape(query_in.shape[0], local_width)

    mixed, pullback = jax.vjp(mixer, query, forget_raw, value, floor_local)
    gate_act = jax.nn.silu(out_gate)
    gated = (mixed * gate_act).astype(jnp.bfloat16)
    branch = row_sum(times_trans(gated, wo_t))
    resid = resid_in + branch
    scale_two = row_scale(resid)
    normed2 = row_gather((resid * scale_two * mlp_full).astype(jnp.bfloat16))
    gate_proj = matmul_plain(normed2, wgate_all)
    up_proj = matmul_plain(normed2, wup_all)
    gate_silu = jax.nn.silu(gate_proj)
    hidden = (gate_silu * up_proj).astype(jnp.bfloat16)
    ffn_out = row_sum(times_trans(hidden, wdown_t))
    layer_out = (resid + ffn_out).astype(jnp.bfloat16).reshape(tokens.shape)
    cot_full = row_gather(cot_local)
    d_hidden = matmul_plain(cot_full, wdown_t)
    d_gate = (d_hidden * up_proj * silu_slope(gate_proj)).astype(jnp.bfloat16)
    d_up = (d_hidden * gate_silu).astype(jnp.bfloat16)
    mlp_grads = grad_pack(
        normed2, cot_full, jnp.concatenate([d_gate, d_up, hidden], axis=1), hidden_width
    )
    mlp_red = lax.psum_scatter(mlp_grads, "dp", scatter_dimension=0, tiled=True).astype(jnp.float32)
    d_normed2 = row_sum(times_trans(d_gate, wgate_all) + times_trans(d_up, wup_all))
    grad_mlp = jnp.sum(d_normed2 * resid * scale_two, axis=0)
    inner_two = jnp.mean(d_normed2 * mlp_full * resid, axis=-1, keepdims=True)
    d_resid = (
        cot_local.astype(jnp.float32)
        + d_normed2 * mlp_full * scale_two
        - resid * scale_two**3 * inner_two
    )
    d_branch = row_gather(d_resid.astype(jnp.bfloat16))
    d_gated = matmul_plain(d_branch, wo_t)
    d_mixed = d_gated * gate_act
    d_outgate = (d_gated * mixed * silu_slope(out_gate)).astype(jnp.bfloat16)
    d_query, d_forget, d_value, d_floor = pullback(d_mixed)
    d_query = d_query.astype(jnp.bfloat16)
    d_forget = d_forget.astype(jnp.bfloat16)
    d_value = d_value.astype(jnp.bfloat16)
    attn_grads = grad_pack(
        normed,
        d_branch,
        jnp.concatenate([d_query, d_forget, d_value, d_outgate, gated], axis=1),
        local_width,
    )
    attn_red = ring_sum(attn_grads)
    d_normed = row_sum(
        times_trans(d_query, wq_all)
        + times_trans(d_forget, wf_all)
        + times_trans(d_value, wv_all)
        + times_trans(d_outgate, wg_all)
    )
    grad_attn = jnp.sum(d_normed * resid_in * scale_one, axis=0)
    inner_one = jnp.mean(d_normed * attn_full * resid_in, axis=-1, keepdims=True)
    grad_tokens = (
        d_resid + d_normed * attn_full * scale_one - resid_in * scale_one**3 * inner_one
    ).reshape(tokens.shape)
    floor_vector = lax.dynamic_update_slice(
        jnp.zeros((model_width,), jnp.float32), d_floor.reshape(-1), (part_index * local_width,)
    )
    reduced_small = small_sum(jnp.stack([grad_attn, floor_vector, grad_mlp]))
    return (
        layer_out,
        grad_tokens,
        reduced_small[0],
        reduced_small[1],
        attn_red[:, 0 * local_width : 1 * local_width],
        attn_red[:, 1 * local_width : 2 * local_width],
        attn_red[:, 2 * local_width : 3 * local_width],
        attn_red[:, 3 * local_width : 4 * local_width],
        attn_red[:, 4 * local_width : 5 * local_width].T,
        reduced_small[2],
        mlp_red[:, 0:hidden_width],
        mlp_red[:, hidden_width : 2 * hidden_width],
        mlp_red[:, 2 * hidden_width : 3 * hidden_width].T,
    )


def solution(mesh):
    return jax.shard_map(
        shards,
        mesh=mesh,
        in_specs=(
            P("dp", "tensor", None, None),
            P("dp", None, None),
            P(("dp", "tensor")),
            P(("dp", "tensor")),
            P("dp", "tensor"),
            P("dp", "tensor"),
            P("dp", "tensor"),
            P("dp", "tensor"),
            P("tensor", "dp"),
            P(("dp", "tensor")),
            P("dp", "tensor"),
            P("dp", "tensor"),
            P("tensor", "dp"),
            P("dp", "tensor", None, None),
        ),
        out_specs=(
            P("dp", "tensor", None, None),
            P("dp", "tensor", None, None),
            P(("dp", "tensor")),
            P(("dp", "tensor")),
            P("dp", "tensor"),
            P("dp", "tensor"),
            P("dp", "tensor"),
            P("dp", "tensor"),
            P("tensor", "dp"),
            P(("dp", "tensor")),
            P("dp", "tensor"),
            P("dp", "tensor"),
            P("tensor", "dp"),
        ),
        check_vma=False,
    )
```

```python
import functools

import jax
import jax.numpy as jnp
from jax import lax
from jax.experimental import pallas as pl
from jax.experimental.pallas import tpu as pltpu
from jax.sharding import PartitionSpec as P

HK = 128
HIGHEST = lax.Precision.HIGHEST


epsilon = 1e-06


def row_scale(values):
    return lax.rsqrt(jnp.mean(values * values, axis=-1, keepdims=True) + epsilon)


def silu_slope(values):
    sigmoid_val = jax.nn.sigmoid(values)
    return sigmoid_val * (1.0 + values * (1.0 - sigmoid_val))


def matmul_plain(left, right):
    return jnp.dot(left, right, preferred_element_type=jnp.float32)


def times_trans(left, right):
    return lax.dot_general(
        left, right, (((1,), (1,)), ((), ())), preferred_element_type=jnp.float32
    )


def trans_times(left, right):
    return lax.dot_general(
        left, right, (((0,), (0,)), ((), ())), preferred_element_type=jnp.float32
    )


def pack_kernel(per, first_ref, second_ref, right_ref, out_ref):
    col = pl.program_id(1)

    @pl.when(col < per)
    def _():
        out_ref[...] = jnp.dot(
            first_ref[...].T, right_ref[...], preferred_element_type=jnp.float32
        ).astype(out_ref.dtype)

    @pl.when(col >= per)
    def _():
        out_ref[...] = jnp.dot(
            second_ref[...].T, right_ref[...], preferred_element_type=jnp.float32
        ).astype(out_ref.dtype)


def grad_pack(first, second, right, width):
    depth, rows_out = first.shape
    cols = right.shape[1]
    blocks = cols // width
    per = blocks - 1
    tile = rows_out
    return pl.pallas_call(
        functools.partial(pack_kernel, per),
        grid=(rows_out // tile, blocks),
        in_specs=[
            pl.BlockSpec((depth, tile), lambda i, j: (0, i)),
            pl.BlockSpec((depth, tile), lambda i, j: (0, i)),
            pl.BlockSpec((depth, width), lambda i, j: (0, j)),
        ],
        out_specs=pl.BlockSpec((tile, width), lambda i, j: (i, j)),
        out_shape=jax.ShapeDtypeStruct((rows_out, cols), jnp.bfloat16),
        cost_estimate=pl.CostEstimate(
            flops=2 * depth * rows_out * cols,
            transcendentals=0,
            bytes_accessed=2 * (2 * depth * rows_out + depth * cols + rows_out * cols),
        ),
    )(first, second, right)


def recurrence(query, forget_raw, value, floor_vec, doc_rows):
    length = query.shape[1]
    forget = floor_vec + (1.0 - floor_vec) * jax.nn.sigmoid(forget_raw)
    log_forget = jnp.log(forget)
    keyed = 1.0 - forget
    position = jnp.arange(length)
    same_doc = doc_rows[:, :, None] == doc_rows[:, None, :]
    causal = same_doc & (position[:, None] >= position[None, :])
    starts = jnp.concatenate(
        [jnp.zeros_like(doc_rows[:, :1], dtype=bool), doc_rows[:, 1:] == doc_rows[:, :-1]], axis=1
    )
    summing = (causal & starts[:, None, :]).astype(jnp.float32)
    running = jnp.einsum("rij,rjhk->rihk", summing, log_forget, precision=HIGHEST)
    query_t = query * jnp.exp(running)
    key_t = keyed * jnp.exp(-running)
    scores = jnp.einsum("rihk,rjhk->rhij", query_t, key_t, precision=HIGHEST)
    scores = jnp.where(causal[:, None], scores, 0.0)
    return jnp.einsum("rhij,rjhv->rihv", scores, value, precision=HIGHEST)


ON_CHIP = [(0, 1), (1, 0), (2, 3), (3, 2)]
ACROSS = [(0, 2), (2, 0), (1, 3), (3, 1)]
SLOT_XOR = (0, 2, 1, 3)


def row_gather(values):
    across = lax.ppermute(values, "tensor", ACROSS)
    pair = jnp.stack([values, across])
    other = lax.ppermute(pair, "tensor", ON_CHIP)
    return jnp.concatenate([pair, other]).reshape((-1,) + values.shape[1:])


def row_sum(values):
    blocks = values.reshape((4, -1) + values.shape[1:])
    got = lax.ppermute(blocks[2:], "tensor", ON_CHIP)
    mine = blocks[0] + got[0]
    theirs = blocks[1] + got[1]
    return mine + lax.ppermute(theirs.astype(jnp.bfloat16), "tensor", ACROSS).astype(jnp.float32)


def spread_sum(values, axis, count):
    blocks = values.reshape((count, -1) + values.shape[1:])
    got = lax.all_to_all(blocks, axis, 0, 0, tiled=False)
    return got.astype(jnp.float32).sum(axis=0)


def ring_pairs(step, stride, size):
    pairs = []
    for i in range(32):
        pos = (i // stride) % size
        pairs.append((i, i + (((pos + step) % size) - pos) * stride))
    return pairs


def ring_stage(chunks, pos, stride, size, step):
    pairs = ring_pairs(step, stride, size)

    def pick(k):
        return lax.dynamic_index_in_dim(chunks, (pos - k * step) % size, 0, keepdims=False).astype(
            jnp.float32
        )

    acc = pick(1)
    for k in range(2, size + 1):
        got = lax.ppermute(acc.astype(jnp.bfloat16), "dp", pairs)
        acc = pick(k % size) + got.astype(jnp.float32)
    return acc


def ring_sum(values):
    index = lax.axis_index("dp")
    x_pos, y_pos, z_pos = index % 4, (index // 4) % 2, index // 8
    blocks = values.reshape((4, 2, 4, -1) + values.shape[1:])
    part_rows = blocks.shape[3] // 4
    pieces = []
    for part, (x_first, step) in enumerate(((True, 1), (True, 3), (False, 1), (False, 3))):
        rows = blocks[:, :, :, part * part_rows : (part + 1) * part_rows]
        if x_first:
            once = ring_stage(jnp.moveaxis(rows, 2, 0), x_pos, 1, 4, step)
            twice = ring_stage(once.astype(jnp.bfloat16), z_pos, 8, 4, step)
        else:
            once = ring_stage(rows, z_pos, 8, 4, step)
            twice = ring_stage(jnp.moveaxis(once, 1, 0).astype(jnp.bfloat16), x_pos, 1, 4, step)
        pieces.append(twice)
    both = jnp.concatenate(pieces, axis=1)
    keep = lax.dynamic_index_in_dim(both, y_pos, 0, keepdims=False)
    give = lax.dynamic_index_in_dim(both, 1 - y_pos, 0, keepdims=False)
    pair = [(i, i ^ 4) for i in range(32)]
    return keep + lax.ppermute(give.astype(jnp.bfloat16), "dp", pair).astype(jnp.float32)


def small_gather(vectors):
    count = 128
    spread = jnp.broadcast_to(vectors[None], (count,) + vectors.shape)
    got = lax.all_to_all(spread, ("dp", "tensor"), 0, 0, tiled=False)
    return jnp.swapaxes(got, 0, 1).reshape(vectors.shape[0], -1)


def small_sum(vectors):
    count = 128
    blocks = vectors.reshape(vectors.shape[0], count, -1)
    got = lax.all_to_all(jnp.swapaxes(blocks, 0, 1), ("dp", "tensor"), 0, 0, tiled=False)
    return got.sum(axis=0)


def shards(
    tokens,
    doc_ids,
    attn_gain,
    forget_floor,
    w_query,
    w_forget,
    w_value,
    w_outgate,
    w_output,
    mlp_gain,
    w_gate,
    w_up,
    w_down,
    cotangent,
):
    gains = small_gather(jnp.stack([attn_gain, forget_floor, mlp_gain]))
    attn_full, floor_full, mlp_full = gains[0], gains[1], gains[2]
    part_index = lax.axis_index("tensor")
    local_width = w_query.shape[1]
    local_heads = local_width // HK
    hidden_width = w_gate.shape[1]
    floor_local = lax.dynamic_slice_in_dim(
        floor_full, part_index * local_width, local_width
    ).reshape(local_heads, HK)
    model_width = attn_full.shape[0]
    slot_rows = jnp.bitwise_xor(part_index, jnp.array(SLOT_XOR, jnp.int32))
    doc_all = jnp.take(doc_ids[0], slot_rows, axis=0)
    row_count = doc_all.shape[0]
    resid_in = tokens[0].reshape(-1, model_width).astype(jnp.float32)
    cot_local = cotangent[0].reshape(-1, model_width)
    attn_pack = jnp.concatenate([w_query, w_forget, w_value, w_outgate, w_output.T], axis=1)
    mlp_pack = jnp.concatenate([w_gate, w_up, w_down.T], axis=1)
    attn_all = lax.all_gather(attn_pack, "dp", axis=0, tiled=True)
    mlp_all = lax.all_gather(mlp_pack, "dp", axis=0, tiled=True)
    wq_all = attn_all[:, 0 * local_width : 1 * local_width]
    wf_all = attn_all[:, 1 * local_width : 2 * local_width]
    wv_all = attn_all[:, 2 * local_width : 3 * local_width]
    wg_all = attn_all[:, 3 * local_width : 4 * local_width]
    wo_t = attn_all[:, 4 * local_width : 5 * local_width]
    wgate_all = mlp_all[:, 0:hidden_width]
    wup_all = mlp_all[:, hidden_width : 2 * hidden_width]
    wdown_t = mlp_all[:, 2 * hidden_width : 3 * hidden_width]
    scale_one = row_scale(resid_in)
    normed = row_gather((resid_in * scale_one * attn_full).astype(jnp.bfloat16))
    query = matmul_plain(normed, wq_all)
    forget_raw = matmul_plain(normed, wf_all)
    value = matmul_plain(normed, wv_all)
    out_gate = matmul_plain(normed, wg_all)

    def mixer(query_in, forget_in, value_in, floor_in):

        def shaped(arr):
            return arr.reshape(row_count, -1, local_heads, HK)

        mixed_rows = recurrence(
            shaped(query_in), shaped(forget_in), shaped(value_in), floor_in, doc_all
        )
        return mixed_rows.reshape(query_in.shape[0], local_width)

    mixed, pullback = jax.vjp(mixer, query, forget_raw, value, floor_local)
    gate_act = jax.nn.silu(out_gate)
    gated = (mixed * gate_act).astype(jnp.bfloat16)
    branch = row_sum(times_trans(gated, wo_t))
    resid = resid_in + branch
    scale_two = row_scale(resid)
    normed2 = row_gather((resid * scale_two * mlp_full).astype(jnp.bfloat16))
    gate_proj = matmul_plain(normed2, wgate_all)
    up_proj = matmul_plain(normed2, wup_all)
    gate_silu = jax.nn.silu(gate_proj)
    hidden = (gate_silu * up_proj).astype(jnp.bfloat16)
    ffn_out = row_sum(times_trans(hidden, wdown_t))
    layer_out = (resid + ffn_out).astype(jnp.bfloat16).reshape(tokens.shape)
    cot_full = row_gather(cot_local)
    d_hidden = matmul_plain(cot_full, wdown_t)
    d_gate = (d_hidden * up_proj * silu_slope(gate_proj)).astype(jnp.bfloat16)
    d_up = (d_hidden * gate_silu).astype(jnp.bfloat16)
    mlp_grads = grad_pack(
        normed2, cot_full, jnp.concatenate([d_gate, d_up, hidden], axis=1), hidden_width
    )
    mlp_red = ring_sum(mlp_grads)
    d_normed2 = row_sum(times_trans(d_gate, wgate_all) + times_trans(d_up, wup_all))
    grad_mlp = jnp.sum(d_normed2 * resid * scale_two, axis=0)
    inner_two = jnp.mean(d_normed2 * mlp_full * resid, axis=-1, keepdims=True)
    d_resid = (
        cot_local.astype(jnp.float32)
        + d_normed2 * mlp_full * scale_two
        - resid * scale_two**3 * inner_two
    )
    d_branch = row_gather(d_resid.astype(jnp.bfloat16))
    d_gated = matmul_plain(d_branch, wo_t)
    d_mixed = d_gated * gate_act
    d_outgate = (d_gated * mixed * silu_slope(out_gate)).astype(jnp.bfloat16)
    d_query, d_forget, d_value, d_floor = pullback(d_mixed)
    d_query = d_query.astype(jnp.bfloat16)
    d_forget = d_forget.astype(jnp.bfloat16)
    d_value = d_value.astype(jnp.bfloat16)
    attn_grads = grad_pack(
        normed,
        d_branch,
        jnp.concatenate([d_query, d_forget, d_value, d_outgate, gated], axis=1),
        local_width,
    )
    attn_red = ring_sum(attn_grads)
    d_normed = row_sum(
        times_trans(d_query, wq_all)
        + times_trans(d_forget, wf_all)
        + times_trans(d_value, wv_all)
        + times_trans(d_outgate, wg_all)
    )
    grad_attn = jnp.sum(d_normed * resid_in * scale_one, axis=0)
    inner_one = jnp.mean(d_normed * attn_full * resid_in, axis=-1, keepdims=True)
    grad_tokens = (
        d_resid + d_normed * attn_full * scale_one - resid_in * scale_one**3 * inner_one
    ).reshape(tokens.shape)
    floor_vector = lax.dynamic_update_slice(
        jnp.zeros((model_width,), jnp.float32), d_floor.reshape(-1), (part_index * local_width,)
    )
    reduced_small = small_sum(jnp.stack([grad_attn, floor_vector, grad_mlp]))
    return (
        layer_out,
        grad_tokens,
        reduced_small[0],
        reduced_small[1],
        attn_red[:, 0 * local_width : 1 * local_width],
        attn_red[:, 1 * local_width : 2 * local_width],
        attn_red[:, 2 * local_width : 3 * local_width],
        attn_red[:, 3 * local_width : 4 * local_width],
        attn_red[:, 4 * local_width : 5 * local_width].T,
        reduced_small[2],
        mlp_red[:, 0:hidden_width],
        mlp_red[:, hidden_width : 2 * hidden_width],
        mlp_red[:, 2 * hidden_width : 3 * hidden_width].T,
    )


def solution(mesh):
    return jax.shard_map(
        shards,
        mesh=mesh,
        in_specs=(
            P("dp", "tensor", None, None),
            P("dp", None, None),
            P(("dp", "tensor")),
            P(("dp", "tensor")),
            P("dp", "tensor"),
            P("dp", "tensor"),
            P("dp", "tensor"),
            P("dp", "tensor"),
            P("tensor", "dp"),
            P(("dp", "tensor")),
            P("dp", "tensor"),
            P("dp", "tensor"),
            P("tensor", "dp"),
            P("dp", "tensor", None, None),
        ),
        out_specs=(
            P("dp", "tensor", None, None),
            P("dp", "tensor", None, None),
            P(("dp", "tensor")),
            P(("dp", "tensor")),
            P("dp", "tensor"),
            P("dp", "tensor"),
            P("dp", "tensor"),
            P("dp", "tensor"),
            P("tensor", "dp"),
            P(("dp", "tensor")),
            P("dp", "tensor"),
            P("dp", "tensor"),
            P("tensor", "dp"),
        ),
        check_vma=False,
    )
```

```python
import functools

import jax
import jax.numpy as jnp
from jax import lax
from jax.experimental import pallas as pl
from jax.experimental.pallas import tpu as pltpu
from jax.sharding import PartitionSpec as P

HK = 128
HIGHEST = lax.Precision.HIGHEST


epsilon = 1e-06


def row_scale(values):
    return lax.rsqrt(jnp.mean(values * values, axis=-1, keepdims=True) + epsilon)


def silu_slope(values):
    sigmoid_val = jax.nn.sigmoid(values)
    return sigmoid_val * (1.0 + values * (1.0 - sigmoid_val))


def matmul_plain(left, right):
    return jnp.dot(left, right, preferred_element_type=jnp.float32)


def times_trans(left, right):
    return lax.dot_general(
        left, right, (((1,), (1,)), ((), ())), preferred_element_type=jnp.float32
    )


def trans_times(left, right):
    return lax.dot_general(
        left, right, (((0,), (0,)), ((), ())), preferred_element_type=jnp.float32
    )


def pack_kernel(per, first_ref, second_ref, right_ref, out_ref):
    col = pl.program_id(1)

    @pl.when(col < per)
    def _():
        out_ref[...] = jnp.dot(
            first_ref[...].T, right_ref[...], preferred_element_type=jnp.float32
        ).astype(out_ref.dtype)

    @pl.when(col >= per)
    def _():
        out_ref[...] = jnp.dot(
            second_ref[...].T, right_ref[...], preferred_element_type=jnp.float32
        ).astype(out_ref.dtype)


def grad_pack(first, second, right, width):
    depth, rows_out = first.shape
    cols = right.shape[1]
    blocks = cols // width
    per = blocks - 1
    tile = rows_out
    return pl.pallas_call(
        functools.partial(pack_kernel, per),
        grid=(rows_out // tile, blocks),
        in_specs=[
            pl.BlockSpec((depth, tile), lambda i, j: (0, i)),
            pl.BlockSpec((depth, tile), lambda i, j: (0, i)),
            pl.BlockSpec((depth, width), lambda i, j: (0, j)),
        ],
        out_specs=pl.BlockSpec((tile, width), lambda i, j: (i, j)),
        out_shape=jax.ShapeDtypeStruct((rows_out, cols), jnp.bfloat16),
        cost_estimate=pl.CostEstimate(
            flops=2 * depth * rows_out * cols,
            transcendentals=0,
            bytes_accessed=2 * (2 * depth * rows_out + depth * cols + rows_out * cols),
        ),
    )(first, second, right)


def recurrence(query, forget_raw, value, floor_vec, doc_rows):
    length = query.shape[1]
    forget = floor_vec + (1.0 - floor_vec) * jax.nn.sigmoid(forget_raw)
    log_forget = jnp.log(forget)
    keyed = 1.0 - forget
    position = jnp.arange(length)
    same_doc = doc_rows[:, :, None] == doc_rows[:, None, :]
    causal = same_doc & (position[:, None] >= position[None, :])
    starts = jnp.concatenate(
        [jnp.zeros_like(doc_rows[:, :1], dtype=bool), doc_rows[:, 1:] == doc_rows[:, :-1]], axis=1
    )
    summing = (causal & starts[:, None, :]).astype(jnp.float32)
    running = jnp.einsum("rij,rjhk->rihk", summing, log_forget, precision=HIGHEST)
    query_t = query * jnp.exp(running)
    key_t = keyed * jnp.exp(-running)
    scores = jnp.einsum("rihk,rjhk->rhij", query_t, key_t, precision=HIGHEST)
    scores = jnp.where(causal[:, None], scores, 0.0)
    return jnp.einsum("rhij,rjhv->rihv", scores, value, precision=HIGHEST)


ON_CHIP = [(0, 1), (1, 0), (2, 3), (3, 2)]
ACROSS = [(0, 2), (2, 0), (1, 3), (3, 1)]
SLOT_XOR = (0, 2, 1, 3)


def row_gather(values):
    across = lax.ppermute(values, "tensor", ACROSS)
    pair = jnp.stack([values, across])
    other = lax.ppermute(pair, "tensor", ON_CHIP)
    return jnp.concatenate([pair, other]).reshape((-1,) + values.shape[1:])


def row_sum(values):
    blocks = values.reshape((4, -1) + values.shape[1:])
    got = lax.ppermute(blocks[2:], "tensor", ON_CHIP)
    mine = blocks[0] + got[0]
    theirs = blocks[1] + got[1]
    return mine + lax.ppermute(theirs.astype(jnp.bfloat16), "tensor", ACROSS).astype(jnp.float32)


def spread_sum(values, axis, count):
    blocks = values.reshape((count, -1) + values.shape[1:])
    got = lax.all_to_all(blocks, axis, 0, 0, tiled=False)
    return got.astype(jnp.float32).sum(axis=0)


def ring_pairs(step, stride, size):
    pairs = []
    for i in range(32):
        pos = (i // stride) % size
        pairs.append((i, i + (((pos + step) % size) - pos) * stride))
    return pairs


def ring_stage(chunks, pos, stride, size):
    half = chunks.shape[-1] // 2
    result = []
    for step, cols in ((1, slice(0, half)), (size - 1, slice(half, None))):
        own = chunks[..., cols]
        pairs = ring_pairs(step, stride, size)

        def pick(k):
            return lax.dynamic_index_in_dim(own, (pos - k * step) % size, 0, keepdims=False)

        acc = pick(1).astype(jnp.float32)
        for k in range(2, size + 1):
            got = lax.ppermute(acc.astype(jnp.bfloat16), "dp", pairs)
            acc = pick(k % size).astype(jnp.float32) + got.astype(jnp.float32)
        result.append(acc)
    return jnp.concatenate(result, axis=-1)


def ring_sum(values):
    index = lax.axis_index("dp")
    x_pos, y_pos, z_pos = index % 4, (index // 4) % 2, index // 8
    blocks = values.reshape((4, 2, 4, -1) + values.shape[1:])
    along_x = ring_stage(jnp.moveaxis(blocks, 2, 0), x_pos, 1, 4)
    along_z = ring_stage(along_x.astype(jnp.bfloat16), z_pos, 8, 4)
    keep = lax.dynamic_index_in_dim(along_z, y_pos, 0, keepdims=False)
    give = lax.dynamic_index_in_dim(along_z, 1 - y_pos, 0, keepdims=False)
    pair = [(i, i ^ 4) for i in range(32)]
    return keep + lax.ppermute(give.astype(jnp.bfloat16), "dp", pair).astype(jnp.float32)


def ring_collect(chunk, pos, stride, size, step):
    pairs = ring_pairs(step, stride, size)
    got = [chunk]
    for _ in range(size - 1):
        got.append(lax.ppermute(got[-1], "dp", pairs))
    relative = jnp.stack(got)
    if step == 1:
        where_from = (pos - jnp.arange(size)) % size
    else:
        where_from = (jnp.arange(size) - pos) % size
    return jnp.take(relative, where_from, axis=0)


def ring_gather(values):
    index = lax.axis_index("dp")
    x_pos, y_pos, z_pos = index % 4, (index // 4) % 2, index // 8
    pair = [(i, i ^ 4) for i in range(32)]
    other = lax.ppermute(values, "dp", pair)
    both = jnp.where(y_pos == 0, jnp.stack([values, other]), jnp.stack([other, values]))
    part_rows = values.shape[0] // 4
    pieces = []
    for part, (x_first, step) in enumerate(((True, 1), (True, 3), (False, 1), (False, 3))):
        rows = both[:, part * part_rows : (part + 1) * part_rows]
        if x_first:
            once = ring_collect(rows, x_pos, 1, 4, step)
            twice = ring_collect(once, z_pos, 8, 4, step)
            pieces.append(jnp.moveaxis(twice, 1, 2))
        else:
            once = ring_collect(rows, z_pos, 8, 4, step)
            twice = ring_collect(once, x_pos, 1, 4, step)
            pieces.append(jnp.moveaxis(twice, 0, 2))
    return jnp.concatenate(pieces, axis=3).reshape((-1,) + values.shape[1:])


def small_gather(vectors):
    count = 128
    spread = jnp.broadcast_to(vectors[None], (count,) + vectors.shape)
    got = lax.all_to_all(spread, ("dp", "tensor"), 0, 0, tiled=False)
    return jnp.swapaxes(got, 0, 1).reshape(vectors.shape[0], -1)


def small_sum(vectors):
    count = 128
    blocks = vectors.reshape(vectors.shape[0], count, -1)
    got = lax.all_to_all(jnp.swapaxes(blocks, 0, 1), ("dp", "tensor"), 0, 0, tiled=False)
    return got.sum(axis=0)


def shards(
    tokens,
    doc_ids,
    attn_gain,
    forget_floor,
    w_query,
    w_forget,
    w_value,
    w_outgate,
    w_output,
    mlp_gain,
    w_gate,
    w_up,
    w_down,
    cotangent,
):
    gains = small_gather(jnp.stack([attn_gain, forget_floor, mlp_gain]))
    attn_full, floor_full, mlp_full = gains[0], gains[1], gains[2]
    part_index = lax.axis_index("tensor")
    local_width = w_query.shape[1]
    local_heads = local_width // HK
    hidden_width = w_gate.shape[1]
    floor_local = lax.dynamic_slice_in_dim(
        floor_full, part_index * local_width, local_width
    ).reshape(local_heads, HK)
    model_width = attn_full.shape[0]
    slot_rows = jnp.bitwise_xor(part_index, jnp.array(SLOT_XOR, jnp.int32))
    doc_all = jnp.take(doc_ids[0], slot_rows, axis=0)
    row_count = doc_all.shape[0]
    resid_in = tokens[0].reshape(-1, model_width).astype(jnp.float32)
    cot_local = cotangent[0].reshape(-1, model_width)
    attn_pack = jnp.concatenate([w_query, w_forget, w_value, w_outgate, w_output.T], axis=1)
    mlp_pack = jnp.concatenate([w_gate, w_up, w_down.T], axis=1)
    attn_all = ring_gather(attn_pack)
    mlp_all = lax.all_gather(mlp_pack, "dp", axis=0, tiled=True)
    wq_all = attn_all[:, 0 * local_width : 1 * local_width]
    wf_all = attn_all[:, 1 * local_width : 2 * local_width]
    wv_all = attn_all[:, 2 * local_width : 3 * local_width]
    wg_all = attn_all[:, 3 * local_width : 4 * local_width]
    wo_t = attn_all[:, 4 * local_width : 5 * local_width]
    wgate_all = mlp_all[:, 0:hidden_width]
    wup_all = mlp_all[:, hidden_width : 2 * hidden_width]
    wdown_t = mlp_all[:, 2 * hidden_width : 3 * hidden_width]
    scale_one = row_scale(resid_in)
    normed = row_gather((resid_in * scale_one * attn_full).astype(jnp.bfloat16))
    query = matmul_plain(normed, wq_all)
    forget_raw = matmul_plain(normed, wf_all)
    value = matmul_plain(normed, wv_all)
    out_gate = matmul_plain(normed, wg_all)

    def mixer(query_in, forget_in, value_in, floor_in):

        def shaped(arr):
            return arr.reshape(row_count, -1, local_heads, HK)

        mixed_rows = recurrence(
            shaped(query_in), shaped(forget_in), shaped(value_in), floor_in, doc_all
        )
        return mixed_rows.reshape(query_in.shape[0], local_width)

    mixed, pullback = jax.vjp(mixer, query, forget_raw, value, floor_local)
    gate_act = jax.nn.silu(out_gate)
    gated = (mixed * gate_act).astype(jnp.bfloat16)
    branch = row_sum(times_trans(gated, wo_t))
    resid = resid_in + branch
    scale_two = row_scale(resid)
    normed2 = row_gather((resid * scale_two * mlp_full).astype(jnp.bfloat16))
    gate_proj = matmul_plain(normed2, wgate_all)
    up_proj = matmul_plain(normed2, wup_all)
    gate_silu = jax.nn.silu(gate_proj)
    hidden = (gate_silu * up_proj).astype(jnp.bfloat16)
    ffn_out = row_sum(times_trans(hidden, wdown_t))
    layer_out = (resid + ffn_out).astype(jnp.bfloat16).reshape(tokens.shape)
    cot_full = row_gather(cot_local)
    d_hidden = matmul_plain(cot_full, wdown_t)
    d_gate = (d_hidden * up_proj * silu_slope(gate_proj)).astype(jnp.bfloat16)
    d_up = (d_hidden * gate_silu).astype(jnp.bfloat16)
    mlp_grads = grad_pack(
        normed2, cot_full, jnp.concatenate([d_gate, d_up, hidden], axis=1), hidden_width
    )
    mlp_red = lax.psum_scatter(mlp_grads, "dp", scatter_dimension=0, tiled=True).astype(jnp.float32)
    d_normed2 = row_sum(times_trans(d_gate, wgate_all) + times_trans(d_up, wup_all))
    grad_mlp = jnp.sum(d_normed2 * resid * scale_two, axis=0)
    inner_two = jnp.mean(d_normed2 * mlp_full * resid, axis=-1, keepdims=True)
    d_resid = (
        cot_local.astype(jnp.float32)
        + d_normed2 * mlp_full * scale_two
        - resid * scale_two**3 * inner_two
    )
    d_branch = row_gather(d_resid.astype(jnp.bfloat16))
    d_gated = matmul_plain(d_branch, wo_t)
    d_mixed = d_gated * gate_act
    d_outgate = (d_gated * mixed * silu_slope(out_gate)).astype(jnp.bfloat16)
    d_query, d_forget, d_value, d_floor = pullback(d_mixed)
    d_query = d_query.astype(jnp.bfloat16)
    d_forget = d_forget.astype(jnp.bfloat16)
    d_value = d_value.astype(jnp.bfloat16)
    attn_grads = grad_pack(
        normed,
        d_branch,
        jnp.concatenate([d_query, d_forget, d_value, d_outgate, gated], axis=1),
        local_width,
    )
    attn_red = ring_sum(attn_grads)
    d_normed = row_sum(
        times_trans(d_query, wq_all)
        + times_trans(d_forget, wf_all)
        + times_trans(d_value, wv_all)
        + times_trans(d_outgate, wg_all)
    )
    grad_attn = jnp.sum(d_normed * resid_in * scale_one, axis=0)
    inner_one = jnp.mean(d_normed * attn_full * resid_in, axis=-1, keepdims=True)
    grad_tokens = (
        d_resid + d_normed * attn_full * scale_one - resid_in * scale_one**3 * inner_one
    ).reshape(tokens.shape)
    floor_vector = lax.dynamic_update_slice(
        jnp.zeros((model_width,), jnp.float32), d_floor.reshape(-1), (part_index * local_width,)
    )
    reduced_small = small_sum(jnp.stack([grad_attn, floor_vector, grad_mlp]))
    return (
        layer_out,
        grad_tokens,
        reduced_small[0],
        reduced_small[1],
        attn_red[:, 0 * local_width : 1 * local_width],
        attn_red[:, 1 * local_width : 2 * local_width],
        attn_red[:, 2 * local_width : 3 * local_width],
        attn_red[:, 3 * local_width : 4 * local_width],
        attn_red[:, 4 * local_width : 5 * local_width].T,
        reduced_small[2],
        mlp_red[:, 0:hidden_width],
        mlp_red[:, hidden_width : 2 * hidden_width],
        mlp_red[:, 2 * hidden_width : 3 * hidden_width].T,
    )


def solution(mesh):
    return jax.shard_map(
        shards,
        mesh=mesh,
        in_specs=(
            P("dp", "tensor", None, None),
            P("dp", None, None),
            P(("dp", "tensor")),
            P(("dp", "tensor")),
            P("dp", "tensor"),
            P("dp", "tensor"),
            P("dp", "tensor"),
            P("dp", "tensor"),
            P("tensor", "dp"),
            P(("dp", "tensor")),
            P("dp", "tensor"),
            P("dp", "tensor"),
            P("tensor", "dp"),
            P("dp", "tensor", None, None),
        ),
        out_specs=(
            P("dp", "tensor", None, None),
            P("dp", "tensor", None, None),
            P(("dp", "tensor")),
            P(("dp", "tensor")),
            P("dp", "tensor"),
            P("dp", "tensor"),
            P("dp", "tensor"),
            P("dp", "tensor"),
            P("tensor", "dp"),
            P(("dp", "tensor")),
            P("dp", "tensor"),
            P("dp", "tensor"),
            P("tensor", "dp"),
        ),
        check_vma=False,
    )
```

```python
import functools

import jax
import jax.numpy as jnp
from jax import lax
from jax.experimental import pallas as pl
from jax.experimental.pallas import tpu as pltpu
from jax.sharding import PartitionSpec as P

HK = 128
HIGHEST = lax.Precision.HIGHEST


epsilon = 1e-06


def row_scale(values):
    return lax.rsqrt(jnp.mean(values * values, axis=-1, keepdims=True) + epsilon)


def silu_slope(values):
    sigmoid_val = jax.nn.sigmoid(values)
    return sigmoid_val * (1.0 + values * (1.0 - sigmoid_val))


def matmul_plain(left, right):
    return jnp.dot(left, right, preferred_element_type=jnp.float32)


def times_trans(left, right):
    return lax.dot_general(
        left, right, (((1,), (1,)), ((), ())), preferred_element_type=jnp.float32
    )


def trans_times(left, right):
    return lax.dot_general(
        left, right, (((0,), (0,)), ((), ())), preferred_element_type=jnp.float32
    )


def pack_kernel(per, first_ref, second_ref, right_ref, out_ref):
    col = pl.program_id(1)

    @pl.when(col < per)
    def _():
        out_ref[...] = jnp.dot(
            first_ref[...].T, right_ref[...], preferred_element_type=jnp.float32
        ).astype(out_ref.dtype)

    @pl.when(col >= per)
    def _():
        out_ref[...] = jnp.dot(
            second_ref[...].T, right_ref[...], preferred_element_type=jnp.float32
        ).astype(out_ref.dtype)


def grad_pack(first, second, right, width):
    depth, rows_out = first.shape
    cols = right.shape[1]
    blocks = cols // width
    per = blocks - 1
    tile = rows_out
    return pl.pallas_call(
        functools.partial(pack_kernel, per),
        grid=(rows_out // tile, blocks),
        in_specs=[
            pl.BlockSpec((depth, tile), lambda i, j: (0, i)),
            pl.BlockSpec((depth, tile), lambda i, j: (0, i)),
            pl.BlockSpec((depth, width), lambda i, j: (0, j)),
        ],
        out_specs=pl.BlockSpec((tile, width), lambda i, j: (i, j)),
        out_shape=jax.ShapeDtypeStruct((rows_out, cols), jnp.bfloat16),
        cost_estimate=pl.CostEstimate(
            flops=2 * depth * rows_out * cols,
            transcendentals=0,
            bytes_accessed=2 * (2 * depth * rows_out + depth * cols + rows_out * cols),
        ),
    )(first, second, right)


def recurrence(query, forget_raw, value, floor_vec, doc_rows):
    length = query.shape[1]
    forget = floor_vec + (1.0 - floor_vec) * jax.nn.sigmoid(forget_raw)
    log_forget = jnp.log(forget)
    keyed = 1.0 - forget
    position = jnp.arange(length)
    same_doc = doc_rows[:, :, None] == doc_rows[:, None, :]
    causal = same_doc & (position[:, None] >= position[None, :])
    starts = jnp.concatenate(
        [jnp.zeros_like(doc_rows[:, :1], dtype=bool), doc_rows[:, 1:] == doc_rows[:, :-1]], axis=1
    )
    summing = (causal & starts[:, None, :]).astype(jnp.float32)
    running = jnp.einsum("rij,rjhk->rihk", summing, log_forget, precision=HIGHEST)
    query_t = query * jnp.exp(running)
    key_t = keyed * jnp.exp(-running)
    scores = jnp.einsum("rihk,rjhk->rhij", query_t, key_t, precision=HIGHEST)
    scores = jnp.where(causal[:, None], scores, 0.0)
    return jnp.einsum("rhij,rjhv->rihv", scores, value, precision=HIGHEST)


ON_CHIP = [(0, 1), (1, 0), (2, 3), (3, 2)]
ACROSS = [(0, 2), (2, 0), (1, 3), (3, 1)]
SLOT_XOR = (0, 2, 1, 3)


def row_gather(values):
    across = lax.ppermute(values, "tensor", ACROSS)
    pair = jnp.stack([values, across])
    other = lax.ppermute(pair, "tensor", ON_CHIP)
    return jnp.concatenate([pair, other]).reshape((-1,) + values.shape[1:])


def row_sum(values):
    blocks = values.reshape((4, -1) + values.shape[1:])
    got = lax.ppermute(blocks[2:], "tensor", ON_CHIP)
    mine = blocks[0] + got[0]
    theirs = blocks[1] + got[1]
    return mine + lax.ppermute(theirs.astype(jnp.bfloat16), "tensor", ACROSS).astype(jnp.float32)


def spread_sum(values, axis, count):
    blocks = values.reshape((count, -1) + values.shape[1:])
    got = lax.all_to_all(blocks, axis, 0, 0, tiled=False)
    return got.astype(jnp.float32).sum(axis=0)


def ring_pairs(step, stride, size):
    pairs = []
    for i in range(32):
        pos = (i // stride) % size
        pairs.append((i, i + (((pos + step) % size) - pos) * stride))
    return pairs


def ring_stage(chunks, pos, stride, size):
    half = chunks.shape[-1] // 2
    result = []
    for step, cols in ((1, slice(0, half)), (size - 1, slice(half, None))):
        own = chunks[..., cols]
        pairs = ring_pairs(step, stride, size)

        def pick(k):
            return lax.dynamic_index_in_dim(own, (pos - k * step) % size, 0, keepdims=False)

        acc = pick(1).astype(jnp.float32)
        for k in range(2, size + 1):
            got = lax.ppermute(acc.astype(jnp.bfloat16), "dp", pairs)
            acc = pick(k % size).astype(jnp.float32) + got.astype(jnp.float32)
        result.append(acc)
    return jnp.concatenate(result, axis=-1)


def ring_sum(values):
    index = lax.axis_index("dp")
    x_pos, y_pos, z_pos = index % 4, (index // 4) % 2, index // 8
    blocks = values.reshape((4, 2, 4, -1) + values.shape[1:])
    along_x = ring_stage(jnp.moveaxis(blocks, 2, 0), x_pos, 1, 4)
    along_z = ring_stage(along_x.astype(jnp.bfloat16), z_pos, 8, 4)
    keep = lax.dynamic_index_in_dim(along_z, y_pos, 0, keepdims=False)
    give = lax.dynamic_index_in_dim(along_z, 1 - y_pos, 0, keepdims=False)
    pair = [(i, i ^ 4) for i in range(32)]
    return keep + lax.ppermute(give.astype(jnp.bfloat16), "dp", pair).astype(jnp.float32)


def ring_gather(values):
    index = lax.axis_index("dp")
    x_pos, y_pos, z_pos = index % 4, (index // 4) % 2, index // 8
    zero = jnp.zeros((), jnp.int32)
    pair = [(i, i ^ 4) for i in range(32)]
    other = lax.ppermute(values, "dp", pair)
    both = jnp.zeros((2,) + values.shape, values.dtype)
    both = lax.dynamic_update_slice(both, values[None], (y_pos, zero, zero))
    both = lax.dynamic_update_slice(both, other[None], (1 - y_pos, zero, zero))
    part_rows = values.shape[0] // 4
    cols = values.shape[1]
    full = jnp.zeros((4, 2, 4) + values.shape, values.dtype)
    for part, (x_first, step) in enumerate(((True, 1), (True, 3), (False, 1), (False, 3))):
        rows = both[:, part * part_rows : (part + 1) * part_rows]
        row_at = jnp.full((), part * part_rows, jnp.int32)
        if x_first:
            pairs = ring_pairs(step, 1, 4)
            first = jnp.zeros((2, 4, part_rows, cols), values.dtype)
            cur = rows
            first = lax.dynamic_update_slice(first, cur[:, None], (zero, x_pos, zero, zero))
            for k in range(1, 4):
                cur = lax.ppermute(cur, "dp", pairs)
                first = lax.dynamic_update_slice(first, cur[:, None], (zero, (x_pos - k * step) % 4, zero, zero))
            pairs = ring_pairs(step, 8, 4)
            cur = first
            full = lax.dynamic_update_slice(full, cur[None], (z_pos, zero, zero, row_at, zero))
            for k in range(1, 4):
                cur = lax.ppermute(cur, "dp", pairs)
                full = lax.dynamic_update_slice(full, cur[None], ((z_pos - k * step) % 4, zero, zero, row_at, zero))
        else:
            pairs = ring_pairs(step, 8, 4)
            first = jnp.zeros((4, 2, part_rows, cols), values.dtype)
            cur = rows
            first = lax.dynamic_update_slice(first, cur[None], (z_pos, zero, zero, zero))
            for k in range(1, 4):
                cur = lax.ppermute(cur, "dp", pairs)
                first = lax.dynamic_update_slice(first, cur[None], ((z_pos - k * step) % 4, zero, zero, zero))
            pairs = ring_pairs(step, 1, 4)
            cur = first
            full = lax.dynamic_update_slice(full, cur[:, :, None], (zero, zero, x_pos, row_at, zero))
            for k in range(1, 4):
                cur = lax.ppermute(cur, "dp", pairs)
                full = lax.dynamic_update_slice(full, cur[:, :, None], (zero, zero, (x_pos - k * step) % 4, row_at, zero))
    return full.reshape((-1, cols))


def small_gather(vectors):
    count = 128
    spread = jnp.broadcast_to(vectors[None], (count,) + vectors.shape)
    got = lax.all_to_all(spread, ("dp", "tensor"), 0, 0, tiled=False)
    return jnp.swapaxes(got, 0, 1).reshape(vectors.shape[0], -1)


def small_sum(vectors):
    count = 128
    blocks = vectors.reshape(vectors.shape[0], count, -1)
    got = lax.all_to_all(jnp.swapaxes(blocks, 0, 1), ("dp", "tensor"), 0, 0, tiled=False)
    return got.sum(axis=0)


def shards(
    tokens,
    doc_ids,
    attn_gain,
    forget_floor,
    w_query,
    w_forget,
    w_value,
    w_outgate,
    w_output,
    mlp_gain,
    w_gate,
    w_up,
    w_down,
    cotangent,
):
    gains = small_gather(jnp.stack([attn_gain, forget_floor, mlp_gain]))
    attn_full, floor_full, mlp_full = gains[0], gains[1], gains[2]
    part_index = lax.axis_index("tensor")
    local_width = w_query.shape[1]
    local_heads = local_width // HK
    hidden_width = w_gate.shape[1]
    floor_local = lax.dynamic_slice_in_dim(
        floor_full, part_index * local_width, local_width
    ).reshape(local_heads, HK)
    model_width = attn_full.shape[0]
    slot_rows = jnp.bitwise_xor(part_index, jnp.array(SLOT_XOR, jnp.int32))
    doc_all = jnp.take(doc_ids[0], slot_rows, axis=0)
    row_count = doc_all.shape[0]
    resid_in = tokens[0].reshape(-1, model_width).astype(jnp.float32)
    cot_local = cotangent[0].reshape(-1, model_width)
    attn_pack = jnp.concatenate([w_query, w_forget, w_value, w_outgate, w_output.T], axis=1)
    mlp_pack = jnp.concatenate([w_gate, w_up, w_down.T], axis=1)
    attn_all = ring_gather(attn_pack)
    mlp_all = lax.all_gather(mlp_pack, "dp", axis=0, tiled=True)
    wq_all = attn_all[:, 0 * local_width : 1 * local_width]
    wf_all = attn_all[:, 1 * local_width : 2 * local_width]
    wv_all = attn_all[:, 2 * local_width : 3 * local_width]
    wg_all = attn_all[:, 3 * local_width : 4 * local_width]
    wo_t = attn_all[:, 4 * local_width : 5 * local_width]
    wgate_all = mlp_all[:, 0:hidden_width]
    wup_all = mlp_all[:, hidden_width : 2 * hidden_width]
    wdown_t = mlp_all[:, 2 * hidden_width : 3 * hidden_width]
    scale_one = row_scale(resid_in)
    normed = row_gather((resid_in * scale_one * attn_full).astype(jnp.bfloat16))
    query = matmul_plain(normed, wq_all)
    forget_raw = matmul_plain(normed, wf_all)
    value = matmul_plain(normed, wv_all)
    out_gate = matmul_plain(normed, wg_all)

    def mixer(query_in, forget_in, value_in, floor_in):

        def shaped(arr):
            return arr.reshape(row_count, -1, local_heads, HK)

        mixed_rows = recurrence(
            shaped(query_in), shaped(forget_in), shaped(value_in), floor_in, doc_all
        )
        return mixed_rows.reshape(query_in.shape[0], local_width)

    mixed, pullback = jax.vjp(mixer, query, forget_raw, value, floor_local)
    gate_act = jax.nn.silu(out_gate)
    gated = (mixed * gate_act).astype(jnp.bfloat16)
    branch = row_sum(times_trans(gated, wo_t))
    resid = resid_in + branch
    scale_two = row_scale(resid)
    normed2 = row_gather((resid * scale_two * mlp_full).astype(jnp.bfloat16))
    gate_proj = matmul_plain(normed2, wgate_all)
    up_proj = matmul_plain(normed2, wup_all)
    gate_silu = jax.nn.silu(gate_proj)
    hidden = (gate_silu * up_proj).astype(jnp.bfloat16)
    ffn_out = row_sum(times_trans(hidden, wdown_t))
    layer_out = (resid + ffn_out).astype(jnp.bfloat16).reshape(tokens.shape)
    cot_full = row_gather(cot_local)
    d_hidden = matmul_plain(cot_full, wdown_t)
    d_gate = (d_hidden * up_proj * silu_slope(gate_proj)).astype(jnp.bfloat16)
    d_up = (d_hidden * gate_silu).astype(jnp.bfloat16)
    mlp_grads = grad_pack(
        normed2, cot_full, jnp.concatenate([d_gate, d_up, hidden], axis=1), hidden_width
    )
    mlp_red = lax.psum_scatter(mlp_grads, "dp", scatter_dimension=0, tiled=True).astype(jnp.float32)
    d_normed2 = row_sum(times_trans(d_gate, wgate_all) + times_trans(d_up, wup_all))
    grad_mlp = jnp.sum(d_normed2 * resid * scale_two, axis=0)
    inner_two = jnp.mean(d_normed2 * mlp_full * resid, axis=-1, keepdims=True)
    d_resid = (
        cot_local.astype(jnp.float32)
        + d_normed2 * mlp_full * scale_two
        - resid * scale_two**3 * inner_two
    )
    d_branch = row_gather(d_resid.astype(jnp.bfloat16))
    d_gated = matmul_plain(d_branch, wo_t)
    d_mixed = d_gated * gate_act
    d_outgate = (d_gated * mixed * silu_slope(out_gate)).astype(jnp.bfloat16)
    d_query, d_forget, d_value, d_floor = pullback(d_mixed)
    d_query = d_query.astype(jnp.bfloat16)
    d_forget = d_forget.astype(jnp.bfloat16)
    d_value = d_value.astype(jnp.bfloat16)
    attn_grads = grad_pack(
        normed,
        d_branch,
        jnp.concatenate([d_query, d_forget, d_value, d_outgate, gated], axis=1),
        local_width,
    )
    attn_red = ring_sum(attn_grads)
    d_normed = row_sum(
        times_trans(d_query, wq_all)
        + times_trans(d_forget, wf_all)
        + times_trans(d_value, wv_all)
        + times_trans(d_outgate, wg_all)
    )
    grad_attn = jnp.sum(d_normed * resid_in * scale_one, axis=0)
    inner_one = jnp.mean(d_normed * attn_full * resid_in, axis=-1, keepdims=True)
    grad_tokens = (
        d_resid + d_normed * attn_full * scale_one - resid_in * scale_one**3 * inner_one
    ).reshape(tokens.shape)
    floor_vector = lax.dynamic_update_slice(
        jnp.zeros((model_width,), jnp.float32), d_floor.reshape(-1), (part_index * local_width,)
    )
    reduced_small = small_sum(jnp.stack([grad_attn, floor_vector, grad_mlp]))
    return (
        layer_out,
        grad_tokens,
        reduced_small[0],
        reduced_small[1],
        attn_red[:, 0 * local_width : 1 * local_width],
        attn_red[:, 1 * local_width : 2 * local_width],
        attn_red[:, 2 * local_width : 3 * local_width],
        attn_red[:, 3 * local_width : 4 * local_width],
        attn_red[:, 4 * local_width : 5 * local_width].T,
        reduced_small[2],
        mlp_red[:, 0:hidden_width],
        mlp_red[:, hidden_width : 2 * hidden_width],
        mlp_red[:, 2 * hidden_width : 3 * hidden_width].T,
    )


def solution(mesh):
    return jax.shard_map(
        shards,
        mesh=mesh,
        in_specs=(
            P("dp", "tensor", None, None),
            P("dp", None, None),
            P(("dp", "tensor")),
            P(("dp", "tensor")),
            P("dp", "tensor"),
            P("dp", "tensor"),
            P("dp", "tensor"),
            P("dp", "tensor"),
            P("tensor", "dp"),
            P(("dp", "tensor")),
            P("dp", "tensor"),
            P("dp", "tensor"),
            P("tensor", "dp"),
            P("dp", "tensor", None, None),
        ),
        out_specs=(
            P("dp", "tensor", None, None),
            P("dp", "tensor", None, None),
            P(("dp", "tensor")),
            P(("dp", "tensor")),
            P("dp", "tensor"),
            P("dp", "tensor"),
            P("dp", "tensor"),
            P("dp", "tensor"),
            P("tensor", "dp"),
            P(("dp", "tensor")),
            P("dp", "tensor"),
            P("dp", "tensor"),
            P("tensor", "dp"),
        ),
        check_vma=False,
    )
```

```python
import functools

import jax
import jax.numpy as jnp
from jax import lax
from jax.experimental import pallas as pl
from jax.experimental.pallas import tpu as pltpu
from jax.sharding import PartitionSpec as P

HK = 128
HIGHEST = lax.Precision.HIGHEST


epsilon = 1e-06


def row_scale(values):
    return lax.rsqrt(jnp.mean(values * values, axis=-1, keepdims=True) + epsilon)


def silu_slope(values):
    sigmoid_val = jax.nn.sigmoid(values)
    return sigmoid_val * (1.0 + values * (1.0 - sigmoid_val))


def matmul_plain(left, right):
    return jnp.dot(left, right, preferred_element_type=jnp.float32)


def times_trans(left, right):
    return lax.dot_general(
        left, right, (((1,), (1,)), ((), ())), preferred_element_type=jnp.float32
    )


def trans_times(left, right):
    return lax.dot_general(
        left, right, (((0,), (0,)), ((), ())), preferred_element_type=jnp.float32
    )


def pack_kernel(per, first_ref, second_ref, right_ref, out_ref):
    col = pl.program_id(1)

    @pl.when(col < per)
    def _():
        out_ref[...] = jnp.dot(
            first_ref[...].T, right_ref[...], preferred_element_type=jnp.float32
        ).astype(out_ref.dtype)

    @pl.when(col >= per)
    def _():
        out_ref[...] = jnp.dot(
            second_ref[...].T, right_ref[...], preferred_element_type=jnp.float32
        ).astype(out_ref.dtype)


def grad_pack(first, second, right, width):
    depth, rows_out = first.shape
    cols = right.shape[1]
    blocks = cols // width
    per = blocks - 1
    tile = rows_out
    return pl.pallas_call(
        functools.partial(pack_kernel, per),
        grid=(rows_out // tile, blocks),
        in_specs=[
            pl.BlockSpec((depth, tile), lambda i, j: (0, i)),
            pl.BlockSpec((depth, tile), lambda i, j: (0, i)),
            pl.BlockSpec((depth, width), lambda i, j: (0, j)),
        ],
        out_specs=pl.BlockSpec((tile, width), lambda i, j: (i, j)),
        out_shape=jax.ShapeDtypeStruct((rows_out, cols), jnp.bfloat16),
        cost_estimate=pl.CostEstimate(
            flops=2 * depth * rows_out * cols,
            transcendentals=0,
            bytes_accessed=2 * (2 * depth * rows_out + depth * cols + rows_out * cols),
        ),
    )(first, second, right)


def recurrence(query, forget_raw, value, floor_vec, doc_rows):
    length = query.shape[1]
    forget = floor_vec + (1.0 - floor_vec) * jax.nn.sigmoid(forget_raw)
    log_forget = jnp.log(forget)
    keyed = 1.0 - forget
    position = jnp.arange(length)
    same_doc = doc_rows[:, :, None] == doc_rows[:, None, :]
    causal = same_doc & (position[:, None] >= position[None, :])
    starts = jnp.concatenate(
        [jnp.zeros_like(doc_rows[:, :1], dtype=bool), doc_rows[:, 1:] == doc_rows[:, :-1]], axis=1
    )
    summing = (causal & starts[:, None, :]).astype(jnp.float32)
    running = jnp.einsum("rij,rjhk->rihk", summing, log_forget, precision=HIGHEST)
    query_t = query * jnp.exp(running)
    key_t = keyed * jnp.exp(-running)
    scores = jnp.einsum("rihk,rjhk->rhij", query_t, key_t, precision=HIGHEST)
    scores = jnp.where(causal[:, None], scores, 0.0)
    return jnp.einsum("rhij,rjhv->rihv", scores, value, precision=HIGHEST)


ON_CHIP = [(0, 1), (1, 0), (2, 3), (3, 2)]
ACROSS = [(0, 2), (2, 0), (1, 3), (3, 1)]
SLOT_XOR = (0, 2, 1, 3)


def row_gather(values):
    across = lax.ppermute(values, "tensor", ACROSS)
    pair = jnp.stack([values, across])
    other = lax.ppermute(pair, "tensor", ON_CHIP)
    return jnp.concatenate([pair, other]).reshape((-1,) + values.shape[1:])


def row_sum(values):
    blocks = values.reshape((4, -1) + values.shape[1:])
    got = lax.ppermute(blocks[2:], "tensor", ON_CHIP)
    mine = blocks[0] + got[0]
    theirs = blocks[1] + got[1]
    return mine + lax.ppermute(theirs.astype(jnp.bfloat16), "tensor", ACROSS).astype(jnp.float32)


def spread_sum(values, axis, count):
    blocks = values.reshape((count, -1) + values.shape[1:])
    got = lax.all_to_all(blocks, axis, 0, 0, tiled=False)
    return got.astype(jnp.float32).sum(axis=0)


def ring_pairs(step, stride, size):
    pairs = []
    for i in range(32):
        pos = (i // stride) % size
        pairs.append((i, i + (((pos + step) % size) - pos) * stride))
    return pairs


def ring_stage(chunks, pos, stride, size, step):
    pairs = ring_pairs(step, stride, size)

    def pick(k):
        return lax.dynamic_index_in_dim(chunks, (pos - k * step) % size, 0, keepdims=False).astype(
            jnp.float32
        )

    acc = pick(1)
    for k in range(2, size + 1):
        got = lax.ppermute(acc.astype(jnp.bfloat16), "dp", pairs)
        acc = pick(k % size) + got.astype(jnp.float32)
    return acc


def ring_sum(values):
    index = lax.axis_index("dp")
    x_pos, y_pos, z_pos = index % 4, (index // 4) % 2, index // 8
    blocks = values.reshape((4, 2, 4, -1) + values.shape[1:])
    part_rows = blocks.shape[3] // 4
    pieces = []
    for part, (x_first, step) in enumerate(((True, 1), (True, 3), (False, 1), (False, 3))):
        rows = blocks[:, :, :, part * part_rows : (part + 1) * part_rows]
        if x_first:
            once = ring_stage(jnp.moveaxis(rows, 2, 0), x_pos, 1, 4, step)
            twice = ring_stage(once.astype(jnp.bfloat16), z_pos, 8, 4, step)
        else:
            once = ring_stage(rows, z_pos, 8, 4, step)
            twice = ring_stage(jnp.moveaxis(once, 1, 0).astype(jnp.bfloat16), x_pos, 1, 4, step)
        pieces.append(twice)
    both = jnp.concatenate(pieces, axis=1)
    keep = lax.dynamic_index_in_dim(both, y_pos, 0, keepdims=False)
    give = lax.dynamic_index_in_dim(both, 1 - y_pos, 0, keepdims=False)
    pair = [(i, i ^ 4) for i in range(32)]
    return keep + lax.ppermute(give.astype(jnp.bfloat16), "dp", pair).astype(jnp.float32)


def ring_gather(values):
    index = lax.axis_index("dp")
    x_pos, y_pos, z_pos = index % 4, (index // 4) % 2, index // 8
    zero = jnp.zeros((), jnp.int32)
    pair = [(i, i ^ 4) for i in range(32)]
    other = lax.ppermute(values, "dp", pair)
    both = jnp.zeros((2,) + values.shape, values.dtype)
    both = lax.dynamic_update_slice(both, values[None], (y_pos, zero, zero))
    both = lax.dynamic_update_slice(both, other[None], (1 - y_pos, zero, zero))
    part_rows = values.shape[0] // 4
    cols = values.shape[1]
    full = jnp.zeros((4, 2, 4) + values.shape, values.dtype)
    for part, (x_first, step) in enumerate(((True, 1), (True, 3), (False, 1), (False, 3))):
        rows = both[:, part * part_rows : (part + 1) * part_rows]
        row_at = jnp.full((), part * part_rows, jnp.int32)
        if x_first:
            pairs = ring_pairs(step, 1, 4)
            first = jnp.zeros((2, 4, part_rows, cols), values.dtype)
            cur = rows
            first = lax.dynamic_update_slice(first, cur[:, None], (zero, x_pos, zero, zero))
            for k in range(1, 4):
                cur = lax.ppermute(cur, "dp", pairs)
                first = lax.dynamic_update_slice(first, cur[:, None], (zero, (x_pos - k * step) % 4, zero, zero))
            pairs = ring_pairs(step, 8, 4)
            cur = first
            full = lax.dynamic_update_slice(full, cur[None], (z_pos, zero, zero, row_at, zero))
            for k in range(1, 4):
                cur = lax.ppermute(cur, "dp", pairs)
                full = lax.dynamic_update_slice(full, cur[None], ((z_pos - k * step) % 4, zero, zero, row_at, zero))
        else:
            pairs = ring_pairs(step, 8, 4)
            first = jnp.zeros((4, 2, part_rows, cols), values.dtype)
            cur = rows
            first = lax.dynamic_update_slice(first, cur[None], (z_pos, zero, zero, zero))
            for k in range(1, 4):
                cur = lax.ppermute(cur, "dp", pairs)
                first = lax.dynamic_update_slice(first, cur[None], ((z_pos - k * step) % 4, zero, zero, zero))
            pairs = ring_pairs(step, 1, 4)
            cur = first
            full = lax.dynamic_update_slice(full, cur[:, :, None], (zero, zero, x_pos, row_at, zero))
            for k in range(1, 4):
                cur = lax.ppermute(cur, "dp", pairs)
                full = lax.dynamic_update_slice(full, cur[:, :, None], (zero, zero, (x_pos - k * step) % 4, row_at, zero))
    return full.reshape((-1, cols))


def small_gather(vectors):
    count = 128
    spread = jnp.broadcast_to(vectors[None], (count,) + vectors.shape)
    got = lax.all_to_all(spread, ("dp", "tensor"), 0, 0, tiled=False)
    return jnp.swapaxes(got, 0, 1).reshape(vectors.shape[0], -1)


def small_sum(vectors):
    count = 128
    blocks = vectors.reshape(vectors.shape[0], count, -1)
    got = lax.all_to_all(jnp.swapaxes(blocks, 0, 1), ("dp", "tensor"), 0, 0, tiled=False)
    return got.sum(axis=0)


def shards(
    tokens,
    doc_ids,
    attn_gain,
    forget_floor,
    w_query,
    w_forget,
    w_value,
    w_outgate,
    w_output,
    mlp_gain,
    w_gate,
    w_up,
    w_down,
    cotangent,
):
    gains = small_gather(jnp.stack([attn_gain, forget_floor, mlp_gain]))
    attn_full, floor_full, mlp_full = gains[0], gains[1], gains[2]
    part_index = lax.axis_index("tensor")
    local_width = w_query.shape[1]
    local_heads = local_width // HK
    hidden_width = w_gate.shape[1]
    floor_local = lax.dynamic_slice_in_dim(
        floor_full, part_index * local_width, local_width
    ).reshape(local_heads, HK)
    model_width = attn_full.shape[0]
    slot_rows = jnp.bitwise_xor(part_index, jnp.array(SLOT_XOR, jnp.int32))
    doc_all = jnp.take(doc_ids[0], slot_rows, axis=0)
    row_count = doc_all.shape[0]
    resid_in = tokens[0].reshape(-1, model_width).astype(jnp.float32)
    cot_local = cotangent[0].reshape(-1, model_width)
    attn_pack = jnp.concatenate([w_query, w_forget, w_value, w_outgate, w_output.T], axis=1)
    mlp_pack = jnp.concatenate([w_gate, w_up, w_down.T], axis=1)
    attn_all = ring_gather(attn_pack)
    mlp_all = lax.all_gather(mlp_pack, "dp", axis=0, tiled=True)
    wq_all = attn_all[:, 0 * local_width : 1 * local_width]
    wf_all = attn_all[:, 1 * local_width : 2 * local_width]
    wv_all = attn_all[:, 2 * local_width : 3 * local_width]
    wg_all = attn_all[:, 3 * local_width : 4 * local_width]
    wo_t = attn_all[:, 4 * local_width : 5 * local_width]
    wgate_all = mlp_all[:, 0:hidden_width]
    wup_all = mlp_all[:, hidden_width : 2 * hidden_width]
    wdown_t = mlp_all[:, 2 * hidden_width : 3 * hidden_width]
    scale_one = row_scale(resid_in)
    normed = row_gather((resid_in * scale_one * attn_full).astype(jnp.bfloat16))
    query = matmul_plain(normed, wq_all)
    forget_raw = matmul_plain(normed, wf_all)
    value = matmul_plain(normed, wv_all)
    out_gate = matmul_plain(normed, wg_all)

    def mixer(query_in, forget_in, value_in, floor_in):

        def shaped(arr):
            return arr.reshape(row_count, -1, local_heads, HK)

        mixed_rows = recurrence(
            shaped(query_in), shaped(forget_in), shaped(value_in), floor_in, doc_all
        )
        return mixed_rows.reshape(query_in.shape[0], local_width)

    mixed, pullback = jax.vjp(mixer, query, forget_raw, value, floor_local)
    gate_act = jax.nn.silu(out_gate)
    gated = (mixed * gate_act).astype(jnp.bfloat16)
    branch = row_sum(times_trans(gated, wo_t))
    resid = resid_in + branch
    scale_two = row_scale(resid)
    normed2 = row_gather((resid * scale_two * mlp_full).astype(jnp.bfloat16))
    gate_proj = matmul_plain(normed2, wgate_all)
    up_proj = matmul_plain(normed2, wup_all)
    gate_silu = jax.nn.silu(gate_proj)
    hidden = (gate_silu * up_proj).astype(jnp.bfloat16)
    ffn_out = row_sum(times_trans(hidden, wdown_t))
    layer_out = (resid + ffn_out).astype(jnp.bfloat16).reshape(tokens.shape)
    cot_full = row_gather(cot_local)
    d_hidden = matmul_plain(cot_full, wdown_t)
    d_gate = (d_hidden * up_proj * silu_slope(gate_proj)).astype(jnp.bfloat16)
    d_up = (d_hidden * gate_silu).astype(jnp.bfloat16)
    mlp_grads = grad_pack(
        normed2, cot_full, jnp.concatenate([d_gate, d_up, hidden], axis=1), hidden_width
    )
    mlp_red = lax.psum_scatter(mlp_grads, "dp", scatter_dimension=0, tiled=True).astype(jnp.float32)
    d_normed2 = row_sum(times_trans(d_gate, wgate_all) + times_trans(d_up, wup_all))
    grad_mlp = jnp.sum(d_normed2 * resid * scale_two, axis=0)
    inner_two = jnp.mean(d_normed2 * mlp_full * resid, axis=-1, keepdims=True)
    d_resid = (
        cot_local.astype(jnp.float32)
        + d_normed2 * mlp_full * scale_two
        - resid * scale_two**3 * inner_two
    )
    d_branch = row_gather(d_resid.astype(jnp.bfloat16))
    d_gated = matmul_plain(d_branch, wo_t)
    d_mixed = d_gated * gate_act
    d_outgate = (d_gated * mixed * silu_slope(out_gate)).astype(jnp.bfloat16)
    d_query, d_forget, d_value, d_floor = pullback(d_mixed)
    d_query = d_query.astype(jnp.bfloat16)
    d_forget = d_forget.astype(jnp.bfloat16)
    d_value = d_value.astype(jnp.bfloat16)
    attn_grads = grad_pack(
        normed,
        d_branch,
        jnp.concatenate([d_query, d_forget, d_value, d_outgate, gated], axis=1),
        local_width,
    )
    attn_red = ring_sum(attn_grads)
    d_normed = row_sum(
        times_trans(d_query, wq_all)
        + times_trans(d_forget, wf_all)
        + times_trans(d_value, wv_all)
        + times_trans(d_outgate, wg_all)
    )
    grad_attn = jnp.sum(d_normed * resid_in * scale_one, axis=0)
    inner_one = jnp.mean(d_normed * attn_full * resid_in, axis=-1, keepdims=True)
    grad_tokens = (
        d_resid + d_normed * attn_full * scale_one - resid_in * scale_one**3 * inner_one
    ).reshape(tokens.shape)
    floor_vector = lax.dynamic_update_slice(
        jnp.zeros((model_width,), jnp.float32), d_floor.reshape(-1), (part_index * local_width,)
    )
    reduced_small = small_sum(jnp.stack([grad_attn, floor_vector, grad_mlp]))
    return (
        layer_out,
        grad_tokens,
        reduced_small[0],
        reduced_small[1],
        attn_red[:, 0 * local_width : 1 * local_width],
        attn_red[:, 1 * local_width : 2 * local_width],
        attn_red[:, 2 * local_width : 3 * local_width],
        attn_red[:, 3 * local_width : 4 * local_width],
        attn_red[:, 4 * local_width : 5 * local_width].T,
        reduced_small[2],
        mlp_red[:, 0:hidden_width],
        mlp_red[:, hidden_width : 2 * hidden_width],
        mlp_red[:, 2 * hidden_width : 3 * hidden_width].T,
    )


def solution(mesh):
    return jax.shard_map(
        shards,
        mesh=mesh,
        in_specs=(
            P("dp", "tensor", None, None),
            P("dp", None, None),
            P(("dp", "tensor")),
            P(("dp", "tensor")),
            P("dp", "tensor"),
            P("dp", "tensor"),
            P("dp", "tensor"),
            P("dp", "tensor"),
            P("tensor", "dp"),
            P(("dp", "tensor")),
            P("dp", "tensor"),
            P("dp", "tensor"),
            P("tensor", "dp"),
            P("dp", "tensor", None, None),
        ),
        out_specs=(
            P("dp", "tensor", None, None),
            P("dp", "tensor", None, None),
            P(("dp", "tensor")),
            P(("dp", "tensor")),
            P("dp", "tensor"),
            P("dp", "tensor"),
            P("dp", "tensor"),
            P("dp", "tensor"),
            P("tensor", "dp"),
            P(("dp", "tensor")),
            P("dp", "tensor"),
            P("dp", "tensor"),
            P("tensor", "dp"),
        ),
        check_vma=False,
    )
```

```python
import functools

import jax
import jax.numpy as jnp
from jax import lax
from jax.experimental import pallas as pl
from jax.experimental.pallas import tpu as pltpu
from jax.sharding import PartitionSpec as P

HK = 128
HIGHEST = lax.Precision.HIGHEST


epsilon = 1e-06


def row_scale(values):
    return lax.rsqrt(jnp.mean(values * values, axis=-1, keepdims=True) + epsilon)


def silu_slope(values):
    sigmoid_val = jax.nn.sigmoid(values)
    return sigmoid_val * (1.0 + values * (1.0 - sigmoid_val))


def matmul_plain(left, right):
    return jnp.dot(left, right, preferred_element_type=jnp.float32)


def times_trans(left, right):
    return lax.dot_general(
        left, right, (((1,), (1,)), ((), ())), preferred_element_type=jnp.float32
    )


def trans_times(left, right):
    return lax.dot_general(
        left, right, (((0,), (0,)), ((), ())), preferred_element_type=jnp.float32
    )


def pack_kernel(per, first_ref, second_ref, right_ref, out_ref):
    col = pl.program_id(1)

    @pl.when(col < per)
    def _():
        out_ref[...] = jnp.dot(
            first_ref[...].T, right_ref[...], preferred_element_type=jnp.float32
        ).astype(out_ref.dtype)

    @pl.when(col >= per)
    def _():
        out_ref[...] = jnp.dot(
            second_ref[...].T, right_ref[...], preferred_element_type=jnp.float32
        ).astype(out_ref.dtype)


def grad_pack(first, second, right, width):
    depth, rows_out = first.shape
    cols = right.shape[1]
    blocks = cols // width
    per = blocks - 1
    tile = rows_out
    return pl.pallas_call(
        functools.partial(pack_kernel, per),
        grid=(rows_out // tile, blocks),
        in_specs=[
            pl.BlockSpec((depth, tile), lambda i, j: (0, i)),
            pl.BlockSpec((depth, tile), lambda i, j: (0, i)),
            pl.BlockSpec((depth, width), lambda i, j: (0, j)),
        ],
        out_specs=pl.BlockSpec((tile, width), lambda i, j: (i, j)),
        out_shape=jax.ShapeDtypeStruct((rows_out, cols), jnp.bfloat16),
        cost_estimate=pl.CostEstimate(
            flops=2 * depth * rows_out * cols,
            transcendentals=0,
            bytes_accessed=2 * (2 * depth * rows_out + depth * cols + rows_out * cols),
        ),
    )(first, second, right)


def recurrence(query, forget_raw, value, floor_vec, doc_rows):
    length = query.shape[1]
    forget = floor_vec + (1.0 - floor_vec) * jax.nn.sigmoid(forget_raw)
    log_forget = jnp.log(forget)
    keyed = 1.0 - forget
    position = jnp.arange(length)
    same_doc = doc_rows[:, :, None] == doc_rows[:, None, :]
    causal = same_doc & (position[:, None] >= position[None, :])
    starts = jnp.concatenate(
        [jnp.zeros_like(doc_rows[:, :1], dtype=bool), doc_rows[:, 1:] == doc_rows[:, :-1]], axis=1
    )
    summing = (causal & starts[:, None, :]).astype(jnp.float32)
    running = jnp.einsum("rij,rjhk->rihk", summing, log_forget, precision=HIGHEST)
    query_t = query * jnp.exp(running)
    key_t = keyed * jnp.exp(-running)
    scores = jnp.einsum("rihk,rjhk->rhij", query_t, key_t, precision=HIGHEST)
    scores = jnp.where(causal[:, None], scores, 0.0)
    return jnp.einsum("rhij,rjhv->rihv", scores, value, precision=HIGHEST)


ON_CHIP = [(0, 1), (1, 0), (2, 3), (3, 2)]
ACROSS = [(0, 2), (2, 0), (1, 3), (3, 1)]
SLOT_XOR = (0, 2, 1, 3)


def row_gather(values):
    across = lax.ppermute(values, "tensor", ACROSS)
    pair = jnp.stack([values, across])
    other = lax.ppermute(pair, "tensor", ON_CHIP)
    return jnp.concatenate([pair, other]).reshape((-1,) + values.shape[1:])


def row_sum(values):
    blocks = values.reshape((4, -1) + values.shape[1:])
    got = lax.ppermute(blocks[2:], "tensor", ON_CHIP)
    mine = blocks[0] + got[0]
    theirs = blocks[1] + got[1]
    return mine + lax.ppermute(theirs.astype(jnp.bfloat16), "tensor", ACROSS).astype(jnp.float32)


def spread_sum(values, axis, count):
    blocks = values.reshape((count, -1) + values.shape[1:])
    got = lax.all_to_all(blocks, axis, 0, 0, tiled=False)
    return got.astype(jnp.float32).sum(axis=0)


def ring_pairs(step, stride, size):
    pairs = []
    for i in range(32):
        pos = (i // stride) % size
        pairs.append((i, i + (((pos + step) % size) - pos) * stride))
    return pairs


def ring_stage(chunks, pos, stride, size):
    half = chunks.shape[-1] // 2
    result = []
    for step, cols in ((1, slice(0, half)), (size - 1, slice(half, None))):
        own = chunks[..., cols]
        pairs = ring_pairs(step, stride, size)

        def pick(k):
            return lax.dynamic_index_in_dim(own, (pos - k * step) % size, 0, keepdims=False)

        acc = pick(1).astype(jnp.float32)
        for k in range(2, size + 1):
            got = lax.ppermute(acc.astype(jnp.bfloat16), "dp", pairs)
            acc = pick(k % size).astype(jnp.float32) + got.astype(jnp.float32)
        result.append(acc)
    return jnp.concatenate(result, axis=-1)


def ring_sum(values):
    index = lax.axis_index("dp")
    x_pos, y_pos, z_pos = index % 4, (index // 4) % 2, index // 8
    blocks = values.reshape((4, 2, 4, -1) + values.shape[1:])
    along_x = ring_stage(jnp.moveaxis(blocks, 2, 0), x_pos, 1, 4)
    along_z = ring_stage(along_x.astype(jnp.bfloat16), z_pos, 8, 4)
    keep = lax.dynamic_index_in_dim(along_z, y_pos, 0, keepdims=False)
    give = lax.dynamic_index_in_dim(along_z, 1 - y_pos, 0, keepdims=False)
    pair = [(i, i ^ 4) for i in range(32)]
    return keep + lax.ppermute(give.astype(jnp.bfloat16), "dp", pair).astype(jnp.float32)


def ring_gather(values):
    index = lax.axis_index("dp")
    x_pos, y_pos, z_pos = index % 4, (index // 4) % 2, index // 8
    zero = jnp.zeros((), jnp.int32)
    pair = [(i, i ^ 4) for i in range(32)]
    other = lax.ppermute(values, "dp", pair)
    both = jnp.zeros((2,) + values.shape, values.dtype)
    both = lax.dynamic_update_slice(both, values[None], (y_pos, zero, zero))
    both = lax.dynamic_update_slice(both, other[None], (1 - y_pos, zero, zero))
    part_rows = values.shape[0] // 4
    cols = values.shape[1]
    full = jnp.zeros((4, 2, 4) + values.shape, values.dtype)
    for part, (x_first, step) in enumerate(((True, 1), (True, 3), (False, 1), (False, 3))):
        rows = both[:, part * part_rows : (part + 1) * part_rows]
        row_at = jnp.full((), part * part_rows, jnp.int32)
        if x_first:
            pairs = ring_pairs(step, 1, 4)
            first = jnp.zeros((2, 4, part_rows, cols), values.dtype)
            cur = rows
            first = lax.dynamic_update_slice(first, cur[:, None], (zero, x_pos, zero, zero))
            for k in range(1, 4):
                cur = lax.ppermute(cur, "dp", pairs)
                first = lax.dynamic_update_slice(first, cur[:, None], (zero, (x_pos - k * step) % 4, zero, zero))
            pairs = ring_pairs(step, 8, 4)
            cur = first
            full = lax.dynamic_update_slice(full, cur[None], (z_pos, zero, zero, row_at, zero))
            for k in range(1, 4):
                cur = lax.ppermute(cur, "dp", pairs)
                full = lax.dynamic_update_slice(full, cur[None], ((z_pos - k * step) % 4, zero, zero, row_at, zero))
        else:
            pairs = ring_pairs(step, 8, 4)
            first = jnp.zeros((4, 2, part_rows, cols), values.dtype)
            cur = rows
            first = lax.dynamic_update_slice(first, cur[None], (z_pos, zero, zero, zero))
            for k in range(1, 4):
                cur = lax.ppermute(cur, "dp", pairs)
                first = lax.dynamic_update_slice(first, cur[None], ((z_pos - k * step) % 4, zero, zero, zero))
            pairs = ring_pairs(step, 1, 4)
            cur = first
            full = lax.dynamic_update_slice(full, cur[:, :, None], (zero, zero, x_pos, row_at, zero))
            for k in range(1, 4):
                cur = lax.ppermute(cur, "dp", pairs)
                full = lax.dynamic_update_slice(full, cur[:, :, None], (zero, zero, (x_pos - k * step) % 4, row_at, zero))
    return full.reshape((-1, cols))


def small_gather(vectors):
    count = 128
    spread = jnp.broadcast_to(vectors[None], (count,) + vectors.shape)
    got = lax.all_to_all(spread, ("dp", "tensor"), 0, 0, tiled=False)
    return jnp.swapaxes(got, 0, 1).reshape(vectors.shape[0], -1)


def small_sum(vectors):
    count = 128
    blocks = vectors.reshape(vectors.shape[0], count, -1)
    got = lax.all_to_all(jnp.swapaxes(blocks, 0, 1), ("dp", "tensor"), 0, 0, tiled=False)
    return got.sum(axis=0)


def shards(
    tokens,
    doc_ids,
    attn_gain,
    forget_floor,
    w_query,
    w_forget,
    w_value,
    w_outgate,
    w_output,
    mlp_gain,
    w_gate,
    w_up,
    w_down,
    cotangent,
):
    gains = small_gather(jnp.stack([attn_gain, forget_floor, mlp_gain]))
    attn_full, floor_full, mlp_full = gains[0], gains[1], gains[2]
    part_index = lax.axis_index("tensor")
    local_width = w_query.shape[1]
    local_heads = local_width // HK
    hidden_width = w_gate.shape[1]
    floor_local = lax.dynamic_slice_in_dim(
        floor_full, part_index * local_width, local_width
    ).reshape(local_heads, HK)
    model_width = attn_full.shape[0]
    slot_rows = jnp.bitwise_xor(part_index, jnp.array(SLOT_XOR, jnp.int32))
    doc_all = jnp.take(doc_ids[0], slot_rows, axis=0)
    row_count = doc_all.shape[0]
    resid_in = tokens[0].reshape(-1, model_width).astype(jnp.float32)
    cot_local = cotangent[0].reshape(-1, model_width)
    attn_pack = jnp.concatenate([w_query, w_forget, w_value, w_outgate], axis=1)
    mlp_pack = jnp.concatenate([w_gate, w_up, w_down.T], axis=1)
    attn_all = ring_gather(attn_pack)
    mlp_all = lax.all_gather(mlp_pack, "dp", axis=0, tiled=True)
    wq_all = attn_all[:, 0 * local_width : 1 * local_width]
    wf_all = attn_all[:, 1 * local_width : 2 * local_width]
    wv_all = attn_all[:, 2 * local_width : 3 * local_width]
    wg_all = attn_all[:, 3 * local_width : 4 * local_width]
    wo_t = ring_gather(w_output.T)
    wgate_all = mlp_all[:, 0:hidden_width]
    wup_all = mlp_all[:, hidden_width : 2 * hidden_width]
    wdown_t = mlp_all[:, 2 * hidden_width : 3 * hidden_width]
    scale_one = row_scale(resid_in)
    normed = row_gather((resid_in * scale_one * attn_full).astype(jnp.bfloat16))
    query = matmul_plain(normed, wq_all)
    forget_raw = matmul_plain(normed, wf_all)
    value = matmul_plain(normed, wv_all)
    out_gate = matmul_plain(normed, wg_all)

    def mixer(query_in, forget_in, value_in, floor_in):

        def shaped(arr):
            return arr.reshape(row_count, -1, local_heads, HK)

        mixed_rows = recurrence(
            shaped(query_in), shaped(forget_in), shaped(value_in), floor_in, doc_all
        )
        return mixed_rows.reshape(query_in.shape[0], local_width)

    mixed, pullback = jax.vjp(mixer, query, forget_raw, value, floor_local)
    gate_act = jax.nn.silu(out_gate)
    gated = (mixed * gate_act).astype(jnp.bfloat16)
    branch = row_sum(times_trans(gated, wo_t))
    resid = resid_in + branch
    scale_two = row_scale(resid)
    normed2 = row_gather((resid * scale_two * mlp_full).astype(jnp.bfloat16))
    gate_proj = matmul_plain(normed2, wgate_all)
    up_proj = matmul_plain(normed2, wup_all)
    gate_silu = jax.nn.silu(gate_proj)
    hidden = (gate_silu * up_proj).astype(jnp.bfloat16)
    ffn_out = row_sum(times_trans(hidden, wdown_t))
    layer_out = (resid + ffn_out).astype(jnp.bfloat16).reshape(tokens.shape)
    cot_full = row_gather(cot_local)
    d_hidden = matmul_plain(cot_full, wdown_t)
    d_gate = (d_hidden * up_proj * silu_slope(gate_proj)).astype(jnp.bfloat16)
    d_up = (d_hidden * gate_silu).astype(jnp.bfloat16)
    mlp_grads = grad_pack(
        normed2, cot_full, jnp.concatenate([d_gate, d_up, hidden], axis=1), hidden_width
    )
    mlp_red = lax.psum_scatter(mlp_grads, "dp", scatter_dimension=0, tiled=True).astype(jnp.float32)
    d_normed2 = row_sum(times_trans(d_gate, wgate_all) + times_trans(d_up, wup_all))
    grad_mlp = jnp.sum(d_normed2 * resid * scale_two, axis=0)
    inner_two = jnp.mean(d_normed2 * mlp_full * resid, axis=-1, keepdims=True)
    d_resid = (
        cot_local.astype(jnp.float32)
        + d_normed2 * mlp_full * scale_two
        - resid * scale_two**3 * inner_two
    )
    d_branch = row_gather(d_resid.astype(jnp.bfloat16))
    d_gated = matmul_plain(d_branch, wo_t)
    d_mixed = d_gated * gate_act
    d_outgate = (d_gated * mixed * silu_slope(out_gate)).astype(jnp.bfloat16)
    d_query, d_forget, d_value, d_floor = pullback(d_mixed)
    d_query = d_query.astype(jnp.bfloat16)
    d_forget = d_forget.astype(jnp.bfloat16)
    d_value = d_value.astype(jnp.bfloat16)
    attn_grads = grad_pack(
        normed,
        d_branch,
        jnp.concatenate([d_query, d_forget, d_value, d_outgate, gated], axis=1),
        local_width,
    )
    attn_red = ring_sum(attn_grads)
    d_normed = row_sum(
        times_trans(d_query, wq_all)
        + times_trans(d_forget, wf_all)
        + times_trans(d_value, wv_all)
        + times_trans(d_outgate, wg_all)
    )
    grad_attn = jnp.sum(d_normed * resid_in * scale_one, axis=0)
    inner_one = jnp.mean(d_normed * attn_full * resid_in, axis=-1, keepdims=True)
    grad_tokens = (
        d_resid + d_normed * attn_full * scale_one - resid_in * scale_one**3 * inner_one
    ).reshape(tokens.shape)
    floor_vector = lax.dynamic_update_slice(
        jnp.zeros((model_width,), jnp.float32), d_floor.reshape(-1), (part_index * local_width,)
    )
    reduced_small = small_sum(jnp.stack([grad_attn, floor_vector, grad_mlp]))
    return (
        layer_out,
        grad_tokens,
        reduced_small[0],
        reduced_small[1],
        attn_red[:, 0 * local_width : 1 * local_width],
        attn_red[:, 1 * local_width : 2 * local_width],
        attn_red[:, 2 * local_width : 3 * local_width],
        attn_red[:, 3 * local_width : 4 * local_width],
        attn_red[:, 4 * local_width : 5 * local_width].T,
        reduced_small[2],
        mlp_red[:, 0:hidden_width],
        mlp_red[:, hidden_width : 2 * hidden_width],
        mlp_red[:, 2 * hidden_width : 3 * hidden_width].T,
    )


def solution(mesh):
    return jax.shard_map(
        shards,
        mesh=mesh,
        in_specs=(
            P("dp", "tensor", None, None),
            P("dp", None, None),
            P(("dp", "tensor")),
            P(("dp", "tensor")),
            P("dp", "tensor"),
            P("dp", "tensor"),
            P("dp", "tensor"),
            P("dp", "tensor"),
            P("tensor", "dp"),
            P(("dp", "tensor")),
            P("dp", "tensor"),
            P("dp", "tensor"),
            P("tensor", "dp"),
            P("dp", "tensor", None, None),
        ),
        out_specs=(
            P("dp", "tensor", None, None),
            P("dp", "tensor", None, None),
            P(("dp", "tensor")),
            P(("dp", "tensor")),
            P("dp", "tensor"),
            P("dp", "tensor"),
            P("dp", "tensor"),
            P("dp", "tensor"),
            P("tensor", "dp"),
            P(("dp", "tensor")),
            P("dp", "tensor"),
            P("dp", "tensor"),
            P("tensor", "dp"),
        ),
        check_vma=False,
    )
```

```python
import functools

import jax
import jax.numpy as jnp
from jax import lax
from jax.experimental import pallas as pl
from jax.experimental.pallas import tpu as pltpu
from jax.sharding import PartitionSpec as P

HK = 128
HIGHEST = lax.Precision.HIGHEST


epsilon = 1e-06


def row_scale(values):
    return lax.rsqrt(jnp.mean(values * values, axis=-1, keepdims=True) + epsilon)


def silu_slope(values):
    sigmoid_val = jax.nn.sigmoid(values)
    return sigmoid_val * (1.0 + values * (1.0 - sigmoid_val))


def matmul_plain(left, right):
    return jnp.dot(left, right, preferred_element_type=jnp.float32)


def times_trans(left, right):
    return lax.dot_general(
        left, right, (((1,), (1,)), ((), ())), preferred_element_type=jnp.float32
    )


def trans_times(left, right):
    return lax.dot_general(
        left, right, (((0,), (0,)), ((), ())), preferred_element_type=jnp.float32
    )


def pack_kernel(per, first_ref, second_ref, right_ref, out_ref):
    col = pl.program_id(1)

    @pl.when(col < per)
    def _():
        out_ref[...] = jnp.dot(
            first_ref[...].T, right_ref[...], preferred_element_type=jnp.float32
        ).astype(out_ref.dtype)

    @pl.when(col >= per)
    def _():
        out_ref[...] = jnp.dot(
            second_ref[...].T, right_ref[...], preferred_element_type=jnp.float32
        ).astype(out_ref.dtype)


def grad_pack(first, second, right, width):
    depth, rows_out = first.shape
    cols = right.shape[1]
    blocks = cols // width
    per = blocks - 1
    tile = rows_out
    return pl.pallas_call(
        functools.partial(pack_kernel, per),
        grid=(rows_out // tile, blocks),
        in_specs=[
            pl.BlockSpec((depth, tile), lambda i, j: (0, i)),
            pl.BlockSpec((depth, tile), lambda i, j: (0, i)),
            pl.BlockSpec((depth, width), lambda i, j: (0, j)),
        ],
        out_specs=pl.BlockSpec((tile, width), lambda i, j: (i, j)),
        out_shape=jax.ShapeDtypeStruct((rows_out, cols), jnp.bfloat16),
        cost_estimate=pl.CostEstimate(
            flops=2 * depth * rows_out * cols,
            transcendentals=0,
            bytes_accessed=2 * (2 * depth * rows_out + depth * cols + rows_out * cols),
        ),
    )(first, second, right)


def recurrence(query, forget_raw, value, floor_vec, doc_rows):
    length = query.shape[1]
    forget = floor_vec + (1.0 - floor_vec) * jax.nn.sigmoid(forget_raw)
    log_forget = jnp.log(forget)
    keyed = 1.0 - forget
    position = jnp.arange(length)
    same_doc = doc_rows[:, :, None] == doc_rows[:, None, :]
    causal = same_doc & (position[:, None] >= position[None, :])
    starts = jnp.concatenate(
        [jnp.zeros_like(doc_rows[:, :1], dtype=bool), doc_rows[:, 1:] == doc_rows[:, :-1]], axis=1
    )
    summing = (causal & starts[:, None, :]).astype(jnp.float32)
    running = jnp.einsum("rij,rjhk->rihk", summing, log_forget, precision=HIGHEST)
    query_t = query * jnp.exp(running)
    key_t = keyed * jnp.exp(-running)
    scores = jnp.einsum("rihk,rjhk->rhij", query_t, key_t, precision=HIGHEST)
    scores = jnp.where(causal[:, None], scores, 0.0)
    return jnp.einsum("rhij,rjhv->rihv", scores, value, precision=HIGHEST)


ON_CHIP = [(0, 1), (1, 0), (2, 3), (3, 2)]
ACROSS = [(0, 2), (2, 0), (1, 3), (3, 1)]
SLOT_XOR = (0, 2, 1, 3)


def row_gather(values):
    across = lax.ppermute(values, "tensor", ACROSS)
    pair = jnp.stack([values, across])
    other = lax.ppermute(pair, "tensor", ON_CHIP)
    return jnp.concatenate([pair, other]).reshape((-1,) + values.shape[1:])


def row_sum(values):
    blocks = values.reshape((4, -1) + values.shape[1:])
    got = lax.ppermute(blocks[2:], "tensor", ON_CHIP)
    mine = blocks[0] + got[0]
    theirs = blocks[1] + got[1]
    return mine + lax.ppermute(theirs.astype(jnp.bfloat16), "tensor", ACROSS).astype(jnp.float32)


def spread_sum(values, axis, count):
    blocks = values.reshape((count, -1) + values.shape[1:])
    got = lax.all_to_all(blocks, axis, 0, 0, tiled=False)
    return got.astype(jnp.float32).sum(axis=0)


def ring_pairs(step, stride, size):
    pairs = []
    for i in range(32):
        pos = (i // stride) % size
        pairs.append((i, i + (((pos + step) % size) - pos) * stride))
    return pairs


def ring_stage(chunks, axis, pos, stride, size, step):
    pairs = ring_pairs(step, stride, size)

    def pick(k):
        return lax.dynamic_index_in_dim(chunks, (pos - k * step) % size, axis, keepdims=False).astype(
            jnp.float32
        )

    acc = pick(1)
    for k in range(2, size + 1):
        got = lax.ppermute(acc.astype(jnp.bfloat16), "dp", pairs)
        acc = pick(k % size) + got.astype(jnp.float32)
    return acc


def ring_sum(values):
    index = lax.axis_index("dp")
    x_pos, y_pos, z_pos = index % 4, (index // 4) % 2, index // 8
    blocks = values.reshape((4, 2, 4, -1) + values.shape[1:])
    half = blocks.shape[3] // 2
    result = []
    for step, rows in ((1, slice(0, half)), (3, slice(half, None))):
        part = blocks[:, :, :, rows]
        along_x = ring_stage(part, 2, x_pos, 1, 4, step)
        result.append(ring_stage(along_x.astype(jnp.bfloat16), 0, z_pos, 8, 4, step))
    along_z = jnp.concatenate(result, axis=1)
    keep = lax.dynamic_index_in_dim(along_z, y_pos, 0, keepdims=False)
    give = lax.dynamic_index_in_dim(along_z, 1 - y_pos, 0, keepdims=False)
    pair = [(i, i ^ 4) for i in range(32)]
    return keep + lax.ppermute(give.astype(jnp.bfloat16), "dp", pair).astype(jnp.float32)


def ring_gather(values):
    index = lax.axis_index("dp")
    x_pos, y_pos, z_pos = index % 4, (index // 4) % 2, index // 8
    zero = jnp.zeros((), jnp.int32)
    pair = [(i, i ^ 4) for i in range(32)]
    other = lax.ppermute(values, "dp", pair)
    both = jnp.zeros((2,) + values.shape, values.dtype)
    both = lax.dynamic_update_slice(both, values[None], (y_pos, zero, zero))
    both = lax.dynamic_update_slice(both, other[None], (1 - y_pos, zero, zero))
    part_rows = values.shape[0] // 4
    cols = values.shape[1]
    full = jnp.zeros((4, 2, 4) + values.shape, values.dtype)
    for part, (x_first, step) in enumerate(((True, 1), (True, 3), (False, 1), (False, 3))):
        rows = both[:, part * part_rows : (part + 1) * part_rows]
        row_at = jnp.full((), part * part_rows, jnp.int32)
        if x_first:
            pairs = ring_pairs(step, 1, 4)
            first = jnp.zeros((2, 4, part_rows, cols), values.dtype)
            cur = rows
            first = lax.dynamic_update_slice(first, cur[:, None], (zero, x_pos, zero, zero))
            for k in range(1, 4):
                cur = lax.ppermute(cur, "dp", pairs)
                first = lax.dynamic_update_slice(first, cur[:, None], (zero, (x_pos - k * step) % 4, zero, zero))
            pairs = ring_pairs(step, 8, 4)
            cur = first
            full = lax.dynamic_update_slice(full, cur[None], (z_pos, zero, zero, row_at, zero))
            for k in range(1, 4):
                cur = lax.ppermute(cur, "dp", pairs)
                full = lax.dynamic_update_slice(full, cur[None], ((z_pos - k * step) % 4, zero, zero, row_at, zero))
        else:
            pairs = ring_pairs(step, 8, 4)
            first = jnp.zeros((4, 2, part_rows, cols), values.dtype)
            cur = rows
            first = lax.dynamic_update_slice(first, cur[None], (z_pos, zero, zero, zero))
            for k in range(1, 4):
                cur = lax.ppermute(cur, "dp", pairs)
                first = lax.dynamic_update_slice(first, cur[None], ((z_pos - k * step) % 4, zero, zero, zero))
            pairs = ring_pairs(step, 1, 4)
            cur = first
            full = lax.dynamic_update_slice(full, cur[:, :, None], (zero, zero, x_pos, row_at, zero))
            for k in range(1, 4):
                cur = lax.ppermute(cur, "dp", pairs)
                full = lax.dynamic_update_slice(full, cur[:, :, None], (zero, zero, (x_pos - k * step) % 4, row_at, zero))
    return full.reshape((-1, cols))


def small_gather(vectors):
    count = 128
    spread = jnp.broadcast_to(vectors[None], (count,) + vectors.shape)
    got = lax.all_to_all(spread, ("dp", "tensor"), 0, 0, tiled=False)
    return jnp.swapaxes(got, 0, 1).reshape(vectors.shape[0], -1)


def small_sum(vectors):
    count = 128
    blocks = vectors.reshape(vectors.shape[0], count, -1)
    got = lax.all_to_all(jnp.swapaxes(blocks, 0, 1), ("dp", "tensor"), 0, 0, tiled=False)
    return got.sum(axis=0)


def shards(
    tokens,
    doc_ids,
    attn_gain,
    forget_floor,
    w_query,
    w_forget,
    w_value,
    w_outgate,
    w_output,
    mlp_gain,
    w_gate,
    w_up,
    w_down,
    cotangent,
):
    gains = small_gather(jnp.stack([attn_gain, forget_floor, mlp_gain]))
    attn_full, floor_full, mlp_full = gains[0], gains[1], gains[2]
    part_index = lax.axis_index("tensor")
    local_width = w_query.shape[1]
    local_heads = local_width // HK
    hidden_width = w_gate.shape[1]
    floor_local = lax.dynamic_slice_in_dim(
        floor_full, part_index * local_width, local_width
    ).reshape(local_heads, HK)
    model_width = attn_full.shape[0]
    slot_rows = jnp.bitwise_xor(part_index, jnp.array(SLOT_XOR, jnp.int32))
    doc_all = jnp.take(doc_ids[0], slot_rows, axis=0)
    row_count = doc_all.shape[0]
    resid_in = tokens[0].reshape(-1, model_width).astype(jnp.float32)
    cot_local = cotangent[0].reshape(-1, model_width)
    attn_pack = jnp.concatenate([w_query, w_forget, w_value, w_outgate, w_output.T], axis=1)
    mlp_pack = jnp.concatenate([w_gate, w_up, w_down.T], axis=1)
    attn_all = ring_gather(attn_pack)
    mlp_all = lax.all_gather(mlp_pack, "dp", axis=0, tiled=True)
    wq_all = attn_all[:, 0 * local_width : 1 * local_width]
    wf_all = attn_all[:, 1 * local_width : 2 * local_width]
    wv_all = attn_all[:, 2 * local_width : 3 * local_width]
    wg_all = attn_all[:, 3 * local_width : 4 * local_width]
    wo_t = attn_all[:, 4 * local_width : 5 * local_width]
    wgate_all = mlp_all[:, 0:hidden_width]
    wup_all = mlp_all[:, hidden_width : 2 * hidden_width]
    wdown_t = mlp_all[:, 2 * hidden_width : 3 * hidden_width]
    scale_one = row_scale(resid_in)
    normed = row_gather((resid_in * scale_one * attn_full).astype(jnp.bfloat16))
    query = matmul_plain(normed, wq_all)
    forget_raw = matmul_plain(normed, wf_all)
    value = matmul_plain(normed, wv_all)
    out_gate = matmul_plain(normed, wg_all)

    def mixer(query_in, forget_in, value_in, floor_in):

        def shaped(arr):
            return arr.reshape(row_count, -1, local_heads, HK)

        mixed_rows = recurrence(
            shaped(query_in), shaped(forget_in), shaped(value_in), floor_in, doc_all
        )
        return mixed_rows.reshape(query_in.shape[0], local_width)

    mixed, pullback = jax.vjp(mixer, query, forget_raw, value, floor_local)
    gate_act = jax.nn.silu(out_gate)
    gated = (mixed * gate_act).astype(jnp.bfloat16)
    branch = row_sum(times_trans(gated, wo_t))
    resid = resid_in + branch
    scale_two = row_scale(resid)
    normed2 = row_gather((resid * scale_two * mlp_full).astype(jnp.bfloat16))
    gate_proj = matmul_plain(normed2, wgate_all)
    up_proj = matmul_plain(normed2, wup_all)
    gate_silu = jax.nn.silu(gate_proj)
    hidden = (gate_silu * up_proj).astype(jnp.bfloat16)
    ffn_out = row_sum(times_trans(hidden, wdown_t))
    layer_out = (resid + ffn_out).astype(jnp.bfloat16).reshape(tokens.shape)
    cot_full = row_gather(cot_local)
    d_hidden = matmul_plain(cot_full, wdown_t)
    d_gate = (d_hidden * up_proj * silu_slope(gate_proj)).astype(jnp.bfloat16)
    d_up = (d_hidden * gate_silu).astype(jnp.bfloat16)
    mlp_grads = grad_pack(
        normed2, cot_full, jnp.concatenate([d_gate, d_up, hidden], axis=1), hidden_width
    )
    mlp_red = lax.psum_scatter(mlp_grads, "dp", scatter_dimension=0, tiled=True).astype(jnp.float32)
    d_normed2 = row_sum(times_trans(d_gate, wgate_all) + times_trans(d_up, wup_all))
    grad_mlp = jnp.sum(d_normed2 * resid * scale_two, axis=0)
    inner_two = jnp.mean(d_normed2 * mlp_full * resid, axis=-1, keepdims=True)
    d_resid = (
        cot_local.astype(jnp.float32)
        + d_normed2 * mlp_full * scale_two
        - resid * scale_two**3 * inner_two
    )
    d_branch = row_gather(d_resid.astype(jnp.bfloat16))
    d_gated = matmul_plain(d_branch, wo_t)
    d_mixed = d_gated * gate_act
    d_outgate = (d_gated * mixed * silu_slope(out_gate)).astype(jnp.bfloat16)
    d_query, d_forget, d_value, d_floor = pullback(d_mixed)
    d_query = d_query.astype(jnp.bfloat16)
    d_forget = d_forget.astype(jnp.bfloat16)
    d_value = d_value.astype(jnp.bfloat16)
    attn_grads = grad_pack(
        normed,
        d_branch,
        jnp.concatenate([d_query, d_forget, d_value, d_outgate, gated], axis=1),
        local_width,
    )
    attn_red = ring_sum(attn_grads)
    d_normed = row_sum(
        times_trans(d_query, wq_all)
        + times_trans(d_forget, wf_all)
        + times_trans(d_value, wv_all)
        + times_trans(d_outgate, wg_all)
    )
    grad_attn = jnp.sum(d_normed * resid_in * scale_one, axis=0)
    inner_one = jnp.mean(d_normed * attn_full * resid_in, axis=-1, keepdims=True)
    grad_tokens = (
        d_resid + d_normed * attn_full * scale_one - resid_in * scale_one**3 * inner_one
    ).reshape(tokens.shape)
    floor_vector = lax.dynamic_update_slice(
        jnp.zeros((model_width,), jnp.float32), d_floor.reshape(-1), (part_index * local_width,)
    )
    reduced_small = small_sum(jnp.stack([grad_attn, floor_vector, grad_mlp]))
    return (
        layer_out,
        grad_tokens,
        reduced_small[0],
        reduced_small[1],
        attn_red[:, 0 * local_width : 1 * local_width],
        attn_red[:, 1 * local_width : 2 * local_width],
        attn_red[:, 2 * local_width : 3 * local_width],
        attn_red[:, 3 * local_width : 4 * local_width],
        attn_red[:, 4 * local_width : 5 * local_width].T,
        reduced_small[2],
        mlp_red[:, 0:hidden_width],
        mlp_red[:, hidden_width : 2 * hidden_width],
        mlp_red[:, 2 * hidden_width : 3 * hidden_width].T,
    )


def solution(mesh):
    return jax.shard_map(
        shards,
        mesh=mesh,
        in_specs=(
            P("dp", "tensor", None, None),
            P("dp", None, None),
            P(("dp", "tensor")),
            P(("dp", "tensor")),
            P("dp", "tensor"),
            P("dp", "tensor"),
            P("dp", "tensor"),
            P("dp", "tensor"),
            P("tensor", "dp"),
            P(("dp", "tensor")),
            P("dp", "tensor"),
            P("dp", "tensor"),
            P("tensor", "dp"),
            P("dp", "tensor", None, None),
        ),
        out_specs=(
            P("dp", "tensor", None, None),
            P("dp", "tensor", None, None),
            P(("dp", "tensor")),
            P(("dp", "tensor")),
            P("dp", "tensor"),
            P("dp", "tensor"),
            P("dp", "tensor"),
            P("dp", "tensor"),
            P("tensor", "dp"),
            P(("dp", "tensor")),
            P("dp", "tensor"),
            P("dp", "tensor"),
            P("tensor", "dp"),
        ),
        check_vma=False,
    )
```

```python
import functools

import jax
import jax.numpy as jnp
from jax import lax
from jax.experimental import pallas as pl
from jax.experimental.pallas import tpu as pltpu
from jax.sharding import PartitionSpec as P

HK = 128
HIGHEST = lax.Precision.HIGHEST


epsilon = 1e-06


def row_scale(values):
    return lax.rsqrt(jnp.mean(values * values, axis=-1, keepdims=True) + epsilon)


def silu_slope(values):
    sigmoid_val = jax.nn.sigmoid(values)
    return sigmoid_val * (1.0 + values * (1.0 - sigmoid_val))


def matmul_plain(left, right):
    return jnp.dot(left, right, preferred_element_type=jnp.float32)


def times_trans(left, right):
    return lax.dot_general(
        left, right, (((1,), (1,)), ((), ())), preferred_element_type=jnp.float32
    )


def trans_times(left, right):
    return lax.dot_general(
        left, right, (((0,), (0,)), ((), ())), preferred_element_type=jnp.float32
    )


def pack_kernel(per, first_ref, second_ref, right_ref, out_ref):
    col = pl.program_id(1)

    @pl.when(col < per)
    def _():
        out_ref[...] = jnp.dot(
            first_ref[...].T, right_ref[...], preferred_element_type=jnp.float32
        ).astype(out_ref.dtype)

    @pl.when(col >= per)
    def _():
        out_ref[...] = jnp.dot(
            second_ref[...].T, right_ref[...], preferred_element_type=jnp.float32
        ).astype(out_ref.dtype)


def grad_pack(first, second, right, width):
    depth, rows_out = first.shape
    cols = right.shape[1]
    blocks = cols // width
    per = blocks - 1
    tile = rows_out
    return pl.pallas_call(
        functools.partial(pack_kernel, per),
        grid=(rows_out // tile, blocks),
        in_specs=[
            pl.BlockSpec((depth, tile), lambda i, j: (0, i)),
            pl.BlockSpec((depth, tile), lambda i, j: (0, i)),
            pl.BlockSpec((depth, width), lambda i, j: (0, j)),
        ],
        out_specs=pl.BlockSpec((tile, width), lambda i, j: (i, j)),
        out_shape=jax.ShapeDtypeStruct((rows_out, cols), jnp.bfloat16),
        cost_estimate=pl.CostEstimate(
            flops=2 * depth * rows_out * cols,
            transcendentals=0,
            bytes_accessed=2 * (2 * depth * rows_out + depth * cols + rows_out * cols),
        ),
    )(first, second, right)


def recurrence(query, forget_raw, value, floor_vec, doc_rows):
    length = query.shape[1]
    forget = floor_vec + (1.0 - floor_vec) * jax.nn.sigmoid(forget_raw)
    log_forget = jnp.log(forget)
    keyed = 1.0 - forget
    position = jnp.arange(length)
    same_doc = doc_rows[:, :, None] == doc_rows[:, None, :]
    causal = same_doc & (position[:, None] >= position[None, :])
    starts = jnp.concatenate(
        [jnp.zeros_like(doc_rows[:, :1], dtype=bool), doc_rows[:, 1:] == doc_rows[:, :-1]], axis=1
    )
    summing = (causal & starts[:, None, :]).astype(jnp.float32)
    running = jnp.einsum("rij,rjhk->rihk", summing, log_forget, precision=HIGHEST)
    query_t = query * jnp.exp(running)
    key_t = keyed * jnp.exp(-running)
    scores = jnp.einsum("rihk,rjhk->rhij", query_t, key_t, precision=HIGHEST)
    scores = jnp.where(causal[:, None], scores, 0.0)
    return jnp.einsum("rhij,rjhv->rihv", scores, value, precision=HIGHEST)


ON_CHIP = [(0, 1), (1, 0), (2, 3), (3, 2)]
ACROSS = [(0, 2), (2, 0), (1, 3), (3, 1)]
SLOT_XOR = (0, 2, 1, 3)


def row_gather(values):
    across = lax.ppermute(values, "tensor", ACROSS)
    pair = jnp.stack([values, across])
    other = lax.ppermute(pair, "tensor", ON_CHIP)
    return jnp.concatenate([pair, other]).reshape((-1,) + values.shape[1:])


def row_sum(values):
    blocks = values.reshape((4, -1) + values.shape[1:])
    got = lax.ppermute(blocks[2:], "tensor", ON_CHIP)
    mine = blocks[0] + got[0]
    theirs = blocks[1] + got[1]
    return mine + lax.ppermute(theirs.astype(jnp.bfloat16), "tensor", ACROSS).astype(jnp.float32)


def spread_sum(values, axis, count):
    blocks = values.reshape((count, -1) + values.shape[1:])
    got = lax.all_to_all(blocks, axis, 0, 0, tiled=False)
    return got.astype(jnp.float32).sum(axis=0)


def ring_pairs(step, stride, size):
    pairs = []
    for i in range(32):
        pos = (i // stride) % size
        pairs.append((i, i + (((pos + step) % size) - pos) * stride))
    return pairs


def ring_stage(chunks, axis, pos, stride, size, step):
    pairs = ring_pairs(step, stride, size)

    def pick(k):
        return lax.dynamic_index_in_dim(chunks, (pos - k * step) % size, axis, keepdims=False).astype(
            jnp.float32
        )

    acc = pick(1)
    for k in range(2, size + 1):
        got = lax.ppermute(acc.astype(jnp.bfloat16), "dp", pairs)
        acc = pick(k % size) + got.astype(jnp.float32)
    return acc


def ring_sum(values):
    index = lax.axis_index("dp")
    x_pos, y_pos, z_pos = index % 4, (index // 4) % 2, index // 8
    blocks = values.reshape((4, 2, 4, -1) + values.shape[1:])
    half = blocks.shape[3] // 2
    result = []
    for step, rows in ((1, slice(0, half)), (3, slice(half, None))):
        part = blocks[:, :, :, rows]
        along_z = ring_stage(part, 0, z_pos, 8, 4, step)
        result.append(ring_stage(along_z.astype(jnp.bfloat16), 1, x_pos, 1, 4, step))
    along_z = jnp.concatenate(result, axis=1)
    keep = lax.dynamic_index_in_dim(along_z, y_pos, 0, keepdims=False)
    give = lax.dynamic_index_in_dim(along_z, 1 - y_pos, 0, keepdims=False)
    pair = [(i, i ^ 4) for i in range(32)]
    return keep + lax.ppermute(give.astype(jnp.bfloat16), "dp", pair).astype(jnp.float32)


def ring_gather(values):
    index = lax.axis_index("dp")
    x_pos, y_pos, z_pos = index % 4, (index // 4) % 2, index // 8
    zero = jnp.zeros((), jnp.int32)
    pair = [(i, i ^ 4) for i in range(32)]
    other = lax.ppermute(values, "dp", pair)
    both = jnp.zeros((2,) + values.shape, values.dtype)
    both = lax.dynamic_update_slice(both, values[None], (y_pos, zero, zero))
    both = lax.dynamic_update_slice(both, other[None], (1 - y_pos, zero, zero))
    part_rows = values.shape[0] // 4
    cols = values.shape[1]
    full = jnp.zeros((4, 2, 4) + values.shape, values.dtype)
    for part, (x_first, step) in enumerate(((True, 1), (True, 3), (False, 1), (False, 3))):
        rows = both[:, part * part_rows : (part + 1) * part_rows]
        row_at = jnp.full((), part * part_rows, jnp.int32)
        if x_first:
            pairs = ring_pairs(step, 1, 4)
            first = jnp.zeros((2, 4, part_rows, cols), values.dtype)
            cur = rows
            first = lax.dynamic_update_slice(first, cur[:, None], (zero, x_pos, zero, zero))
            for k in range(1, 4):
                cur = lax.ppermute(cur, "dp", pairs)
                first = lax.dynamic_update_slice(first, cur[:, None], (zero, (x_pos - k * step) % 4, zero, zero))
            pairs = ring_pairs(step, 8, 4)
            cur = first
            full = lax.dynamic_update_slice(full, cur[None], (z_pos, zero, zero, row_at, zero))
            for k in range(1, 4):
                cur = lax.ppermute(cur, "dp", pairs)
                full = lax.dynamic_update_slice(full, cur[None], ((z_pos - k * step) % 4, zero, zero, row_at, zero))
        else:
            pairs = ring_pairs(step, 8, 4)
            first = jnp.zeros((4, 2, part_rows, cols), values.dtype)
            cur = rows
            first = lax.dynamic_update_slice(first, cur[None], (z_pos, zero, zero, zero))
            for k in range(1, 4):
                cur = lax.ppermute(cur, "dp", pairs)
                first = lax.dynamic_update_slice(first, cur[None], ((z_pos - k * step) % 4, zero, zero, zero))
            pairs = ring_pairs(step, 1, 4)
            cur = first
            full = lax.dynamic_update_slice(full, cur[:, :, None], (zero, zero, x_pos, row_at, zero))
            for k in range(1, 4):
                cur = lax.ppermute(cur, "dp", pairs)
                full = lax.dynamic_update_slice(full, cur[:, :, None], (zero, zero, (x_pos - k * step) % 4, row_at, zero))
    return full.reshape((-1, cols))


def small_gather(vectors):
    count = 128
    spread = jnp.broadcast_to(vectors[None], (count,) + vectors.shape)
    got = lax.all_to_all(spread, ("dp", "tensor"), 0, 0, tiled=False)
    return jnp.swapaxes(got, 0, 1).reshape(vectors.shape[0], -1)


def small_sum(vectors):
    count = 128
    blocks = vectors.reshape(vectors.shape[0], count, -1)
    got = lax.all_to_all(jnp.swapaxes(blocks, 0, 1), ("dp", "tensor"), 0, 0, tiled=False)
    return got.sum(axis=0)


def shards(
    tokens,
    doc_ids,
    attn_gain,
    forget_floor,
    w_query,
    w_forget,
    w_value,
    w_outgate,
    w_output,
    mlp_gain,
    w_gate,
    w_up,
    w_down,
    cotangent,
):
    gains = small_gather(jnp.stack([attn_gain, forget_floor, mlp_gain]))
    attn_full, floor_full, mlp_full = gains[0], gains[1], gains[2]
    part_index = lax.axis_index("tensor")
    local_width = w_query.shape[1]
    local_heads = local_width // HK
    hidden_width = w_gate.shape[1]
    floor_local = lax.dynamic_slice_in_dim(
        floor_full, part_index * local_width, local_width
    ).reshape(local_heads, HK)
    model_width = attn_full.shape[0]
    slot_rows = jnp.bitwise_xor(part_index, jnp.array(SLOT_XOR, jnp.int32))
    doc_all = jnp.take(doc_ids[0], slot_rows, axis=0)
    row_count = doc_all.shape[0]
    resid_in = tokens[0].reshape(-1, model_width).astype(jnp.float32)
    cot_local = cotangent[0].reshape(-1, model_width)
    attn_pack = jnp.concatenate([w_query, w_forget, w_value, w_outgate, w_output.T], axis=1)
    mlp_pack = jnp.concatenate([w_gate, w_up, w_down.T], axis=1)
    attn_all = ring_gather(attn_pack)
    mlp_all = lax.all_gather(mlp_pack, "dp", axis=0, tiled=True)
    wq_all = attn_all[:, 0 * local_width : 1 * local_width]
    wf_all = attn_all[:, 1 * local_width : 2 * local_width]
    wv_all = attn_all[:, 2 * local_width : 3 * local_width]
    wg_all = attn_all[:, 3 * local_width : 4 * local_width]
    wo_t = attn_all[:, 4 * local_width : 5 * local_width]
    wgate_all = mlp_all[:, 0:hidden_width]
    wup_all = mlp_all[:, hidden_width : 2 * hidden_width]
    wdown_t = mlp_all[:, 2 * hidden_width : 3 * hidden_width]
    scale_one = row_scale(resid_in)
    normed = row_gather((resid_in * scale_one * attn_full).astype(jnp.bfloat16))
    query = matmul_plain(normed, wq_all)
    forget_raw = matmul_plain(normed, wf_all)
    value = matmul_plain(normed, wv_all)
    out_gate = matmul_plain(normed, wg_all)

    def mixer(query_in, forget_in, value_in, floor_in):

        def shaped(arr):
            return arr.reshape(row_count, -1, local_heads, HK)

        mixed_rows = recurrence(
            shaped(query_in), shaped(forget_in), shaped(value_in), floor_in, doc_all
        )
        return mixed_rows.reshape(query_in.shape[0], local_width)

    mixed, pullback = jax.vjp(mixer, query, forget_raw, value, floor_local)
    gate_act = jax.nn.silu(out_gate)
    gated = (mixed * gate_act).astype(jnp.bfloat16)
    branch = row_sum(times_trans(gated, wo_t))
    resid = resid_in + branch
    scale_two = row_scale(resid)
    normed2 = row_gather((resid * scale_two * mlp_full).astype(jnp.bfloat16))
    gate_proj = matmul_plain(normed2, wgate_all)
    up_proj = matmul_plain(normed2, wup_all)
    gate_silu = jax.nn.silu(gate_proj)
    hidden = (gate_silu * up_proj).astype(jnp.bfloat16)
    ffn_out = row_sum(times_trans(hidden, wdown_t))
    layer_out = (resid + ffn_out).astype(jnp.bfloat16).reshape(tokens.shape)
    cot_full = row_gather(cot_local)
    d_hidden = matmul_plain(cot_full, wdown_t)
    d_gate = (d_hidden * up_proj * silu_slope(gate_proj)).astype(jnp.bfloat16)
    d_up = (d_hidden * gate_silu).astype(jnp.bfloat16)
    mlp_grads = grad_pack(
        normed2, cot_full, jnp.concatenate([d_gate, d_up, hidden], axis=1), hidden_width
    )
    mlp_red = lax.psum_scatter(mlp_grads, "dp", scatter_dimension=0, tiled=True).astype(jnp.float32)
    d_normed2 = row_sum(times_trans(d_gate, wgate_all) + times_trans(d_up, wup_all))
    grad_mlp = jnp.sum(d_normed2 * resid * scale_two, axis=0)
    inner_two = jnp.mean(d_normed2 * mlp_full * resid, axis=-1, keepdims=True)
    d_resid = (
        cot_local.astype(jnp.float32)
        + d_normed2 * mlp_full * scale_two
        - resid * scale_two**3 * inner_two
    )
    d_branch = row_gather(d_resid.astype(jnp.bfloat16))
    d_gated = matmul_plain(d_branch, wo_t)
    d_mixed = d_gated * gate_act
    d_outgate = (d_gated * mixed * silu_slope(out_gate)).astype(jnp.bfloat16)
    d_query, d_forget, d_value, d_floor = pullback(d_mixed)
    d_query = d_query.astype(jnp.bfloat16)
    d_forget = d_forget.astype(jnp.bfloat16)
    d_value = d_value.astype(jnp.bfloat16)
    attn_grads = grad_pack(
        normed,
        d_branch,
        jnp.concatenate([d_query, d_forget, d_value, d_outgate, gated], axis=1),
        local_width,
    )
    attn_red = ring_sum(attn_grads)
    d_normed = row_sum(
        times_trans(d_query, wq_all)
        + times_trans(d_forget, wf_all)
        + times_trans(d_value, wv_all)
        + times_trans(d_outgate, wg_all)
    )
    grad_attn = jnp.sum(d_normed * resid_in * scale_one, axis=0)
    inner_one = jnp.mean(d_normed * attn_full * resid_in, axis=-1, keepdims=True)
    grad_tokens = (
        d_resid + d_normed * attn_full * scale_one - resid_in * scale_one**3 * inner_one
    ).reshape(tokens.shape)
    floor_vector = lax.dynamic_update_slice(
        jnp.zeros((model_width,), jnp.float32), d_floor.reshape(-1), (part_index * local_width,)
    )
    reduced_small = small_sum(jnp.stack([grad_attn, floor_vector, grad_mlp]))
    return (
        layer_out,
        grad_tokens,
        reduced_small[0],
        reduced_small[1],
        attn_red[:, 0 * local_width : 1 * local_width],
        attn_red[:, 1 * local_width : 2 * local_width],
        attn_red[:, 2 * local_width : 3 * local_width],
        attn_red[:, 3 * local_width : 4 * local_width],
        attn_red[:, 4 * local_width : 5 * local_width].T,
        reduced_small[2],
        mlp_red[:, 0:hidden_width],
        mlp_red[:, hidden_width : 2 * hidden_width],
        mlp_red[:, 2 * hidden_width : 3 * hidden_width].T,
    )


def solution(mesh):
    return jax.shard_map(
        shards,
        mesh=mesh,
        in_specs=(
            P("dp", "tensor", None, None),
            P("dp", None, None),
            P(("dp", "tensor")),
            P(("dp", "tensor")),
            P("dp", "tensor"),
            P("dp", "tensor"),
            P("dp", "tensor"),
            P("dp", "tensor"),
            P("tensor", "dp"),
            P(("dp", "tensor")),
            P("dp", "tensor"),
            P("dp", "tensor"),
            P("tensor", "dp"),
            P("dp", "tensor", None, None),
        ),
        out_specs=(
            P("dp", "tensor", None, None),
            P("dp", "tensor", None, None),
            P(("dp", "tensor")),
            P(("dp", "tensor")),
            P("dp", "tensor"),
            P("dp", "tensor"),
            P("dp", "tensor"),
            P("dp", "tensor"),
            P("tensor", "dp"),
            P(("dp", "tensor")),
            P("dp", "tensor"),
            P("dp", "tensor"),
            P("tensor", "dp"),
        ),
        check_vma=False,
    )
```

```python
import functools

import jax
import jax.numpy as jnp
from jax import lax
from jax.experimental import pallas as pl
from jax.experimental.pallas import tpu as pltpu
from jax.sharding import PartitionSpec as P

HK = 128
HIGHEST = lax.Precision.HIGHEST


epsilon = 1e-06


def row_scale(values):
    return lax.rsqrt(jnp.mean(values * values, axis=-1, keepdims=True) + epsilon)


def silu_slope(values):
    sigmoid_val = jax.nn.sigmoid(values)
    return sigmoid_val * (1.0 + values * (1.0 - sigmoid_val))


def matmul_plain(left, right):
    return jnp.dot(left, right, preferred_element_type=jnp.float32)


def times_trans(left, right):
    return lax.dot_general(
        left, right, (((1,), (1,)), ((), ())), preferred_element_type=jnp.float32
    )


def trans_times(left, right):
    return lax.dot_general(
        left, right, (((0,), (0,)), ((), ())), preferred_element_type=jnp.float32
    )


def pack_kernel(per, first_ref, second_ref, right_ref, out_ref):
    col = pl.program_id(1)

    @pl.when(col < per)
    def _():
        out_ref[...] = jnp.dot(
            first_ref[...].T, right_ref[...], preferred_element_type=jnp.float32
        ).astype(out_ref.dtype)

    @pl.when(col >= per)
    def _():
        out_ref[...] = jnp.dot(
            second_ref[...].T, right_ref[...], preferred_element_type=jnp.float32
        ).astype(out_ref.dtype)


def grad_pack(first, second, right, width):
    depth, rows_out = first.shape
    cols = right.shape[1]
    blocks = cols // width
    per = blocks - 1
    tile = rows_out
    return pl.pallas_call(
        functools.partial(pack_kernel, per),
        grid=(rows_out // tile, blocks),
        in_specs=[
            pl.BlockSpec((depth, tile), lambda i, j: (0, i)),
            pl.BlockSpec((depth, tile), lambda i, j: (0, i)),
            pl.BlockSpec((depth, width), lambda i, j: (0, j)),
        ],
        out_specs=pl.BlockSpec((tile, width), lambda i, j: (i, j)),
        out_shape=jax.ShapeDtypeStruct((rows_out, cols), jnp.bfloat16),
        cost_estimate=pl.CostEstimate(
            flops=2 * depth * rows_out * cols,
            transcendentals=0,
            bytes_accessed=2 * (2 * depth * rows_out + depth * cols + rows_out * cols),
        ),
    )(first, second, right)


def recurrence(query, forget_raw, value, floor_vec, doc_rows):
    length = query.shape[1]
    forget = floor_vec + (1.0 - floor_vec) * jax.nn.sigmoid(forget_raw)
    log_forget = jnp.log(forget)
    keyed = 1.0 - forget
    position = jnp.arange(length)
    same_doc = doc_rows[:, :, None] == doc_rows[:, None, :]
    causal = same_doc & (position[:, None] >= position[None, :])
    starts = jnp.concatenate(
        [jnp.zeros_like(doc_rows[:, :1], dtype=bool), doc_rows[:, 1:] == doc_rows[:, :-1]], axis=1
    )
    summing = (causal & starts[:, None, :]).astype(jnp.float32)
    running = jnp.einsum("rij,rjhk->rihk", summing, log_forget, precision=HIGHEST)
    query_t = query * jnp.exp(running)
    key_t = keyed * jnp.exp(-running)
    scores = jnp.einsum("rihk,rjhk->rhij", query_t, key_t, precision=HIGHEST)
    scores = jnp.where(causal[:, None], scores, 0.0)
    return jnp.einsum("rhij,rjhv->rihv", scores, value, precision=HIGHEST)


ON_CHIP = [(0, 1), (1, 0), (2, 3), (3, 2)]
ACROSS = [(0, 2), (2, 0), (1, 3), (3, 1)]
SLOT_XOR = (0, 2, 1, 3)


def row_gather(values):
    across = lax.ppermute(values, "tensor", ACROSS)
    pair = jnp.stack([values, across])
    other = lax.ppermute(pair, "tensor", ON_CHIP)
    return jnp.concatenate([pair, other]).reshape((-1,) + values.shape[1:])


def row_sum(values):
    blocks = values.reshape((4, -1) + values.shape[1:])
    got = lax.ppermute(blocks[2:], "tensor", ON_CHIP)
    mine = blocks[0] + got[0]
    theirs = blocks[1] + got[1]
    return mine + lax.ppermute(theirs.astype(jnp.bfloat16), "tensor", ACROSS).astype(jnp.float32)


def spread_sum(values, axis, count):
    blocks = values.reshape((count, -1) + values.shape[1:])
    got = lax.all_to_all(blocks, axis, 0, 0, tiled=False)
    return got.astype(jnp.float32).sum(axis=0)


def ring_pairs(step, stride, size):
    pairs = []
    for i in range(32):
        pos = (i // stride) % size
        pairs.append((i, i + (((pos + step) % size) - pos) * stride))
    return pairs


def ring_stage(chunks, pos, stride, size):
    half = chunks.shape[-1] // 2
    result = []
    for step, cols in ((1, slice(0, half)), (size - 1, slice(half, None))):
        own = chunks[..., cols]
        pairs = ring_pairs(step, stride, size)

        def pick(k):
            return lax.dynamic_index_in_dim(own, (pos - k * step) % size, 0, keepdims=False)

        acc = pick(1).astype(jnp.float32)
        for k in range(2, size + 1):
            got = lax.ppermute(acc.astype(jnp.bfloat16), "dp", pairs)
            acc = pick(k % size).astype(jnp.float32) + got.astype(jnp.float32)
        result.append(acc)
    return jnp.concatenate(result, axis=-1)


def ring_sum(values):
    index = lax.axis_index("dp")
    x_pos, y_pos, z_pos = index % 4, (index // 4) % 2, index // 8
    blocks = values.reshape((4, 2, 4, -1) + values.shape[1:])
    along_x = ring_stage(jnp.moveaxis(blocks, 2, 0), x_pos, 1, 4)
    along_z = ring_stage(along_x.astype(jnp.bfloat16), z_pos, 8, 4)
    keep = lax.dynamic_index_in_dim(along_z, y_pos, 0, keepdims=False)
    give = lax.dynamic_index_in_dim(along_z, 1 - y_pos, 0, keepdims=False)
    pair = [(i, i ^ 4) for i in range(32)]
    return keep + lax.ppermute(give.astype(jnp.bfloat16), "dp", pair).astype(jnp.float32)


def ring_gather(values, rider):
    index = lax.axis_index("dp")
    x_pos, y_pos, z_pos = index % 4, (index // 4) % 2, index // 8
    zero = jnp.zeros((), jnp.int32)
    pair = [(i, i ^ 4) for i in range(32)]
    other = lax.ppermute(values, "dp", pair)
    rider, other = lax.optimization_barrier((rider, other))
    both = jnp.zeros((2,) + values.shape, values.dtype)
    both = lax.dynamic_update_slice(both, values[None], (y_pos, zero, zero))
    both = lax.dynamic_update_slice(both, other[None], (1 - y_pos, zero, zero))
    part_rows = values.shape[0] // 4
    cols = values.shape[1]
    full = jnp.zeros((4, 2, 4) + values.shape, values.dtype)
    for part, (x_first, step) in enumerate(((True, 1), (True, 3), (False, 1), (False, 3))):
        rows = both[:, part * part_rows : (part + 1) * part_rows]
        row_at = jnp.full((), part * part_rows, jnp.int32)
        if x_first:
            pairs = ring_pairs(step, 1, 4)
            first = jnp.zeros((2, 4, part_rows, cols), values.dtype)
            cur = rows
            first = lax.dynamic_update_slice(first, cur[:, None], (zero, x_pos, zero, zero))
            for k in range(1, 4):
                cur = lax.ppermute(cur, "dp", pairs)
                first = lax.dynamic_update_slice(first, cur[:, None], (zero, (x_pos - k * step) % 4, zero, zero))
            pairs = ring_pairs(step, 8, 4)
            cur = first
            full = lax.dynamic_update_slice(full, cur[None], (z_pos, zero, zero, row_at, zero))
            for k in range(1, 4):
                cur = lax.ppermute(cur, "dp", pairs)
                full = lax.dynamic_update_slice(full, cur[None], ((z_pos - k * step) % 4, zero, zero, row_at, zero))
        else:
            pairs = ring_pairs(step, 8, 4)
            first = jnp.zeros((4, 2, part_rows, cols), values.dtype)
            cur = rows
            first = lax.dynamic_update_slice(first, cur[None], (z_pos, zero, zero, zero))
            for k in range(1, 4):
                cur = lax.ppermute(cur, "dp", pairs)
                first = lax.dynamic_update_slice(first, cur[None], ((z_pos - k * step) % 4, zero, zero, zero))
            pairs = ring_pairs(step, 1, 4)
            cur = first
            full = lax.dynamic_update_slice(full, cur[:, :, None], (zero, zero, x_pos, row_at, zero))
            for k in range(1, 4):
                cur = lax.ppermute(cur, "dp", pairs)
                full = lax.dynamic_update_slice(full, cur[:, :, None], (zero, zero, (x_pos - k * step) % 4, row_at, zero))
    return full.reshape((-1, cols)), rider


def small_gather(vectors):
    count = 128
    spread = jnp.broadcast_to(vectors[None], (count,) + vectors.shape)
    got = lax.all_to_all(spread, ("dp", "tensor"), 0, 0, tiled=False)
    return jnp.swapaxes(got, 0, 1).reshape(vectors.shape[0], -1)


def small_sum(vectors):
    count = 128
    blocks = vectors.reshape(vectors.shape[0], count, -1)
    got = lax.all_to_all(jnp.swapaxes(blocks, 0, 1), ("dp", "tensor"), 0, 0, tiled=False)
    return got.sum(axis=0)


def shards(
    tokens,
    doc_ids,
    attn_gain,
    forget_floor,
    w_query,
    w_forget,
    w_value,
    w_outgate,
    w_output,
    mlp_gain,
    w_gate,
    w_up,
    w_down,
    cotangent,
):
    part_index = lax.axis_index("tensor")
    local_width = w_query.shape[1]
    local_heads = local_width // HK
    hidden_width = w_gate.shape[1]
    model_width = tokens.shape[-1]
    slot_rows = jnp.bitwise_xor(part_index, jnp.array(SLOT_XOR, jnp.int32))
    doc_all = jnp.take(doc_ids[0], slot_rows, axis=0)
    row_count = doc_all.shape[0]
    resid_in = tokens[0].reshape(-1, model_width).astype(jnp.float32)
    cot_local = cotangent[0].reshape(-1, model_width)
    attn_pack = jnp.concatenate([w_query, w_forget, w_value, w_outgate, w_output.T], axis=1)
    mlp_pack = jnp.concatenate([w_gate, w_up, w_down.T], axis=1)
    attn_all, gain_rows = ring_gather(attn_pack, jnp.stack([attn_gain, forget_floor, mlp_gain]))
    gains = small_gather(gain_rows)
    attn_full, floor_full, mlp_full = gains[0], gains[1], gains[2]
    floor_local = lax.dynamic_slice_in_dim(
        floor_full, part_index * local_width, local_width
    ).reshape(local_heads, HK)
    mlp_all = lax.all_gather(mlp_pack, "dp", axis=0, tiled=True)
    wq_all = attn_all[:, 0 * local_width : 1 * local_width]
    wf_all = attn_all[:, 1 * local_width : 2 * local_width]
    wv_all = attn_all[:, 2 * local_width : 3 * local_width]
    wg_all = attn_all[:, 3 * local_width : 4 * local_width]
    wo_t = attn_all[:, 4 * local_width : 5 * local_width]
    wgate_all = mlp_all[:, 0:hidden_width]
    wup_all = mlp_all[:, hidden_width : 2 * hidden_width]
    wdown_t = mlp_all[:, 2 * hidden_width : 3 * hidden_width]
    scale_one = row_scale(resid_in)
    normed = row_gather((resid_in * scale_one * attn_full).astype(jnp.bfloat16))
    query = matmul_plain(normed, wq_all)
    forget_raw = matmul_plain(normed, wf_all)
    value = matmul_plain(normed, wv_all)
    out_gate = matmul_plain(normed, wg_all)

    def mixer(query_in, forget_in, value_in, floor_in):

        def shaped(arr):
            return arr.reshape(row_count, -1, local_heads, HK)

        mixed_rows = recurrence(
            shaped(query_in), shaped(forget_in), shaped(value_in), floor_in, doc_all
        )
        return mixed_rows.reshape(query_in.shape[0], local_width)

    mixed, pullback = jax.vjp(mixer, query, forget_raw, value, floor_local)
    gate_act = jax.nn.silu(out_gate)
    gated = (mixed * gate_act).astype(jnp.bfloat16)
    branch = row_sum(times_trans(gated, wo_t))
    resid = resid_in + branch
    scale_two = row_scale(resid)
    normed2 = row_gather((resid * scale_two * mlp_full).astype(jnp.bfloat16))
    gate_proj = matmul_plain(normed2, wgate_all)
    up_proj = matmul_plain(normed2, wup_all)
    gate_silu = jax.nn.silu(gate_proj)
    hidden = (gate_silu * up_proj).astype(jnp.bfloat16)
    ffn_out = row_sum(times_trans(hidden, wdown_t))
    layer_out = (resid + ffn_out).astype(jnp.bfloat16).reshape(tokens.shape)
    cot_full = row_gather(cot_local)
    d_hidden = matmul_plain(cot_full, wdown_t)
    d_gate = (d_hidden * up_proj * silu_slope(gate_proj)).astype(jnp.bfloat16)
    d_up = (d_hidden * gate_silu).astype(jnp.bfloat16)
    mlp_grads = grad_pack(
        normed2, cot_full, jnp.concatenate([d_gate, d_up, hidden], axis=1), hidden_width
    )
    mlp_red = lax.psum_scatter(mlp_grads, "dp", scatter_dimension=0, tiled=True).astype(jnp.float32)
    d_normed2 = row_sum(times_trans(d_gate, wgate_all) + times_trans(d_up, wup_all))
    grad_mlp = jnp.sum(d_normed2 * resid * scale_two, axis=0)
    inner_two = jnp.mean(d_normed2 * mlp_full * resid, axis=-1, keepdims=True)
    d_resid = (
        cot_local.astype(jnp.float32)
        + d_normed2 * mlp_full * scale_two
        - resid * scale_two**3 * inner_two
    )
    d_branch = row_gather(d_resid.astype(jnp.bfloat16))
    d_gated = matmul_plain(d_branch, wo_t)
    d_mixed = d_gated * gate_act
    d_outgate = (d_gated * mixed * silu_slope(out_gate)).astype(jnp.bfloat16)
    d_query, d_forget, d_value, d_floor = pullback(d_mixed)
    d_query = d_query.astype(jnp.bfloat16)
    d_forget = d_forget.astype(jnp.bfloat16)
    d_value = d_value.astype(jnp.bfloat16)
    attn_grads = grad_pack(
        normed,
        d_branch,
        jnp.concatenate([d_query, d_forget, d_value, d_outgate, gated], axis=1),
        local_width,
    )
    attn_red = ring_sum(attn_grads)
    d_normed = row_sum(
        times_trans(d_query, wq_all)
        + times_trans(d_forget, wf_all)
        + times_trans(d_value, wv_all)
        + times_trans(d_outgate, wg_all)
    )
    grad_attn = jnp.sum(d_normed * resid_in * scale_one, axis=0)
    inner_one = jnp.mean(d_normed * attn_full * resid_in, axis=-1, keepdims=True)
    grad_tokens = (
        d_resid + d_normed * attn_full * scale_one - resid_in * scale_one**3 * inner_one
    ).reshape(tokens.shape)
    floor_vector = lax.dynamic_update_slice(
        jnp.zeros((model_width,), jnp.float32), d_floor.reshape(-1), (part_index * local_width,)
    )
    reduced_small = small_sum(jnp.stack([grad_attn, floor_vector, grad_mlp]))
    return (
        layer_out,
        grad_tokens,
        reduced_small[0],
        reduced_small[1],
        attn_red[:, 0 * local_width : 1 * local_width],
        attn_red[:, 1 * local_width : 2 * local_width],
        attn_red[:, 2 * local_width : 3 * local_width],
        attn_red[:, 3 * local_width : 4 * local_width],
        attn_red[:, 4 * local_width : 5 * local_width].T,
        reduced_small[2],
        mlp_red[:, 0:hidden_width],
        mlp_red[:, hidden_width : 2 * hidden_width],
        mlp_red[:, 2 * hidden_width : 3 * hidden_width].T,
    )


def solution(mesh):
    return jax.shard_map(
        shards,
        mesh=mesh,
        in_specs=(
            P("dp", "tensor", None, None),
            P("dp", None, None),
            P(("dp", "tensor")),
            P(("dp", "tensor")),
            P("dp", "tensor"),
            P("dp", "tensor"),
            P("dp", "tensor"),
            P("dp", "tensor"),
            P("tensor", "dp"),
            P(("dp", "tensor")),
            P("dp", "tensor"),
            P("dp", "tensor"),
            P("tensor", "dp"),
            P("dp", "tensor", None, None),
        ),
        out_specs=(
            P("dp", "tensor", None, None),
            P("dp", "tensor", None, None),
            P(("dp", "tensor")),
            P(("dp", "tensor")),
            P("dp", "tensor"),
            P("dp", "tensor"),
            P("dp", "tensor"),
            P("dp", "tensor"),
            P("tensor", "dp"),
            P(("dp", "tensor")),
            P("dp", "tensor"),
            P("dp", "tensor"),
            P("tensor", "dp"),
        ),
        check_vma=False,
    )
```

```python
import functools

import jax
import jax.numpy as jnp
from jax import lax
from jax.experimental import pallas as pl
from jax.experimental.pallas import tpu as pltpu
from jax.sharding import PartitionSpec as P

HK = 128
HIGHEST = lax.Precision.HIGH


epsilon = 1e-06


def row_scale(values):
    return lax.rsqrt(jnp.mean(values * values, axis=-1, keepdims=True) + epsilon)


def silu_slope(values):
    sigmoid_val = jax.nn.sigmoid(values)
    return sigmoid_val * (1.0 + values * (1.0 - sigmoid_val))


def matmul_plain(left, right):
    return jnp.dot(left, right, preferred_element_type=jnp.float32)


def times_trans(left, right):
    return lax.dot_general(
        left, right, (((1,), (1,)), ((), ())), preferred_element_type=jnp.float32
    )


def trans_times(left, right):
    return lax.dot_general(
        left, right, (((0,), (0,)), ((), ())), preferred_element_type=jnp.float32
    )


def pack_kernel(per, first_ref, second_ref, right_ref, out_ref):
    col = pl.program_id(1)

    @pl.when(col < per)
    def _():
        out_ref[...] = jnp.dot(
            first_ref[...].T, right_ref[...], preferred_element_type=jnp.float32
        ).astype(out_ref.dtype)

    @pl.when(col >= per)
    def _():
        out_ref[...] = jnp.dot(
            second_ref[...].T, right_ref[...], preferred_element_type=jnp.float32
        ).astype(out_ref.dtype)


def grad_pack(first, second, right, width):
    depth, rows_out = first.shape
    cols = right.shape[1]
    blocks = cols // width
    per = blocks - 1
    tile = rows_out
    return pl.pallas_call(
        functools.partial(pack_kernel, per),
        grid=(rows_out // tile, blocks),
        in_specs=[
            pl.BlockSpec((depth, tile), lambda i, j: (0, i)),
            pl.BlockSpec((depth, tile), lambda i, j: (0, i)),
            pl.BlockSpec((depth, width), lambda i, j: (0, j)),
        ],
        out_specs=pl.BlockSpec((tile, width), lambda i, j: (i, j)),
        out_shape=jax.ShapeDtypeStruct((rows_out, cols), jnp.bfloat16),
        cost_estimate=pl.CostEstimate(
            flops=2 * depth * rows_out * cols,
            transcendentals=0,
            bytes_accessed=2 * (2 * depth * rows_out + depth * cols + rows_out * cols),
        ),
    )(first, second, right)


def recurrence(query, forget_raw, value, floor_vec, doc_rows):
    length = query.shape[1]
    forget = floor_vec + (1.0 - floor_vec) * jax.nn.sigmoid(forget_raw)
    log_forget = jnp.log(forget)
    keyed = 1.0 - forget
    position = jnp.arange(length)
    same_doc = doc_rows[:, :, None] == doc_rows[:, None, :]
    causal = same_doc & (position[:, None] >= position[None, :])
    starts = jnp.concatenate(
        [jnp.zeros_like(doc_rows[:, :1], dtype=bool), doc_rows[:, 1:] == doc_rows[:, :-1]], axis=1
    )
    summing = (causal & starts[:, None, :]).astype(jnp.float32)
    running = jnp.einsum("rij,rjhk->rihk", summing, log_forget, precision=HIGHEST)
    query_t = query * jnp.exp(running)
    key_t = keyed * jnp.exp(-running)
    scores = jnp.einsum("rihk,rjhk->rhij", query_t, key_t, precision=HIGHEST)
    scores = jnp.where(causal[:, None], scores, 0.0)
    return jnp.einsum("rhij,rjhv->rihv", scores, value, precision=HIGHEST)


ON_CHIP = [(0, 1), (1, 0), (2, 3), (3, 2)]
ACROSS = [(0, 2), (2, 0), (1, 3), (3, 1)]
SLOT_XOR = (0, 2, 1, 3)


def row_gather(values):
    across = lax.ppermute(values, "tensor", ACROSS)
    pair = jnp.stack([values, across])
    other = lax.ppermute(pair, "tensor", ON_CHIP)
    return jnp.concatenate([pair, other]).reshape((-1,) + values.shape[1:])


def row_sum(values):
    blocks = values.reshape((4, -1) + values.shape[1:])
    got = lax.ppermute(blocks[2:], "tensor", ON_CHIP)
    mine = blocks[0] + got[0]
    theirs = blocks[1] + got[1]
    return mine + lax.ppermute(theirs.astype(jnp.bfloat16), "tensor", ACROSS).astype(jnp.float32)


def spread_sum(values, axis, count):
    blocks = values.reshape((count, -1) + values.shape[1:])
    got = lax.all_to_all(blocks, axis, 0, 0, tiled=False)
    return got.astype(jnp.float32).sum(axis=0)


def ring_pairs(step, stride, size):
    pairs = []
    for i in range(32):
        pos = (i // stride) % size
        pairs.append((i, i + (((pos + step) % size) - pos) * stride))
    return pairs


def ring_stage(chunks, pos, stride, size):
    half = chunks.shape[-1] // 2
    result = []
    for step, cols in ((1, slice(0, half)), (size - 1, slice(half, None))):
        own = chunks[..., cols]
        pairs = ring_pairs(step, stride, size)

        def pick(k):
            return lax.dynamic_index_in_dim(own, (pos - k * step) % size, 0, keepdims=False)

        acc = pick(1).astype(jnp.float32)
        for k in range(2, size + 1):
            got = lax.ppermute(acc.astype(jnp.bfloat16), "dp", pairs)
            acc = pick(k % size).astype(jnp.float32) + got.astype(jnp.float32)
        result.append(acc)
    return jnp.concatenate(result, axis=-1)


def ring_sum(values):
    index = lax.axis_index("dp")
    x_pos, y_pos, z_pos = index % 4, (index // 4) % 2, index // 8
    blocks = values.reshape((4, 2, 4, -1) + values.shape[1:])
    along_x = ring_stage(jnp.moveaxis(blocks, 2, 0), x_pos, 1, 4)
    along_z = ring_stage(along_x.astype(jnp.bfloat16), z_pos, 8, 4)
    keep = lax.dynamic_index_in_dim(along_z, y_pos, 0, keepdims=False)
    give = lax.dynamic_index_in_dim(along_z, 1 - y_pos, 0, keepdims=False)
    pair = [(i, i ^ 4) for i in range(32)]
    return keep + lax.ppermute(give.astype(jnp.bfloat16), "dp", pair).astype(jnp.float32)


def ring_gather(values):
    index = lax.axis_index("dp")
    x_pos, y_pos, z_pos = index % 4, (index // 4) % 2, index // 8
    zero = jnp.zeros((), jnp.int32)
    pair = [(i, i ^ 4) for i in range(32)]
    other = lax.ppermute(values, "dp", pair)
    both = jnp.zeros((2,) + values.shape, values.dtype)
    both = lax.dynamic_update_slice(both, values[None], (y_pos, zero, zero))
    both = lax.dynamic_update_slice(both, other[None], (1 - y_pos, zero, zero))
    part_rows = values.shape[0] // 4
    cols = values.shape[1]
    full = jnp.zeros((4, 2, 4) + values.shape, values.dtype)
    for part, (x_first, step) in enumerate(((True, 1), (True, 3), (False, 1), (False, 3))):
        rows = both[:, part * part_rows : (part + 1) * part_rows]
        row_at = jnp.full((), part * part_rows, jnp.int32)
        if x_first:
            pairs = ring_pairs(step, 1, 4)
            first = jnp.zeros((2, 4, part_rows, cols), values.dtype)
            cur = rows
            first = lax.dynamic_update_slice(first, cur[:, None], (zero, x_pos, zero, zero))
            for k in range(1, 4):
                cur = lax.ppermute(cur, "dp", pairs)
                first = lax.dynamic_update_slice(first, cur[:, None], (zero, (x_pos - k * step) % 4, zero, zero))
            pairs = ring_pairs(step, 8, 4)
            cur = first
            full = lax.dynamic_update_slice(full, cur[None], (z_pos, zero, zero, row_at, zero))
            for k in range(1, 4):
                cur = lax.ppermute(cur, "dp", pairs)
                full = lax.dynamic_update_slice(full, cur[None], ((z_pos - k * step) % 4, zero, zero, row_at, zero))
        else:
            pairs = ring_pairs(step, 8, 4)
            first = jnp.zeros((4, 2, part_rows, cols), values.dtype)
            cur = rows
            first = lax.dynamic_update_slice(first, cur[None], (z_pos, zero, zero, zero))
            for k in range(1, 4):
                cur = lax.ppermute(cur, "dp", pairs)
                first = lax.dynamic_update_slice(first, cur[None], ((z_pos - k * step) % 4, zero, zero, zero))
            pairs = ring_pairs(step, 1, 4)
            cur = first
            full = lax.dynamic_update_slice(full, cur[:, :, None], (zero, zero, x_pos, row_at, zero))
            for k in range(1, 4):
                cur = lax.ppermute(cur, "dp", pairs)
                full = lax.dynamic_update_slice(full, cur[:, :, None], (zero, zero, (x_pos - k * step) % 4, row_at, zero))
    return full.reshape((-1, cols))


def small_gather(vectors):
    count = 128
    spread = jnp.broadcast_to(vectors[None], (count,) + vectors.shape)
    got = lax.all_to_all(spread, ("dp", "tensor"), 0, 0, tiled=False)
    return jnp.swapaxes(got, 0, 1).reshape(vectors.shape[0], -1)


def small_sum(vectors):
    count = 128
    blocks = vectors.reshape(vectors.shape[0], count, -1)
    got = lax.all_to_all(jnp.swapaxes(blocks, 0, 1), ("dp", "tensor"), 0, 0, tiled=False)
    return got.sum(axis=0)


def shards(
    tokens,
    doc_ids,
    attn_gain,
    forget_floor,
    w_query,
    w_forget,
    w_value,
    w_outgate,
    w_output,
    mlp_gain,
    w_gate,
    w_up,
    w_down,
    cotangent,
):
    gains = small_gather(jnp.stack([attn_gain, forget_floor, mlp_gain]))
    attn_full, floor_full, mlp_full = gains[0], gains[1], gains[2]
    part_index = lax.axis_index("tensor")
    local_width = w_query.shape[1]
    local_heads = local_width // HK
    hidden_width = w_gate.shape[1]
    floor_local = lax.dynamic_slice_in_dim(
        floor_full, part_index * local_width, local_width
    ).reshape(local_heads, HK)
    model_width = attn_full.shape[0]
    slot_rows = jnp.bitwise_xor(part_index, jnp.array(SLOT_XOR, jnp.int32))
    doc_all = jnp.take(doc_ids[0], slot_rows, axis=0)
    row_count = doc_all.shape[0]
    resid_in = tokens[0].reshape(-1, model_width).astype(jnp.float32)
    cot_local = cotangent[0].reshape(-1, model_width)
    attn_pack = jnp.concatenate([w_query, w_forget, w_value, w_outgate, w_output.T], axis=1)
    mlp_pack = jnp.concatenate([w_gate, w_up, w_down.T], axis=1)
    attn_all = ring_gather(attn_pack)
    mlp_all = lax.all_gather(mlp_pack, "dp", axis=0, tiled=True)
    wq_all = attn_all[:, 0 * local_width : 1 * local_width]
    wf_all = attn_all[:, 1 * local_width : 2 * local_width]
    wv_all = attn_all[:, 2 * local_width : 3 * local_width]
    wg_all = attn_all[:, 3 * local_width : 4 * local_width]
    wo_t = attn_all[:, 4 * local_width : 5 * local_width]
    wgate_all = mlp_all[:, 0:hidden_width]
    wup_all = mlp_all[:, hidden_width : 2 * hidden_width]
    wdown_t = mlp_all[:, 2 * hidden_width : 3 * hidden_width]
    scale_one = row_scale(resid_in)
    normed = row_gather((resid_in * scale_one * attn_full).astype(jnp.bfloat16))
    query = matmul_plain(normed, wq_all)
    forget_raw = matmul_plain(normed, wf_all)
    value = matmul_plain(normed, wv_all)
    out_gate = matmul_plain(normed, wg_all)

    def mixer(query_in, forget_in, value_in, floor_in):

        def shaped(arr):
            return arr.reshape(row_count, -1, local_heads, HK)

        mixed_rows = recurrence(
            shaped(query_in), shaped(forget_in), shaped(value_in), floor_in, doc_all
        )
        return mixed_rows.reshape(query_in.shape[0], local_width)

    mixed, pullback = jax.vjp(mixer, query, forget_raw, value, floor_local)
    gate_act = jax.nn.silu(out_gate)
    gated = (mixed * gate_act).astype(jnp.bfloat16)
    branch = row_sum(times_trans(gated, wo_t))
    resid = resid_in + branch
    scale_two = row_scale(resid)
    normed2 = row_gather((resid * scale_two * mlp_full).astype(jnp.bfloat16))
    gate_proj = matmul_plain(normed2, wgate_all)
    up_proj = matmul_plain(normed2, wup_all)
    gate_silu = jax.nn.silu(gate_proj)
    hidden = (gate_silu * up_proj).astype(jnp.bfloat16)
    ffn_out = row_sum(times_trans(hidden, wdown_t))
    layer_out = (resid + ffn_out).astype(jnp.bfloat16).reshape(tokens.shape)
    cot_full = row_gather(cot_local)
    d_hidden = matmul_plain(cot_full, wdown_t)
    d_gate = (d_hidden * up_proj * silu_slope(gate_proj)).astype(jnp.bfloat16)
    d_up = (d_hidden * gate_silu).astype(jnp.bfloat16)
    mlp_grads = grad_pack(
        normed2, cot_full, jnp.concatenate([d_gate, d_up, hidden], axis=1), hidden_width
    )
    mlp_red = lax.psum_scatter(mlp_grads, "dp", scatter_dimension=0, tiled=True).astype(jnp.float32)
    d_normed2 = row_sum(times_trans(d_gate, wgate_all) + times_trans(d_up, wup_all))
    grad_mlp = jnp.sum(d_normed2 * resid * scale_two, axis=0)
    inner_two = jnp.mean(d_normed2 * mlp_full * resid, axis=-1, keepdims=True)
    d_resid = (
        cot_local.astype(jnp.float32)
        + d_normed2 * mlp_full * scale_two
        - resid * scale_two**3 * inner_two
    )
    d_branch = row_gather(d_resid.astype(jnp.bfloat16))
    d_gated = matmul_plain(d_branch, wo_t)
    d_mixed = d_gated * gate_act
    d_outgate = (d_gated * mixed * silu_slope(out_gate)).astype(jnp.bfloat16)
    d_query, d_forget, d_value, d_floor = pullback(d_mixed)
    d_query = d_query.astype(jnp.bfloat16)
    d_forget = d_forget.astype(jnp.bfloat16)
    d_value = d_value.astype(jnp.bfloat16)
    attn_grads = grad_pack(
        normed,
        d_branch,
        jnp.concatenate([d_query, d_forget, d_value, d_outgate, gated], axis=1),
        local_width,
    )
    attn_red = ring_sum(attn_grads)
    d_normed = row_sum(
        times_trans(d_query, wq_all)
        + times_trans(d_forget, wf_all)
        + times_trans(d_value, wv_all)
        + times_trans(d_outgate, wg_all)
    )
    grad_attn = jnp.sum(d_normed * resid_in * scale_one, axis=0)
    inner_one = jnp.mean(d_normed * attn_full * resid_in, axis=-1, keepdims=True)
    grad_tokens = (
        d_resid + d_normed * attn_full * scale_one - resid_in * scale_one**3 * inner_one
    ).reshape(tokens.shape)
    floor_vector = lax.dynamic_update_slice(
        jnp.zeros((model_width,), jnp.float32), d_floor.reshape(-1), (part_index * local_width,)
    )
    reduced_small = small_sum(jnp.stack([grad_attn, floor_vector, grad_mlp]))
    return (
        layer_out,
        grad_tokens,
        reduced_small[0],
        reduced_small[1],
        attn_red[:, 0 * local_width : 1 * local_width],
        attn_red[:, 1 * local_width : 2 * local_width],
        attn_red[:, 2 * local_width : 3 * local_width],
        attn_red[:, 3 * local_width : 4 * local_width],
        attn_red[:, 4 * local_width : 5 * local_width].T,
        reduced_small[2],
        mlp_red[:, 0:hidden_width],
        mlp_red[:, hidden_width : 2 * hidden_width],
        mlp_red[:, 2 * hidden_width : 3 * hidden_width].T,
    )


def solution(mesh):
    return jax.shard_map(
        shards,
        mesh=mesh,
        in_specs=(
            P("dp", "tensor", None, None),
            P("dp", None, None),
            P(("dp", "tensor")),
            P(("dp", "tensor")),
            P("dp", "tensor"),
            P("dp", "tensor"),
            P("dp", "tensor"),
            P("dp", "tensor"),
            P("tensor", "dp"),
            P(("dp", "tensor")),
            P("dp", "tensor"),
            P("dp", "tensor"),
            P("tensor", "dp"),
            P("dp", "tensor", None, None),
        ),
        out_specs=(
            P("dp", "tensor", None, None),
            P("dp", "tensor", None, None),
            P(("dp", "tensor")),
            P(("dp", "tensor")),
            P("dp", "tensor"),
            P("dp", "tensor"),
            P("dp", "tensor"),
            P("dp", "tensor"),
            P("tensor", "dp"),
            P(("dp", "tensor")),
            P("dp", "tensor"),
            P("dp", "tensor"),
            P("tensor", "dp"),
        ),
        check_vma=False,
    )
```

```python
import functools

import jax
import jax.numpy as jnp
from jax import lax
from jax.experimental import pallas as pl
from jax.experimental.pallas import tpu as pltpu
from jax.sharding import PartitionSpec as P

HK = 128
HIGHEST = lax.Precision.HIGH


epsilon = 1e-06


def row_scale(values):
    return lax.rsqrt(jnp.mean(values * values, axis=-1, keepdims=True) + epsilon)


def silu_slope(values):
    sigmoid_val = jax.nn.sigmoid(values)
    return sigmoid_val * (1.0 + values * (1.0 - sigmoid_val))


def matmul_plain(left, right):
    return jnp.dot(left, right, preferred_element_type=jnp.float32)


def times_trans(left, right):
    return lax.dot_general(
        left, right, (((1,), (1,)), ((), ())), preferred_element_type=jnp.float32
    )


def trans_times(left, right):
    return lax.dot_general(
        left, right, (((0,), (0,)), ((), ())), preferred_element_type=jnp.float32
    )


def pack_kernel(per, first_ref, second_ref, right_ref, out_ref):
    col = pl.program_id(1)

    @pl.when(col < per)
    def _():
        out_ref[...] = jnp.dot(
            first_ref[...].T, right_ref[...], preferred_element_type=jnp.float32
        ).astype(out_ref.dtype)

    @pl.when(col >= per)
    def _():
        out_ref[...] = jnp.dot(
            second_ref[...].T, right_ref[...], preferred_element_type=jnp.float32
        ).astype(out_ref.dtype)


def grad_pack(first, second, right, width):
    depth, rows_out = first.shape
    cols = right.shape[1]
    blocks = cols // width
    per = blocks - 1
    tile = rows_out
    return pl.pallas_call(
        functools.partial(pack_kernel, per),
        grid=(rows_out // tile, blocks),
        in_specs=[
            pl.BlockSpec((depth, tile), lambda i, j: (0, i)),
            pl.BlockSpec((depth, tile), lambda i, j: (0, i)),
            pl.BlockSpec((depth, width), lambda i, j: (0, j)),
        ],
        out_specs=pl.BlockSpec((tile, width), lambda i, j: (i, j)),
        out_shape=jax.ShapeDtypeStruct((rows_out, cols), jnp.bfloat16),
        cost_estimate=pl.CostEstimate(
            flops=2 * depth * rows_out * cols,
            transcendentals=0,
            bytes_accessed=2 * (2 * depth * rows_out + depth * cols + rows_out * cols),
        ),
    )(first, second, right)


def recurrence(query, forget_raw, value, floor_vec, doc_rows):
    length = query.shape[1]
    forget = floor_vec + (1.0 - floor_vec) * jax.nn.sigmoid(forget_raw)
    log_forget = jnp.log(forget)
    keyed = 1.0 - forget
    position = jnp.arange(length)
    same_doc = doc_rows[:, :, None] == doc_rows[:, None, :]
    causal = same_doc & (position[:, None] >= position[None, :])
    starts = jnp.concatenate(
        [jnp.zeros_like(doc_rows[:, :1], dtype=bool), doc_rows[:, 1:] == doc_rows[:, :-1]], axis=1
    )
    summing = (causal & starts[:, None, :]).astype(jnp.float32)
    running = jnp.einsum("rij,rjhk->rihk", summing, log_forget, precision=HIGHEST)
    query_t = query * jnp.exp(running)
    key_t = keyed * jnp.exp(-running)
    scores = jnp.einsum("rihk,rjhk->rhij", query_t, key_t, precision=HIGHEST)
    scores = jnp.where(causal[:, None], scores, 0.0)
    return jnp.einsum("rhij,rjhv->rihv", scores, value, precision=HIGHEST)


ON_CHIP = [(0, 1), (1, 0), (2, 3), (3, 2)]
ACROSS = [(0, 2), (2, 0), (1, 3), (3, 1)]
SLOT_XOR = (0, 2, 1, 3)


def row_gather(values):
    across = lax.ppermute(values, "tensor", ACROSS)
    pair = jnp.stack([values, across])
    other = lax.ppermute(pair, "tensor", ON_CHIP)
    return jnp.concatenate([pair, other]).reshape((-1,) + values.shape[1:])


def row_sum(values):
    blocks = values.reshape((4, -1) + values.shape[1:])
    got = lax.ppermute(blocks[2:], "tensor", ON_CHIP)
    mine = blocks[0] + got[0]
    theirs = blocks[1] + got[1]
    return mine + lax.ppermute(theirs.astype(jnp.bfloat16), "tensor", ACROSS).astype(jnp.float32)


def spread_sum(values, axis, count):
    blocks = values.reshape((count, -1) + values.shape[1:])
    got = lax.all_to_all(blocks, axis, 0, 0, tiled=False)
    return got.astype(jnp.float32).sum(axis=0)


def ring_pairs(step, stride, size):
    pairs = []
    for i in range(32):
        pos = (i // stride) % size
        pairs.append((i, i + (((pos + step) % size) - pos) * stride))
    return pairs


def ring_stage(chunks, pos, stride, size):
    half = chunks.shape[-1] // 2
    result = []
    for step, cols in ((1, slice(0, half)), (size - 1, slice(half, None))):
        own = chunks[..., cols]
        pairs = ring_pairs(step, stride, size)

        def pick(k):
            return lax.dynamic_index_in_dim(own, (pos - k * step) % size, 0, keepdims=False)

        acc = pick(1).astype(jnp.float32)
        for k in range(2, size + 1):
            got = lax.ppermute(acc.astype(jnp.bfloat16), "dp", pairs)
            acc = pick(k % size).astype(jnp.float32) + got.astype(jnp.float32)
        result.append(acc)
    return jnp.concatenate(result, axis=-1)


def ring_sum(values):
    index = lax.axis_index("dp")
    x_pos, y_pos, z_pos = index % 4, (index // 4) % 2, index // 8
    blocks = values.reshape((4, 2, 4, -1) + values.shape[1:])
    along_x = ring_stage(jnp.moveaxis(blocks, 2, 0), x_pos, 1, 4)
    along_z = ring_stage(along_x.astype(jnp.bfloat16), z_pos, 8, 4)
    keep = lax.dynamic_index_in_dim(along_z, y_pos, 0, keepdims=False)
    give = lax.dynamic_index_in_dim(along_z, 1 - y_pos, 0, keepdims=False)
    pair = [(i, i ^ 4) for i in range(32)]
    return keep + lax.ppermute(give.astype(jnp.bfloat16), "dp", pair).astype(jnp.float32)


def ring_gather(values):
    index = lax.axis_index("dp")
    x_pos, y_pos, z_pos = index % 4, (index // 4) % 2, index // 8
    zero = jnp.zeros((), jnp.int32)
    pair = [(i, i ^ 4) for i in range(32)]
    other = lax.ppermute(values, "dp", pair)
    both = jnp.zeros((2,) + values.shape, values.dtype)
    both = lax.dynamic_update_slice(both, values[None], (y_pos, zero, zero))
    both = lax.dynamic_update_slice(both, other[None], (1 - y_pos, zero, zero))
    part_rows = values.shape[0] // 2
    cols = values.shape[1]
    full = jnp.zeros((4, 2, 4) + values.shape, values.dtype)
    for part, (x_first, step) in enumerate(((True, 1), (True, 3))):
        rows = both[:, part * part_rows : (part + 1) * part_rows]
        row_at = jnp.full((), part * part_rows, jnp.int32)
        if x_first:
            pairs = ring_pairs(step, 1, 4)
            first = jnp.zeros((2, 4, part_rows, cols), values.dtype)
            cur = rows
            first = lax.dynamic_update_slice(first, cur[:, None], (zero, x_pos, zero, zero))
            for k in range(1, 4):
                cur = lax.ppermute(cur, "dp", pairs)
                first = lax.dynamic_update_slice(first, cur[:, None], (zero, (x_pos - k * step) % 4, zero, zero))
            pairs = ring_pairs(step, 8, 4)
            cur = first
            full = lax.dynamic_update_slice(full, cur[None], (z_pos, zero, zero, row_at, zero))
            for k in range(1, 4):
                cur = lax.ppermute(cur, "dp", pairs)
                full = lax.dynamic_update_slice(full, cur[None], ((z_pos - k * step) % 4, zero, zero, row_at, zero))
        else:
            pairs = ring_pairs(step, 8, 4)
            first = jnp.zeros((4, 2, part_rows, cols), values.dtype)
            cur = rows
            first = lax.dynamic_update_slice(first, cur[None], (z_pos, zero, zero, zero))
            for k in range(1, 4):
                cur = lax.ppermute(cur, "dp", pairs)
                first = lax.dynamic_update_slice(first, cur[None], ((z_pos - k * step) % 4, zero, zero, zero))
            pairs = ring_pairs(step, 1, 4)
            cur = first
            full = lax.dynamic_update_slice(full, cur[:, :, None], (zero, zero, x_pos, row_at, zero))
            for k in range(1, 4):
                cur = lax.ppermute(cur, "dp", pairs)
                full = lax.dynamic_update_slice(full, cur[:, :, None], (zero, zero, (x_pos - k * step) % 4, row_at, zero))
    return full.reshape((-1, cols))


def small_gather(vectors):
    count = 128
    spread = jnp.broadcast_to(vectors[None], (count,) + vectors.shape)
    got = lax.all_to_all(spread, ("dp", "tensor"), 0, 0, tiled=False)
    return jnp.swapaxes(got, 0, 1).reshape(vectors.shape[0], -1)


def small_sum(vectors):
    count = 128
    blocks = vectors.reshape(vectors.shape[0], count, -1)
    got = lax.all_to_all(jnp.swapaxes(blocks, 0, 1), ("dp", "tensor"), 0, 0, tiled=False)
    return got.sum(axis=0)


def shards(
    tokens,
    doc_ids,
    attn_gain,
    forget_floor,
    w_query,
    w_forget,
    w_value,
    w_outgate,
    w_output,
    mlp_gain,
    w_gate,
    w_up,
    w_down,
    cotangent,
):
    gains = small_gather(jnp.stack([attn_gain, forget_floor, mlp_gain]))
    attn_full, floor_full, mlp_full = gains[0], gains[1], gains[2]
    part_index = lax.axis_index("tensor")
    local_width = w_query.shape[1]
    local_heads = local_width // HK
    hidden_width = w_gate.shape[1]
    floor_local = lax.dynamic_slice_in_dim(
        floor_full, part_index * local_width, local_width
    ).reshape(local_heads, HK)
    model_width = attn_full.shape[0]
    slot_rows = jnp.bitwise_xor(part_index, jnp.array(SLOT_XOR, jnp.int32))
    doc_all = jnp.take(doc_ids[0], slot_rows, axis=0)
    row_count = doc_all.shape[0]
    resid_in = tokens[0].reshape(-1, model_width).astype(jnp.float32)
    cot_local = cotangent[0].reshape(-1, model_width)
    attn_pack = jnp.concatenate([w_query, w_forget, w_value, w_outgate, w_output.T], axis=1)
    mlp_pack = jnp.concatenate([w_gate, w_up, w_down.T], axis=1)
    attn_all = ring_gather(attn_pack)
    mlp_all = lax.all_gather(mlp_pack, "dp", axis=0, tiled=True)
    wq_all = attn_all[:, 0 * local_width : 1 * local_width]
    wf_all = attn_all[:, 1 * local_width : 2 * local_width]
    wv_all = attn_all[:, 2 * local_width : 3 * local_width]
    wg_all = attn_all[:, 3 * local_width : 4 * local_width]
    wo_t = attn_all[:, 4 * local_width : 5 * local_width]
    wgate_all = mlp_all[:, 0:hidden_width]
    wup_all = mlp_all[:, hidden_width : 2 * hidden_width]
    wdown_t = mlp_all[:, 2 * hidden_width : 3 * hidden_width]
    scale_one = row_scale(resid_in)
    normed = row_gather((resid_in * scale_one * attn_full).astype(jnp.bfloat16))
    query = matmul_plain(normed, wq_all)
    forget_raw = matmul_plain(normed, wf_all)
    value = matmul_plain(normed, wv_all)
    out_gate = matmul_plain(normed, wg_all)

    def mixer(query_in, forget_in, value_in, floor_in):

        def shaped(arr):
            return arr.reshape(row_count, -1, local_heads, HK)

        mixed_rows = recurrence(
            shaped(query_in), shaped(forget_in), shaped(value_in), floor_in, doc_all
        )
        return mixed_rows.reshape(query_in.shape[0], local_width)

    mixed, pullback = jax.vjp(mixer, query, forget_raw, value, floor_local)
    gate_act = jax.nn.silu(out_gate)
    gated = (mixed * gate_act).astype(jnp.bfloat16)
    branch = row_sum(times_trans(gated, wo_t))
    resid = resid_in + branch
    scale_two = row_scale(resid)
    normed2 = row_gather((resid * scale_two * mlp_full).astype(jnp.bfloat16))
    gate_proj = matmul_plain(normed2, wgate_all)
    up_proj = matmul_plain(normed2, wup_all)
    gate_silu = jax.nn.silu(gate_proj)
    hidden = (gate_silu * up_proj).astype(jnp.bfloat16)
    ffn_out = row_sum(times_trans(hidden, wdown_t))
    layer_out = (resid + ffn_out).astype(jnp.bfloat16).reshape(tokens.shape)
    cot_full = row_gather(cot_local)
    d_hidden = matmul_plain(cot_full, wdown_t)
    d_gate = (d_hidden * up_proj * silu_slope(gate_proj)).astype(jnp.bfloat16)
    d_up = (d_hidden * gate_silu).astype(jnp.bfloat16)
    mlp_grads = grad_pack(
        normed2, cot_full, jnp.concatenate([d_gate, d_up, hidden], axis=1), hidden_width
    )
    mlp_red = lax.psum_scatter(mlp_grads, "dp", scatter_dimension=0, tiled=True).astype(jnp.float32)
    d_normed2 = row_sum(times_trans(d_gate, wgate_all) + times_trans(d_up, wup_all))
    grad_mlp = jnp.sum(d_normed2 * resid * scale_two, axis=0)
    inner_two = jnp.mean(d_normed2 * mlp_full * resid, axis=-1, keepdims=True)
    d_resid = (
        cot_local.astype(jnp.float32)
        + d_normed2 * mlp_full * scale_two
        - resid * scale_two**3 * inner_two
    )
    d_branch = row_gather(d_resid.astype(jnp.bfloat16))
    d_gated = matmul_plain(d_branch, wo_t)
    d_mixed = d_gated * gate_act
    d_outgate = (d_gated * mixed * silu_slope(out_gate)).astype(jnp.bfloat16)
    d_query, d_forget, d_value, d_floor = pullback(d_mixed)
    d_query = d_query.astype(jnp.bfloat16)
    d_forget = d_forget.astype(jnp.bfloat16)
    d_value = d_value.astype(jnp.bfloat16)
    attn_grads = grad_pack(
        normed,
        d_branch,
        jnp.concatenate([d_query, d_forget, d_value, d_outgate, gated], axis=1),
        local_width,
    )
    attn_red = ring_sum(attn_grads)
    d_normed = row_sum(
        times_trans(d_query, wq_all)
        + times_trans(d_forget, wf_all)
        + times_trans(d_value, wv_all)
        + times_trans(d_outgate, wg_all)
    )
    grad_attn = jnp.sum(d_normed * resid_in * scale_one, axis=0)
    inner_one = jnp.mean(d_normed * attn_full * resid_in, axis=-1, keepdims=True)
    grad_tokens = (
        d_resid + d_normed * attn_full * scale_one - resid_in * scale_one**3 * inner_one
    ).reshape(tokens.shape)
    floor_vector = lax.dynamic_update_slice(
        jnp.zeros((model_width,), jnp.float32), d_floor.reshape(-1), (part_index * local_width,)
    )
    reduced_small = small_sum(jnp.stack([grad_attn, floor_vector, grad_mlp]))
    return (
        layer_out,
        grad_tokens,
        reduced_small[0],
        reduced_small[1],
        attn_red[:, 0 * local_width : 1 * local_width],
        attn_red[:, 1 * local_width : 2 * local_width],
        attn_red[:, 2 * local_width : 3 * local_width],
        attn_red[:, 3 * local_width : 4 * local_width],
        attn_red[:, 4 * local_width : 5 * local_width].T,
        reduced_small[2],
        mlp_red[:, 0:hidden_width],
        mlp_red[:, hidden_width : 2 * hidden_width],
        mlp_red[:, 2 * hidden_width : 3 * hidden_width].T,
    )


def solution(mesh):
    return jax.shard_map(
        shards,
        mesh=mesh,
        in_specs=(
            P("dp", "tensor", None, None),
            P("dp", None, None),
            P(("dp", "tensor")),
            P(("dp", "tensor")),
            P("dp", "tensor"),
            P("dp", "tensor"),
            P("dp", "tensor"),
            P("dp", "tensor"),
            P("tensor", "dp"),
            P(("dp", "tensor")),
            P("dp", "tensor"),
            P("dp", "tensor"),
            P("tensor", "dp"),
            P("dp", "tensor", None, None),
        ),
        out_specs=(
            P("dp", "tensor", None, None),
            P("dp", "tensor", None, None),
            P(("dp", "tensor")),
            P(("dp", "tensor")),
            P("dp", "tensor"),
            P("dp", "tensor"),
            P("dp", "tensor"),
            P("dp", "tensor"),
            P("tensor", "dp"),
            P(("dp", "tensor")),
            P("dp", "tensor"),
            P("dp", "tensor"),
            P("tensor", "dp"),
        ),
        check_vma=False,
    )
```
